32 devices in a mesh: groups: 2 (over x), ctx: 16 (over z, y, core).
Axes of the slice: x: 2, y: 2, z: 4, core: 2. Of those that a mesh axis runs over, the one named last changes fastest.
Arguments:
- queries: bfloat16 [12288, 8, 128], P(('groups', 'ctx')), parts along dimension 0, may hold values from -3 to 3
- key_vectors: bfloat16 [12288, 8, 128], P(('groups', 'ctx')), parts along dimension 0, may hold values from -4 to 4
- values: bfloat16 [12288, 8, 128], P(('groups', 'ctx')), parts along dimension 0, may hold values from -6 to 6
- gate_rates: float32 [8, 12288], P(None, ('groups', 'ctx')), parts along dimension 1, may hold values from 0 to 0.9
- log_decay: float32 [8, 12288], P(None, ('groups', 'ctx')), parts along dimension 1, may hold values from -2.5 to 0
- level_weights: float32 [5, 8, 12288], P(None, None, ('groups', 'ctx')), parts along dimension 2, may hold values from 0.25 to 4
- block_levels: int32 [32], P(('groups', 'ctx')), parts along dimension 0, may hold values from 0 to 4, as said below
- grad_out: bfloat16 [12288, 8, 128], P(('groups', 'ctx')), parts along dimension 0, may hold values from -6 to 6
Outputs:
- layer_out: bfloat16 [12288, 8, 128], P(('groups', 'ctx')), parts along dimension 0
- grad_queries: float32 [12288, 8, 128], P(('groups', 'ctx')), parts along dimension 0
- grad_values: float32 [12288, 8, 128], P(('groups', 'ctx')), parts along dimension 0
- grad_level_weights: float32 [5, 8, 12288], P(None, None, ('groups', 'ctx')), parts along dimension 2
The draws below stay inside these ranges and needn't reach their ends.
There are 2 independent parts, one for each index of `groups`. The reference program is written for one: setup_inputs(seed, part) draws one part's arguments, and reference() takes and returns one part's arrays. A program takes and returns all parts, laid end to end along the dimension named above; each array names one. Nothing has to cross between parts.
Inputs may be any that keep to these rules, and one draw needn't show every extreme that they name: `block_levels`: block 0 holds 0 and the last two blocks hold 4; every other block holds a value of 1 to 4.
All inputs are finite; a program needn't handle non-finite values.
Results may differ from the reference program's by a relative error of at most 0.001.
Values sent between devices are 32-bit elements; how exact they have to be, the bound alone decides.
No kernel may reach another device: no remote copies, remote signals or barrier semaphores. Data moves between devices by JAX's collectives and lax.ppermute only.
A program may use at most 128 MiB of HBM per device.

```python
import math
import jax
import jax.numpy as jnp
from jax import lax

HALF_HEAD_COUNT = 8
KEY_DIM = 128
VALUE_DIM = 128
TOK_DEV = 384
BLOCKS = 16
SEQUENCE_LENGTH = 6144
LEVELS = 4
WEIGHT_LEVELS = 5


coherence = 0.8


def slow_count():
    return max(1, HALF_HEAD_COUNT // 2)


def head_order(key):
    return jax.random.permutation(jax.random.fold_in(key, 11), HALF_HEAD_COUNT)


def slow_heads(key):
    return (head_order(key) < slow_count()).astype(jnp.float32)


def block_strength(key):
    steps = max(slow_count() - 1, 1)
    ranks = head_order(key).astype(jnp.float32) / steps
    return 2.5 * jnp.exp(ranks * math.log(4.0))


def draw_log_decay(key, part):
    slow = slow_heads(key)[:, None]
    chain = BLOCKS // 2 * TOK_DEV
    token_shift_amounts = jnp.arange(SEQUENCE_LENGTH, dtype=jnp.int32)
    owners = token_shift_amounts // TOK_DEV
    processor_multiplier = jnp.exp(jax.random.uniform(jax.random.fold_in(key, 1), (HALF_HEAD_COUNT, BLOCKS), minval=math.log(0.5), maxval=math.log(2.0)))
    processor_multiplier = jnp.take(processor_multiplier, owners, axis=1)
    token_multiplier = jnp.exp(jax.random.uniform(jax.random.fold_in(key, 2), (HALF_HEAD_COUNT, SEQUENCE_LENGTH), minval=math.log(0.5), maxval=math.log(2.0)))
    fast_rate = jax.random.uniform(jax.random.fold_in(key, 3), (HALF_HEAD_COUNT, 1), minval=1.0 / 50.0, maxval=1.0 / 30.0)
    slow_rate = jax.random.uniform(jax.random.fold_in(key, 4), (HALF_HEAD_COUNT, 1), minval=0.05, maxval=0.3) / chain
    head_decay_rate = slow * slow_rate + (1.0 - slow) * fast_rate
    cluster_positions = jax.random.randint(jax.random.fold_in(key, 5), (HALF_HEAD_COUNT, 3), 0, SEQUENCE_LENGTH)
    cluster_lengths = jax.random.uniform(jax.random.fold_in(key, 6), (HALF_HEAD_COUNT, 3), minval=math.log(0.5), maxval=math.log(0.8))
    agreement_flags = token_shift_amounts[None, :, None] == cluster_positions[:, None, :]
    token_clusters = jnp.sum(jnp.where(agreement_flags, cluster_lengths[:, None, :], 0.0), axis=-1)
    return (-head_decay_rate * processor_multiplier * token_multiplier + token_clusters).astype(jnp.float32)


def draw_gate_rates(key, part):
    slow = slow_heads(key)[:, None]
    strength = block_strength(key)[:, None]
    fast_beta = jax.random.uniform(jax.random.fold_in(key, 21), (HALF_HEAD_COUNT, SEQUENCE_LENGTH), minval=0.2, maxval=0.9)
    jitter = jax.random.uniform(jax.random.fold_in(key, 22), (HALF_HEAD_COUNT, SEQUENCE_LENGTH), minval=0.5, maxval=1.5)
    slow_beta = jnp.minimum(strength * jitter / (TOK_DEV * coherence), 0.9)
    return (slow * slow_beta + (1.0 - slow) * fast_beta).astype(jnp.float32)


def draw_key_vectors(key, part):
    share = slow_heads(key) * coherence
    direction = jax.random.rademacher(jax.random.fold_in(key, 31), (HALF_HEAD_COUNT, KEY_DIM), dtype=jnp.float32)
    token_signs = jax.random.rademacher(jax.random.fold_in(key, 32), (SEQUENCE_LENGTH, HALF_HEAD_COUNT), dtype=jnp.float32)
    noise = jnp.clip(jax.random.normal(jax.random.fold_in(key, 33), (SEQUENCE_LENGTH, HALF_HEAD_COUNT, KEY_DIM)), -4.0, 4.0)
    common = jnp.sqrt(share)[None, :, None] * token_signs[:, :, None] * direction[None, :, :]
    keys = common + jnp.sqrt(1.0 - share)[None, :, None] * noise
    return keys.astype(jnp.bfloat16)


def draw_block_levels(key, part):
    index = jnp.arange(BLOCKS, dtype=jnp.int32)
    caps = jax.random.randint(jax.random.fold_in(key, 100), (BLOCKS,), 1, LEVELS + 1)
    caps = jnp.where(index >= BLOCKS - 2, LEVELS, caps)
    caps = jnp.where(index == 0, 0, caps)
    return caps.astype(jnp.int32)


def levels(key, extent, pieces, smallest, largest):
    gain = 1.0
    for dim, parts in pieces:
        heights = jax.random.uniform(jax.random.fold_in(jax.random.fold_in(key, 6), dim), (parts,), jnp.float32, smallest / len(pieces), largest / len(pieces))
        gain = gain * jnp.repeat(jnp.exp(heights), extent[dim] // parts).reshape((-1,) + (1,) * (len(extent) - 1 - dim))
    return gain


def gaussian(rng, shape, deviation, reach, split=(), held_as=jnp.bfloat16):
    values = jax.random.normal(rng, shape, jnp.float32) * deviation
    if len(split) > 0:
        values = levels(rng, shape, split, -0.22, 0.18) * values
    return jnp.clip(values, min=-reach, max=reach).astype(held_as)


def setup_inputs(seed: int = 0, part: int = 0) -> dict:
    key_of = jax.random.split(jax.random.key(seed), 9)
    part_splits = jax.random.split(jax.random.fold_in(key_of[8], part), 9)
    queries = gaussian(part_splits[0], (SEQUENCE_LENGTH, HALF_HEAD_COUNT, KEY_DIM), 0.5, 3.0, ((0, 16),))
    key_vectors = draw_key_vectors(jax.random.fold_in(jax.random.fold_in(key_of[8], part), 71), part)
    values = gaussian(part_splits[2], (SEQUENCE_LENGTH, HALF_HEAD_COUNT, VALUE_DIM), 1.0, 6.0, ((0, 16),))
    gate_rates = draw_gate_rates(jax.random.fold_in(jax.random.fold_in(key_of[8], part), 71), part)
    log_decay = draw_log_decay(jax.random.fold_in(jax.random.fold_in(key_of[8], part), 71), part)
    level_weights = jnp.clip(jnp.exp(math.log(4.0) - 2.7725887 * jax.random.uniform(part_splits[5], (WEIGHT_LEVELS, HALF_HEAD_COUNT, SEQUENCE_LENGTH), jnp.float32) ** levels(part_splits[5], (WEIGHT_LEVELS, HALF_HEAD_COUNT, SEQUENCE_LENGTH), ((2, 16),), -0.2, 0.2)), 0.25, 4.0)
    block_levels = draw_block_levels(jax.random.fold_in(jax.random.fold_in(key_of[8], part), 71), part)
    grad_out = gaussian(part_splits[7], (SEQUENCE_LENGTH, HALF_HEAD_COUNT, VALUE_DIM), 1.0, 6.0, ((0, 16),))
    return {"queries": queries, "key_vectors": key_vectors, "values": values, "gate_rates": gate_rates, "log_decay": log_decay, "level_weights": level_weights, "block_levels": block_levels, "grad_out": grad_out}


highest = lax.Precision.HIGHEST

def block_terms(query_rows, key_rows, value_rows, beta_rows, decay_rows):
    length = key_rows.shape[1]
    float_type = key_rows.dtype
    row_ids = lax.broadcasted_iota(jnp.int32, (length, length), 0)
    col_ids = lax.broadcasted_iota(jnp.int32, (length, length), 1)
    lower_incl = row_ids >= col_ids
    lower_strict = row_ids > col_ids
    key_unit = key_rows / jnp.sqrt(lax.optimization_barrier(jnp.sum(key_rows * key_rows, axis=-1, keepdims=True)) + 1e-06)
    cumulative = jnp.cumsum(decay_rows, axis=-1)
    spread = cumulative[:, :, None] - cumulative[:, None, :]
    ratios = jnp.where(lower_incl, jnp.exp(jnp.where(lower_incl, spread, 0.0)), 0.0)
    key_gram = jnp.einsum('htd,hsd->hts', key_unit, key_unit, precision=highest)
    identity_n = jnp.eye(length, dtype=float_type)
    system_w = identity_n + jnp.where(lower_strict, beta_rows[:, :, None] * key_gram, 0.0)
    system_u = identity_n + jnp.where(lower_strict, beta_rows[:, :, None] * ratios * key_gram, 0.0)
    wy_keys = lax.linalg.triangular_solve(system_w, beta_rows[:, :, None] * key_unit, left_side=True, lower=True, unit_diagonal=True)
    wy_values = lax.linalg.triangular_solve(system_u, beta_rows[:, :, None] * value_rows, left_side=True, lower=True, unit_diagonal=True)
    decay_total = cumulative[:, -1]
    last_ratio = jnp.exp(decay_total[:, None] - cumulative)
    identity_k = jnp.eye(key_rows.shape[2], dtype=float_type)
    transition = jnp.exp(decay_total)[:, None, None] * (identity_k - jnp.einsum('hsd,hse->hde', key_unit, wy_keys, precision=highest))
    block_state = jnp.einsum('hsd,hse->hde', key_unit * last_ratio[:, :, None], wy_values, precision=highest)
    query_key = jnp.where(lower_incl, jnp.einsum('htd,hsd->hts', query_rows, key_unit, precision=highest), 0.0)
    local_out = jnp.einsum('hts,hse->hte', ratios * query_key, wy_values, precision=highest)
    gain_curve = jnp.exp(cumulative)
    carried = gain_curve[:, :, None] * (query_rows - jnp.einsum('hts,hsd->htd', query_key, wy_keys, precision=highest))
    return (transition, block_state, local_out, carried)

def reference(queries, key_vectors, values, gate_rates, log_decay, level_weights, block_levels, grad_out):
    float_type = log_decay.dtype

    def to_blocks(array, width):
        return array.astype(float_type).reshape(BLOCKS, TOK_DEV, HALF_HEAD_COUNT, width).transpose(0, 2, 1, 3)
    query_blocks = to_blocks(queries, KEY_DIM)
    key_blocks = to_blocks(key_vectors, KEY_DIM)
    value_blocks = to_blocks(values, VALUE_DIM)
    delta_blocks = to_blocks(grad_out, VALUE_DIM)
    beta_blocks = gate_rates.reshape(HALF_HEAD_COUNT, BLOCKS, TOK_DEV).transpose(1, 0, 2)
    decay_blocks = log_decay.reshape(HALF_HEAD_COUNT, BLOCKS, TOK_DEV).transpose(1, 0, 2)
    weight_blocks = level_weights.reshape(WEIGHT_LEVELS, HALF_HEAD_COUNT, BLOCKS, TOK_DEV).transpose(2, 0, 1, 3)
    token_shift_amounts = jnp.arange(BLOCKS, dtype=jnp.int32)
    level_ids = jnp.arange(1, WEIGHT_LEVELS, dtype=jnp.int32)
    level_bits = jnp.left_shift(jnp.ones_like(level_ids), level_ids - 1)

    def forward(query_in, value_in, weight_in):

        def local_terms(inputs):
            return block_terms(*inputs)
        transitions, states, local_outs, carried = lax.map(local_terms, (query_in, key_blocks, value_in, beta_blocks, decay_blocks))

        def advance(levels_carry, inputs):
            position, trans_now, state_now, carried_now, local_now, weights_now, doc_level = inputs
            visible = (position // level_bits % 2 == 1) & (level_ids <= doc_level)
            visible_states = jnp.where(visible[:, None, None, None], levels_carry, 0.0)
            cross_out = jnp.einsum('htd,lhde->lhte', carried_now, visible_states, precision=highest)
            block_out = weights_now[0][:, :, None] * local_now + lax.optimization_barrier(jnp.sum(weights_now[1:][:, :, :, None] * cross_out, axis=0))
            transported = jnp.einsum('hde,lhef->lhdf', trans_now, levels_carry, precision=highest)
            flipped = jnp.bitwise_xor(position, position + 1)
            within = flipped // level_bits % 2 == 1
            at_top = within & (flipped // (2 * level_bits) % 2 == 0)
            merged = lax.optimization_barrier(jnp.sum(jnp.where(within[:, None, None, None], transported, 0.0), axis=0)) + state_now
            updated = jnp.where(at_top[:, None, None, None], merged[None], jnp.where(within[:, None, None, None], 0.0, transported))
            return (updated, block_out)
        empty_levels = jnp.zeros((LEVELS, HALF_HEAD_COUNT, KEY_DIM, VALUE_DIM), dtype=float_type)
        final_levels, block_outs = lax.scan(advance, empty_levels, (token_shift_amounts, transitions, states, carried, local_outs, weight_in, block_levels))
        return block_outs
    forward_out, pullback = jax.vjp(forward, query_blocks, value_blocks, weight_blocks)
    grad_query, grad_value, grad_weight = pullback(delta_blocks)
    layer_out = forward_out.transpose(0, 2, 1, 3).reshape(SEQUENCE_LENGTH, HALF_HEAD_COUNT, VALUE_DIM).astype(jnp.bfloat16)
    grad_queries = grad_query.transpose(0, 2, 1, 3).reshape(SEQUENCE_LENGTH, HALF_HEAD_COUNT, KEY_DIM).astype(jnp.float32)
    grad_values = grad_value.transpose(0, 2, 1, 3).reshape(SEQUENCE_LENGTH, HALF_HEAD_COUNT, VALUE_DIM).astype(jnp.float32)
    grad_level_weights = grad_weight.transpose(1, 2, 0, 3).reshape(WEIGHT_LEVELS, HALF_HEAD_COUNT, SEQUENCE_LENGTH).astype(jnp.float32)
    return (layer_out, grad_queries, grad_values, grad_level_weights)
```

```python
import functools

import jax
import jax.numpy as jnp
from jax import lax
from jax.experimental import pallas as pl
from jax.experimental.pallas import tpu as pltpu
from jax.sharding import PartitionSpec as P

F32 = jnp.float32
BF16 = jnp.bfloat16
TILE = 128
SUB = 32
highest = lax.Precision.HIGHEST

NN = (((1,), (0,)), ((), ()))
NT = (((1,), (1,)), ((), ()))


def split(x):
    high = x.astype(BF16)
    return high, (x - high.astype(F32)).astype(BF16)


def dot(a, b, dims=NN):
    return lax.dot_general(a, b, dims, preferred_element_type=F32)


def dot_left(a, b, dims=NN):
    high, low = split(a)
    return dot(high, b, dims) + dot(low, b, dims)


def dot_right(a, b, dims=NN):
    high, low = split(b)
    return dot(a, high, dims) + dot(a, low, dims)


def dot3(a, b, dims=NN):
    ah, al = split(a)
    bh, bl = split(b)
    return dot(ah, bh, dims) + (dot(ah, bl, dims) + dot(al, bh, dims))


def column(row):
    return [
        jnp.transpose(jnp.broadcast_to(row[:, s : s + TILE], (TILE, TILE)))
        for s in range(0, row.shape[1], TILE)
    ]


def wide(tile, width):
    return jnp.concatenate([tile] * (width // TILE), axis=1) if width > TILE else tile


def rows_of(i):
    return slice(i * TILE, (i + 1) * TILE)


def key_norms(keys):
    k32 = keys.astype(F32)
    scale = 1.0 / jnp.sqrt(jnp.sum(k32 * k32, axis=1, keepdims=True) + 1e-06)
    cols = [
        jnp.broadcast_to(scale[rows_of(i)], (TILE, TILE)) for i in range(keys.shape[0] // TILE)
    ]
    row = jnp.concatenate([jnp.transpose(c)[0:1] for c in cols], axis=1)
    return cols, row


def causal(i, strict):
    width = (i + 1) * TILE
    r = lax.broadcasted_iota(jnp.int32, (TILE, width), 0) + i * TILE
    c = lax.broadcasted_iota(jnp.int32, (TILE, width), 1)
    return r > c if strict else r >= c


def decay_ratio(c_cols, c_row, i):
    width = (i + 1) * TILE
    keep = causal(i, False)
    spread = wide(c_cols[i], width) - c_row[:, :width]
    return jnp.where(keep, jnp.exp(jnp.where(keep, spread, 0.0)), 0.0)


def small_inverses(blocks):
    lane = lax.broadcasted_iota(jnp.int32, (8, TILE), 1)
    sub_row = lax.broadcasted_iota(jnp.int32, (8, TILE), 0)
    owner = lane // SUB
    within = lane - owner * SUB
    first = owner * SUB
    tiles = SUB // 8
    coefs, sols = [], []
    for block in blocks:
        packed, unit = [], []
        for q in range(tiles):
            piece = jnp.zeros((8, TILE), F32)
            for b in range(TILE // SUB):
                start = b * SUB + q * 8
                piece = jnp.where(owner == b, block[start : start + 8], piece)
            packed.append(piece)
            unit.append(jnp.where(within == sub_row + q * 8, 1.0, 0.0).astype(F32))
        coefs.append(packed)
        sols.append(unit)
    for j in range(SUB - 1):
        index = first + j
        for coef, sol in zip(coefs, sols):
            row = jnp.broadcast_to(sol[j // 8][j % 8 : j % 8 + 1], (8, TILE))
            for q in range((j + 1) // 8, tiles):
                factor = jnp.take_along_axis(coef[q], index, axis=1, mode="promise_in_bounds")
                sol[q] = sol[q] - factor * row
    out = []
    for sol in sols:
        pieces = []
        for b in range(TILE // SUB):
            for q in range(tiles):
                pieces.append(jnp.where(owner == b, sol[q], 0.0))
        out.append(jnp.concatenate(pieces, axis=0))
    return out


def tile_inverses(blocks):
    r = lax.broadcasted_iota(jnp.int32, (TILE, TILE), 0)
    c = lax.broadcasted_iota(jnp.int32, (TILE, TILE), 1)
    inverses = small_inverses(blocks)
    size = SUB
    while size < TILE:
        below = (r // size == c // size + 1) & (r // (2 * size) == c // (2 * size))
        inverses = [
            x - dot3(x, dot3(jnp.where(below, block, 0.0), x))
            for x, block in zip(inverses, blocks)
        ]
        size *= 2
    return inverses


def by_head(scratch, head, tokens, heads):
    return scratch[pl.ds(head, tokens, stride=heads), :]


def state_kernel(k_ref, v_ref, beta_ref, decay_ref, a_ref, bt_ref, ms_ref, c_ref, k_all, v_all):
    tokens, heads, width = k_ref.shape
    head = pl.program_id(0)
    count = tokens // TILE

    @pl.when(head == 0)
    def _():
        k_all[...] = k_ref[...].astype(F32).reshape(tokens * heads, width)
        v_all[...] = v_ref[...].astype(F32).reshape(tokens * heads, width)
        r = lax.broadcasted_iota(jnp.int32, (tokens, tokens), 0)
        c = lax.broadcasted_iota(jnp.int32, (tokens, tokens), 1)
        upper = jnp.where(r <= c, 1.0, 0.0).astype(BF16)
        high, rest = split(decay_ref[...])
        low = (decay_ref[...] - high.astype(F32) - rest.astype(F32)).astype(BF16)
        c_ref[...] = dot(high, upper) + (dot(rest, upper) + dot(low, upper))

    k32 = by_head(k_all, head, tokens, heads)
    keys = k32.astype(BF16)
    values = by_head(v_all, head, tokens, heads).astype(BF16)
    beta_row = beta_ref[pl.ds(head, 1), :]
    c_row = c_ref[pl.ds(head, 1), :]
    norm_cols, norm_row = key_norms(keys)
    beta_cols = column(beta_row)
    lower = []
    for i in range(count):
        n = (i + 1) * TILE
        gram = dot(keys[rows_of(i)], keys[:n], NT)
        scaled = wide(beta_cols[i] * norm_cols[i], n) * gram * norm_row[:, :n]
        lower.append(jnp.where(causal(i, True), scaled, 0.0))
    diagonal = tile_inverses([lower[i][:, rows_of(i)] for i in range(count)])
    rows = [diagonal[0]]
    for i in range(1, count):
        below = None
        parts = []
        for j in range(i):
            stack = [rows[k][:, rows_of(j)] for k in range(j, i)]
            stack = jnp.concatenate(stack, axis=0) if len(stack) > 1 else stack[0]
            parts.append(dot3(lower[i][:, j * TILE : i * TILE], stack))
        below = jnp.concatenate(parts, axis=1) if len(parts) > 1 else parts[0]
        rows.append(jnp.concatenate([-dot3(diagonal[i], below), diagonal[i]], axis=1))
    keys_t = jnp.transpose(k32).astype(BF16)
    scaled_rows = []
    for i in range(count):
        n = (i + 1) * TILE
        a_row = rows[i] * beta_row[:, :n]
        a_ref[rows_of(i), :n] = a_row
        scaled_rows.append(wide(norm_cols[i], n) * a_row)
    pieces = []
    for j in range(count):
        stack = [scaled_rows[i][:, rows_of(j)] for i in range(j, count)]
        stack = jnp.concatenate(stack, axis=0) if len(stack) > 1 else stack[0]
        pieces.append(dot_right(keys_t[:, j * TILE :], stack))
    bt = jnp.concatenate(pieces, axis=1)
    total = c_row[:, tokens - 1 :]
    faded = bt * jnp.exp(total - c_row)
    bt_ref[...] = faded
    r = lax.broadcasted_iota(jnp.int32, (width, width), 0)
    c = lax.broadcasted_iota(jnp.int32, (width, width), 1)
    identity = jnp.where(r == c, 1.0, 0.0).astype(F32)
    ms_ref[0] = jnp.exp(total) * (identity - dot_left(bt * norm_row, keys))
    ms_ref[1] = dot_left(faded, values)


def local_kernel(
    q_ref, k_ref, v_ref, d_ref, c_ref, w_ref, see_ref, a_ref,
    carried_ref, w_keys_ref, local_ref, dq_ref, dvt_ref, adj_ref, gw_ref,
    q_all, k_all, v_all, d_all,
):
    tokens, heads, width = k_ref.shape
    head = pl.program_id(0)
    count = tokens // TILE
    levels = adj_ref.shape[0]

    @pl.when(head == 0)
    def _():
        for source, target in ((q_ref, q_all), (k_ref, k_all), (v_ref, v_all), (d_ref, d_all)):
            target[...] = source[...].astype(F32).reshape(tokens * heads, width)

    q32 = by_head(q_all, head, tokens, heads)
    d32 = by_head(d_all, head, tokens, heads)
    queries = q32.astype(BF16)
    keys = by_head(k_all, head, tokens, heads).astype(BF16)
    values = by_head(v_all, head, tokens, heads).astype(BF16)
    delta = d32.astype(BF16)
    c_row = c_ref[pl.ds(head, 1), :]
    c_cols = column(c_row)
    weight_cols = [column(w_ref[l, pl.ds(head, 1), :]) for l in range(levels + 1)]
    _, norm_row = key_norms(keys)
    wy_keys, wy_values, ratios, faded_a, query_key = [], [], [], [], []
    for i in range(count):
        n = (i + 1) * TILE
        a_row = a_ref[rows_of(i), :n]
        ratio = decay_ratio(c_cols, c_row, i)
        ratios.append(ratio)
        faded_a.append(ratio * a_row)
        wy_keys.append(dot_left(a_row * norm_row[:, :n], keys[:n]))
        wy_values.append(dot_left(faded_a[i], values[:n]))
        scores = dot(queries[rows_of(i)], keys[:n], NT) * norm_row[:, :n]
        query_key.append(jnp.where(causal(i, False), scores, 0.0))
    keys_w = jnp.concatenate(wy_keys, axis=0)
    values_u = jnp.concatenate(wy_values, axis=0)
    w_keys_ref[...] = keys_w
    weighted_pq, carried, dots = [], [], []
    for i in range(count):
        n = (i + 1) * TILE
        pq = ratios[i] * query_key[i]
        local = dot3(pq, values_u[:n])
        local_ref[rows_of(i), :] = weight_cols[0][i] * local
        dots.append(d32[rows_of(i)] * local)
        gained = jnp.exp(c_cols[i]) * (q32[rows_of(i)] - dot3(query_key[i], keys_w[:n]))
        carried.append(gained)
        carried_ref[rows_of(i), :] = gained
        w0 = wide(weight_cols[0][i], n)
        weighted_pq.append(w0 * pq)
        grad_qk = ratios[i] * w0 * dot_right(delta[rows_of(i)], values_u[:n], NT)
        dq_ref[rows_of(i), :] = dot_left(grad_qk * norm_row[:, :n], keys[:n])
    ones = jnp.ones((8, width), BF16)
    gw_ref[...] = dot_right(ones, jnp.concatenate(dots, axis=0), NT)[0:1]
    delta_t = jnp.transpose(d32).astype(BF16)
    adjoint_u = []
    for j in range(count):
        stack = [weighted_pq[i][:, rows_of(j)] for i in range(j, count)]
        stack = jnp.concatenate(stack, axis=0) if len(stack) > 1 else stack[0]
        adjoint_u.append(dot_right(delta_t[:, j * TILE :], stack))
    adjoint_u = jnp.concatenate(adjoint_u, axis=1)
    for j in range(count):
        stack = [faded_a[i][:, rows_of(j)] for i in range(j, count)]
        stack = jnp.concatenate(stack, axis=0) if len(stack) > 1 else stack[0]
        dvt_ref[:, rows_of(j)] = dot3(adjoint_u[:, j * TILE :], stack)
    for l in range(levels):
        scaled = [weight_cols[l + 1][i] * carried[i] for i in range(count)]
        adj_ref[l] = see_ref[l] * dot_right(delta_t, jnp.concatenate(scaled, axis=0))


def cross_kernel(
    k_ref, d_ref, c_ref, w_ref, x_ref, carried_ref, w_keys_ref, local_ref, dq_in_ref, gw_in_ref,
    out_ref, dq_ref, gw_ref, k_all, d_all, out_all,
):
    tokens, heads, width = k_ref.shape
    head = pl.program_id(0)
    count = tokens // TILE
    levels = x_ref.shape[0]

    @pl.when(head == 0)
    def _():
        for source, target in ((k_ref, k_all), (d_ref, d_all)):
            target[...] = source[...].astype(F32).reshape(tokens * heads, width)

    keys = by_head(k_all, head, tokens, heads).astype(BF16)
    delta = by_head(d_all, head, tokens, heads).astype(BF16)
    c_cols = column(c_ref[pl.ds(head, 1), :])
    weight_cols = [column(w_ref[l + 1, pl.ds(head, 1), :]) for l in range(levels)]
    _, norm_row = key_norms(keys)
    states = jnp.concatenate([x_ref[l] for l in range(levels)], axis=0)
    states_h, states_l = split(states)
    keys_h, keys_l = split(w_keys_ref[...])
    ones = jnp.ones((8, width), BF16)
    gw_ref[0, pl.ds(head, 1), :] = gw_in_ref[...]
    weight_rows = [[] for _ in range(levels)]
    for i in range(count):
        n = (i + 1) * TILE
        carried = carried_ref[rows_of(i), :]
        d_i = delta[rows_of(i)]
        pulled = dot(d_i, states_h, NT) + dot(d_i, states_l, NT)
        grad_carried = None
        lefts = []
        for l in range(levels):
            one = pulled[:, rows_of(l)]
            lefts.append(weight_cols[l][i] * carried)
            weight_rows[l].append(dot_right(ones, carried * one, NT)[0:1])
            term = weight_cols[l][i] * one
            grad_carried = term if grad_carried is None else grad_carried + term
        left_h, left_l = split(jnp.concatenate(lefts, axis=1))
        cross = dot(left_h, states_h) + (dot(left_h, states_l) + dot(left_l, states_h))
        forward = local_ref[rows_of(i), :] + cross
        out_all[pl.ds(head + i * TILE * heads, TILE, stride=heads), :] = forward
        scaled = jnp.exp(c_cols[i]) * grad_carried
        scaled_h, scaled_l = split(scaled)
        scores = dot(scaled_h, keys_h[:n], NT) + (
            dot(scaled_h, keys_l[:n], NT) + dot(scaled_l, keys_h[:n], NT)
        )
        scores = jnp.where(causal(i, False), scores, 0.0) * norm_row[:, :n]
        grad = dq_in_ref[rows_of(i), :] + scaled - dot_left(scores, keys[:n])
        dq_ref[pl.ds(head + i * TILE * heads, TILE, stride=heads), :] = grad
    for l in range(levels):
        gw_ref[l + 1, pl.ds(head, 1), :] = jnp.concatenate(weight_rows[l], axis=1)

    @pl.when(head == heads - 1)
    def _():
        out_ref[...] = out_all[...].reshape(tokens, heads, width).astype(BF16)


def value_kernel(bt_ref, dvt_ref, g_ref, dv_ref):
    heads = pl.num_programs(0)
    head = pl.program_id(0)
    tokens = bt_ref.shape[1]
    grad_t = dvt_ref[...] + dot3(g_ref[...], bt_ref[...])
    dv_ref[pl.ds(head, tokens, stride=heads), :] = jnp.transpose(grad_t)


def whole(shape):
    return pl.BlockSpec(shape, lambda h: (0,) * len(shape))


def headed(*shape):
    return pl.BlockSpec((pl.Squeezed(),) + shape, lambda h: (h,) + (0,) * len(shape))


def headed_second(first, *shape):
    return pl.BlockSpec(
        (first, pl.Squeezed()) + shape, lambda h: (0, h) + (0,) * len(shape)
    )


def struct(*shape, dtype=F32):
    return jax.ShapeDtypeStruct(shape, dtype)


PARAMS = pltpu.CompilerParams(
    dimension_semantics=("arbitrary",), vmem_limit_bytes=48 * 1024 * 1024
)


def cost(flops, size):
    return pl.CostEstimate(flops=flops, bytes_accessed=size, transcendentals=0)


def swap(x, round_bit):
    size = lax.axis_size("ctx")
    return lax.ppermute(x, "ctx", [(i, i ^ 1 << round_bit) for i in range(size)])


def halves(x, axis, side):
    half = x.shape[axis] // 2
    mine = lax.dynamic_slice_in_dim(x, side * half, half, axis)
    other = lax.dynamic_slice_in_dim(x, (1 - side) * half, half, axis)
    return mine, other


def joined(own, received, axis, side):
    return jnp.where(
        side == 1,
        jnp.concatenate([received, own], axis=axis),
        jnp.concatenate([own, received], axis=axis),
    )


def mul(a, b):
    return jnp.einsum("...ij,...jk->...ik", a, b, precision=highest)


def up_states(pair, levels, sides):
    lows, ups, low_states = [], [], []
    for r in range(levels):
        up = sides[r] == 1
        if r == levels - 1:
            pair = pair[1:]
        if pair.shape[1] > 1:
            mine, other = halves(pair, 1, sides[r])
        else:
            mine = other = pair
        received = swap(other, r)
        low = jnp.where(up, received, mine)
        high = jnp.where(up, mine, received)
        low_states.append(low[-1])
        if r < levels - 1:
            lows.append(low[0])
            ups.append(high[0])
            product = mul(high[0][None], low)
            pair = jnp.stack([product[0], product[1] + high[1]])
    return lows, ups, low_states


def down_states(lows, low_states, levels, sides, heads):
    states = None
    for r in reversed(range(levels)):
        up = sides[r] == 1
        first = low_states[r][None]
        if states is None:
            moved = kept = first
        else:
            moved = jnp.concatenate([first, mul(lows[r][None], states)], axis=0)
            kept = jnp.concatenate([first, states], axis=0)
        own = jnp.where(up, moved, kept)
        if heads >> r > 1:
            received = swap(jnp.where(up, kept, moved), r)
            own = joined(own, received, 1, sides[r])
        states = own
    return states


def up_adjoints(adjoints, lows, levels, sides):
    runs = []
    for r in range(levels):
        up = sides[r] == 1
        if adjoints.shape[1] > 1:
            mine, other = halves(adjoints, 1, sides[r])
        else:
            mine = other = adjoints
        received = swap(other, r)
        low = jnp.where(up, received, mine)
        high = jnp.where(up, mine, received)
        runs.append(high[0])
        if r < levels - 1:
            adjoints = low[1:] + mul(high[1:], lows[r][None])
    return runs


def down_adjoints(runs, ups, levels, sides, heads):
    grad = None
    for r in reversed(range(levels)):
        up = sides[r] == 1
        if grad is None:
            low, high = runs[r], jnp.zeros_like(runs[r])
        else:
            low, high = runs[r] + mul(grad, ups[r]), grad
        own = jnp.where(up, high, low)
        if heads >> r > 1:
            own = joined(own, swap(jnp.where(up, low, high), r), 0, sides[r])
        grad = own
    return grad


def shards(
    queries, key_vectors, values, gate_rates, log_decay, level_weights, block_levels, grad_out
):
    levels = lax.axis_size("ctx").bit_length() - 1
    position = lax.axis_index("ctx")
    sides = [position // (1 << r) % 2 for r in range(levels)]
    tokens, heads, width = key_vectors.shape
    level_ids = jnp.arange(1, levels + 1, dtype=jnp.int32)
    sees = (jnp.right_shift(position, level_ids - 1) % 2 == 1) & (level_ids <= block_levels[0])
    sees_f = sees.astype(F32)
    smem = pl.BlockSpec(memory_space=pltpu.SMEM)
    packed = whole((tokens, heads, width))
    rows = whole((heads, tokens))
    flat = pltpu.VMEM((tokens * heads, width), F32)
    unit = 2 * heads * tokens * width * width

    a_full, bt, pair, c_rows = pl.pallas_call(
        state_kernel,
        grid=(heads,),
        in_specs=[packed, packed, rows, rows],
        out_specs=[
            headed(tokens, tokens),
            headed(width, tokens),
            headed_second(2, width, width),
            rows,
        ],
        out_shape=[
            struct(heads, tokens, tokens),
            struct(heads, width, tokens),
            struct(2, heads, width, width),
            struct(heads, tokens),
        ],
        scratch_shapes=[flat, flat],
        compiler_params=PARAMS,
        cost_estimate=cost(40 * unit, 10 << 20),
        name="state",
    )(key_vectors, values, gate_rates, log_decay)

    lows, ups, low_states = up_states(pair, levels, sides)

    carried, wy_keys, local, dq_local, dvt_local, adjoints, gw_local = pl.pallas_call(
        local_kernel,
        grid=(heads,),
        in_specs=[
            packed, packed, packed, packed, rows, whole((levels + 1, heads, tokens)), smem,
            headed(tokens, tokens),
        ],
        out_specs=[
            headed(tokens, width),
            headed(tokens, width),
            headed(tokens, width),
            headed(tokens, width),
            headed(width, tokens),
            headed_second(levels, width, width),
            headed(1, tokens),
        ],
        out_shape=[
            struct(heads, tokens, width),
            struct(heads, tokens, width),
            struct(heads, tokens, width),
            struct(heads, tokens, width),
            struct(heads, width, tokens),
            struct(levels, heads, width, width),
            struct(heads, 1, tokens),
        ],
        scratch_shapes=[flat] * 4,
        compiler_params=PARAMS,
        cost_estimate=cost(60 * unit, 20 << 20),
        name="local",
    )(queries, key_vectors, values, grad_out, c_rows, level_weights, sees_f, a_full)

    states = down_states(lows, low_states, levels, sides, heads)
    states = jnp.where(sees[:, None, None, None], states, 0.0)
    runs = up_adjoints(adjoints, lows, levels, sides)
    grad_state = down_adjoints(runs, ups, levels, sides, heads)

    layer_out, grad_queries, grad_level_weights = pl.pallas_call(
        cross_kernel,
        grid=(heads,),
        in_specs=[
            packed, packed, rows, whole((levels + 1, heads, tokens)),
            headed_second(levels, width, width),
            headed(tokens, width),
            headed(tokens, width),
            headed(tokens, width),
            headed(tokens, width),
            headed(1, tokens),
        ],
        out_specs=[packed, whole((tokens * heads, width)), whole((levels + 1, heads, tokens))],
        out_shape=[
            struct(tokens, heads, width, dtype=BF16),
            struct(tokens * heads, width),
            struct(levels + 1, heads, tokens),
        ],
        scratch_shapes=[flat] * 3,
        compiler_params=PARAMS,
        cost_estimate=cost(40 * unit, 16 << 20),
        name="cross",
    )(
        key_vectors, grad_out, c_rows, level_weights, states, carried, wy_keys, local, dq_local,
        gw_local,
    )

    grad_values = pl.pallas_call(
        value_kernel,
        grid=(heads,),
        in_specs=[headed(width, tokens), headed(width, tokens), headed(width, width)],
        out_specs=whole((tokens * heads, width)),
        out_shape=struct(tokens * heads, width),
        compiler_params=PARAMS,
        cost_estimate=cost(3 * unit, 5 << 20),
        name="value",
    )(bt, dvt_local, grad_state)
    shape = (tokens, heads, width)
    return (
        layer_out, grad_queries.reshape(shape), grad_values.reshape(shape), grad_level_weights
    )


def solution(mesh):
    tokens = P(("groups", "ctx"), None, None)
    rows = P(None, ("groups", "ctx"))
    weights = P(None, None, ("groups", "ctx"))
    return jax.shard_map(
        shards,
        mesh=mesh,
        in_specs=(tokens, tokens, tokens, rows, rows, weights, P(("groups", "ctx")), tokens),
        out_specs=(tokens, tokens, tokens, weights),
        check_vma=False,
    )
```

```python
import functools

import jax
import jax.numpy as jnp
from jax import lax
from jax.experimental import pallas as pl
from jax.experimental.pallas import tpu as pltpu
from jax.sharding import PartitionSpec as P

F32 = jnp.float32
BF16 = jnp.bfloat16
TILE = 128
SUB = 16
NN = (((1,), (0,)), ((), ()))
NT = (((1,), (1,)), ((), ()))


def split(x):
    high = x.astype(BF16)
    return high, (x - high.astype(F32)).astype(BF16)


def dot(a, b, dims=NN):
    return lax.dot_general(a, b, dims, preferred_element_type=F32)


def dot_left(a, b, dims=NN):
    high, low = split(a)
    return dot(high, b, dims) + dot(low, b, dims)


def free_axis(dims):
    return 1 - dims[0][1][0]


def fold(x):
    half = x.shape[1] // 2
    return x[:, :half] + x[:, half:]


def dot_right(a, b, dims=NN):
    high, low = split(b)
    axis = free_axis(dims)
    if b.shape[axis] <= TILE:
        return fold(dot(a, jnp.concatenate([high, low], axis=axis), dims))
    return dot(a, high, dims) + dot(a, low, dims)


def dot_parts(a, b, dims=NN):
    ah, al = a
    bh, bl = b
    axis = free_axis(dims)
    if bh.shape[axis] <= TILE:
        return fold(dot(ah, jnp.concatenate([bh, bl], axis=axis), dims)) + dot(al, bh, dims)
    return dot(ah, bh, dims) + (dot(ah, bl, dims) + dot(al, bh, dims))


def dot3(a, b, dims=NN):
    return dot_parts(split(a), split(b), dims)


def batch_parts(pairs, dims=NN):
    axis = free_axis(dims)
    first = [dot(a[0], jnp.concatenate(b, axis=axis), dims) for a, b in pairs]
    second = [dot(a[1], b[0], dims) for a, b in pairs]
    return [fold(f) + g for f, g in zip(first, second)]


def column(row):
    return [
        jnp.transpose(jnp.broadcast_to(row[:, s : s + TILE], (TILE, TILE)))
        for s in range(0, row.shape[1], TILE)
    ]


def wide(tile, width):
    return jnp.concatenate([tile] * (width // TILE), axis=1) if width > TILE else tile


def rows_of(i):
    return slice(i * TILE, (i + 1) * TILE)


def key_norms(keys):
    k32 = keys.astype(F32)
    scale = 1.0 / jnp.sqrt(jnp.sum(k32 * k32, axis=1, keepdims=True) + 1e-06)
    cols = [
        jnp.broadcast_to(scale[rows_of(i)], (TILE, TILE)) for i in range(keys.shape[0] // TILE)
    ]
    row = jnp.concatenate([jnp.transpose(c)[0:1] for c in cols], axis=1)
    return cols, row


def causal(i, strict):
    width = (i + 1) * TILE
    r = lax.broadcasted_iota(jnp.int32, (TILE, width), 0) + i * TILE
    c = lax.broadcasted_iota(jnp.int32, (TILE, width), 1)
    return r > c if strict else r >= c


def decay_ratio(c_cols, c_row, i):
    width = (i + 1) * TILE
    keep = causal(i, False)
    spread = wide(c_cols[i], width) - c_row[:, :width]
    return jnp.where(keep, jnp.exp(jnp.where(keep, spread, 0.0)), 0.0)


def small_inverses(blocks):
    lane = lax.broadcasted_iota(jnp.int32, (8, TILE), 1)
    sub_row = lax.broadcasted_iota(jnp.int32, (8, TILE), 0)
    owner = lane // SUB
    within = lane - owner * SUB
    first = owner * SUB
    tiles = SUB // 8
    coefs, sols = [], []
    for block in blocks:
        packed, unit = [], []
        for q in range(tiles):
            piece = jnp.zeros((8, TILE), F32)
            for b in range(TILE // SUB):
                start = b * SUB + q * 8
                piece = jnp.where(owner == b, block[start : start + 8], piece)
            packed.append(piece)
            unit.append(jnp.where(within == sub_row + q * 8, 1.0, 0.0).astype(F32))
        coefs.append(packed)
        sols.append(unit)
    for j in range(SUB - 1):
        index = first + j
        for coef, sol in zip(coefs, sols):
            row = jnp.broadcast_to(sol[j // 8][j % 8 : j % 8 + 1], (8, TILE))
            for q in range((j + 1) // 8, tiles):
                factor = jnp.take_along_axis(coef[q], index, axis=1, mode="promise_in_bounds")
                sol[q] = sol[q] - factor * row
    out = []
    for sol in sols:
        pieces = []
        for b in range(TILE // SUB):
            for q in range(tiles):
                pieces.append(jnp.where(owner == b, sol[q], 0.0))
        out.append(jnp.concatenate(pieces, axis=0))
    return out


def tile_inverses(blocks):
    r = lax.broadcasted_iota(jnp.int32, (TILE, TILE), 0)
    c = lax.broadcasted_iota(jnp.int32, (TILE, TILE), 1)
    inverses = small_inverses(blocks)
    size = SUB
    while size < TILE:
        below_half = (r // size == c // size + 1) & (r // (2 * size) == c // (2 * size))
        parts = [split(x) for x in inverses]
        inner = batch_parts(
            [(split(jnp.where(below_half, t, 0.0)), x) for t, x in zip(blocks, parts)]
        )
        outer = batch_parts([(x, split(y)) for x, y in zip(parts, inner)])
        inverses = [x - y for x, y in zip(inverses, outer)]
        size *= 2
    return inverses


def piled(parts):
    return jnp.concatenate(parts, axis=0) if len(parts) > 1 else parts[0]


def below(rows, j):
    return piled([rows[i][:, rows_of(j)] for i in range(j, len(rows))])


def head_at(position, side, heads):
    return (position + (1 - side) * (heads // 2)) % heads


def state_kernel(
    sides_ref, q_in, k_in, v_in, d_in, beta_ref, decay_ref, w_ref,
    q_ref, k_ref, v_ref, d_ref, aux_ref, a_ref, bt_ref, other_ref, mine_ref,
    q_all, k_all, v_all, d_all, c_all,
):
    tokens, heads, width = k_in.shape
    per = k_ref.shape[0]
    half = heads // 2
    step = pl.program_id(0)
    count = tokens // TILE

    @pl.when(step == 0)
    def _():
        for source, target in ((q_in, q_all), (k_in, k_all), (v_in, v_all), (d_in, d_all)):
            target[...] = source[...].astype(F32).reshape(tokens * heads, width)
        r = lax.broadcasted_iota(jnp.int32, (tokens, tokens), 0)
        c = lax.broadcasted_iota(jnp.int32, (tokens, tokens), 1)
        upper = jnp.where(r <= c, 1.0, 0.0).astype(BF16)
        high, rest = split(decay_ref[...])
        low = (decay_ref[...] - high.astype(F32) - rest.astype(F32)).astype(BF16)
        c_all[...] = dot(high, upper) + (dot(rest, upper) + dot(low, upper))

    r = lax.broadcasted_iota(jnp.int32, (width, width), 0)
    c = lax.broadcasted_iota(jnp.int32, (width, width), 1)
    identity = jnp.where(r == c, 1.0, 0.0).astype(F32)
    k32s, keyss, norms, betas, c_rows, lowers, tiles = [], [], [], [], [], [], []
    for s in range(per):
        head = head_at(step * per + s, sides_ref[0], heads)
        mine = pl.ds(head, tokens, stride=heads)
        k32 = k_all[mine, :]
        keys = k32.astype(BF16)
        q_ref[s] = q_all[mine, :].astype(BF16)
        k_ref[s] = keys
        v_ref[s] = v_all[mine, :].astype(BF16)
        d_ref[s] = d_all[mine, :].astype(BF16)
        beta_row = beta_ref[pl.ds(head, 1), :]
        c_row = c_all[pl.ds(head, 1), :]
        norm_cols, norm_row = key_norms(keys)
        aux = [c_row, norm_row] + [w_ref[l, pl.ds(head, 1), :] for l in range(w_ref.shape[0])]
        aux_ref[s, : len(aux)] = jnp.concatenate(aux, axis=0)
        beta_cols = column(beta_row)
        lower = []
        for i in range(count):
            n = (i + 1) * TILE
            gram = dot(keys[rows_of(i)], keys[:n], NT)
            scaled = wide(beta_cols[i] * norm_cols[i], n) * gram * norm_row[:, :n]
            lower.append(jnp.where(causal(i, True), scaled, 0.0))
        k32s.append(k32)
        keyss.append(keys)
        norms.append((norm_cols, norm_row))
        betas.append(beta_row)
        c_rows.append(c_row)
        lowers.append(lower)
        tiles += [lower[i][:, rows_of(i)] for i in range(count)]
    inverses = tile_inverses(tiles)
    diagonal = [split(x) for x in inverses]
    lower_parts = [[split(row) for row in lower] for lower in lowers]
    group = range(per)
    solved = [{(i, i): diagonal[s * count + i] for i in range(count)} for s in group]
    exact = [{(i, i): inverses[s * count + i] for i in range(count)} for s in group]
    for off in range(1, count):
        pairs = []
        for s in group:
            for i in range(off, count):
                j = i - off
                left = tuple(x[:, j * TILE : i * TILE] for x in lower_parts[s][i])
                right = tuple(piled([solved[s][k, j][z] for k in range(j, i)]) for z in range(2))
                pairs.append((left, right))
        inner = batch_parts(pairs)
        places = [(s, i) for s in group for i in range(off, count)]
        outer = batch_parts(
            [(diagonal[s * count + i], split(y)) for (s, i), y in zip(places, inner)]
        )
        for (s, i), y in zip(places, outer):
            exact[s][i, i - off] = -y
            solved[s][i, i - off] = split(-y)
    scaled_rows = []
    for s in group:
        norm_cols, beta_row = norms[s][0], betas[s]
        scaled = []
        for i in range(count):
            n = (i + 1) * TILE
            row = [exact[s][i, j] for j in range(i + 1)]
            a_row = (jnp.concatenate(row, axis=1) if i else row[0]) * beta_row[:, :n]
            a_ref[s, rows_of(i), :n] = a_row
            scaled.append(wide(norm_cols[i], n) * a_row)
        scaled_rows.append(scaled)
    keys_t = [jnp.transpose(k32).astype(BF16) for k32 in k32s]
    bts = [
        jnp.concatenate(
            [
                dot_right(keys_t[s][:, j * TILE :], below(scaled_rows[s], j))
                for j in range(count)
            ],
            axis=1,
        )
        for s in group
    ]
    totals = [c_rows[s][:, tokens - 1 :] for s in group]
    fadeds = [bts[s] * jnp.exp(totals[s] - c_rows[s]) for s in group]
    overlaps = [dot_left(bts[s] * norms[s][1], keyss[s]) for s in group]
    states = [dot_left(fadeds[s], v_ref[s]) for s in group]
    for s in group:
        bt_ref[s] = fadeds[s]
        moved = jnp.exp(totals[s]) * (identity - overlaps[s])
        position = step * per + s

        @pl.when(position < half)
        def _():
            other_ref[0, position] = moved
            other_ref[1, position] = states[s]

        @pl.when(position >= half)
        def _():
            mine_ref[0, position - half] = moved
            mine_ref[1, position - half] = states[s]


def early_kernel(sees_ref, q_ref, k_ref, d_ref, aux_ref, a_ref, carried_ref, w_keys_ref, adj_ref):
    tokens, width = q_ref.shape
    count = tokens // TILE
    levels = adj_ref.shape[0]
    queries, keys = q_ref[...], k_ref[...]
    c_row, norm_row = aux_ref[0:1, :], aux_ref[1:2, :]
    gains = [jnp.exp(t) for t in column(c_row)]
    delta_t = jnp.transpose(d_ref[...].astype(F32)).astype(BF16)
    weight_cols = [column(aux_ref[3 + l : 4 + l, :]) for l in range(levels)]
    span = range(count)
    sizes = [(i + 1) * TILE for i in span]
    wy_keys = [
        dot_left(a_ref[rows_of(i), : sizes[i]] * norm_row[:, : sizes[i]], keys[: sizes[i]])
        for i in span
    ]
    scores = [dot(queries[rows_of(i)], keys[: sizes[i]], NT) for i in span]
    query_key = [jnp.where(causal(i, False), scores[i] * norm_row[:, : sizes[i]], 0.0) for i in span]
    keys_w = piled(wy_keys)
    w_keys_ref[...] = keys_w
    keys_h, keys_l = split(keys_w)
    inner = [
        dot_parts(split(query_key[i]), (keys_h[: sizes[i]], keys_l[: sizes[i]])) for i in span
    ]
    carried = [gains[i] * (queries[rows_of(i)].astype(F32) - inner[i]) for i in span]
    for i in span:
        carried_ref[rows_of(i), :] = carried[i]
    for l in range(levels):
        scaled = piled([weight_cols[l][i] * carried[i] for i in range(count)])
        adj_ref[l] = jnp.where(sees_ref[l] == 1, dot_right(delta_t, scaled), 0.0)


def late_kernel(q_ref, k_ref, v_ref, d_ref, aux_ref, a_ref, local_ref, dq_ref, dvt_ref, gw_ref):
    tokens, width = q_ref.shape
    count = tokens // TILE
    queries, keys, values, delta = q_ref[...], k_ref[...], v_ref[...], d_ref[...]
    d32 = delta.astype(F32)
    c_row, norm_row = aux_ref[0:1, :], aux_ref[1:2, :]
    c_cols = column(c_row)
    w_cols = column(aux_ref[2:3, :])
    wy_values, ratios, faded_a = [], [], []
    for i in range(count):
        n = (i + 1) * TILE
        ratios.append(decay_ratio(c_cols, c_row, i))
        faded_a.append(ratios[i] * a_ref[rows_of(i), :n])
        wy_values.append(dot_left(faded_a[i], values[:n]))
    values_h, values_l = split(piled(wy_values))
    span = range(count)
    sizes = [(i + 1) * TILE for i in span]
    scores = [dot(queries[rows_of(i)], keys[: sizes[i]], NT) for i in span]
    outers = [
        dot(delta[rows_of(i)], values_h[: sizes[i]], NT)
        + dot(delta[rows_of(i)], values_l[: sizes[i]], NT)
        for i in span
    ]
    scales = [ratios[i] * norm_row[:, : sizes[i]] for i in span]
    pqs = [scales[i] * scores[i] for i in span]
    weights = [wide(w_cols[i], sizes[i]) for i in span]
    weighted_pq = [weights[i] * pqs[i] for i in span]
    locals_ = [
        dot_parts(split(pqs[i]), (values_h[: sizes[i]], values_l[: sizes[i]])) for i in span
    ]
    for i in span:
        dq_ref[rows_of(i), :] = dot_left(scales[i] * weights[i] * outers[i], keys[: sizes[i]])
        local_ref[rows_of(i), :] = w_cols[i] * locals_[i]
    dots = [d32[rows_of(i)] * locals_[i] for i in span]
    ones = jnp.ones((8, width), BF16)
    gw_ref[...] = dot_right(ones, piled(dots), NT)[0:1]
    delta_t = jnp.transpose(d32).astype(BF16)
    adjoint_u = jnp.concatenate(
        [dot_right(delta_t[:, j * TILE :], below(weighted_pq, j)) for j in range(count)], axis=1
    )
    u_h, u_l = split(adjoint_u)
    for j in range(count):
        part = (u_h[:, j * TILE :], u_l[:, j * TILE :])
        dvt_ref[:, rows_of(j)] = dot_parts(part, split(below(faded_a, j)))


def cross_kernel(
    sees_ref, k_ref, d_ref, aux_ref, x_ref, carried_ref, w_keys_ref, local_ref, dq_in_ref, gw_in_ref,
    out_ref, dq_ref, gw_ref,
):
    tokens, width = k_ref.shape
    count = tokens // TILE
    levels = x_ref.shape[0]
    keys, delta = k_ref[...], d_ref[...]
    norm_row = aux_ref[1:2, :]
    gains = [jnp.exp(t) for t in column(aux_ref[0:1, :])]
    weight_cols = [column(aux_ref[3 + l : 4 + l, :]) for l in range(levels)]
    states = piled([jnp.where(sees_ref[l] == 1, x_ref[l], 0.0) for l in range(levels)])
    states_h, states_l = split(states)
    keys_h, keys_l = split(w_keys_ref[...])
    ones = jnp.ones((8, width), BF16)
    span = range(count)
    pulled = [
        dot(delta[rows_of(i)], states_h, NT) + dot(delta[rows_of(i)], states_l, NT) for i in span
    ]
    carried = [carried_ref[rows_of(i), :] for i in span]
    lefts = [
        split(jnp.concatenate([weight_cols[l][i] * carried[i] for l in range(levels)], axis=1))
        for i in span
    ]
    crosses = [dot_parts(lefts[i], (states_h, states_l)) for i in span]
    scaled = []
    for i in span:
        terms = [weight_cols[l][i] * pulled[i][:, rows_of(l)] for l in range(levels)]
        scaled.append(gains[i] * functools.reduce(jnp.add, terms))
    scores = [
        dot_parts(split(scaled[i]), (keys_h[: (i + 1) * TILE], keys_l[: (i + 1) * TILE]), NT)
        for i in span
    ]
    weight_rows = [
        [dot_right(ones, carried[i] * pulled[i][:, rows_of(l)], NT)[0:1] for i in span]
        for l in range(levels)
    ]
    for i in span:
        n = (i + 1) * TILE
        kept = jnp.where(causal(i, False), scores[i], 0.0) * norm_row[:, :n]
        dq_ref[rows_of(i), :] = dq_in_ref[rows_of(i), :] + scaled[i] - dot_left(kept, keys[:n])
        out_ref[rows_of(i), :] = local_ref[rows_of(i), :] + crosses[i]
    rows = [gw_in_ref[...]] + [jnp.concatenate(weight_rows[l], axis=1) for l in range(levels)]
    gw_ref[...] = jnp.concatenate(rows, axis=0)


def value_kernel(sizes, per, sides_ref, bt_ref, recv_ref, own_ref, *refs):
    steps = pl.num_programs(0)
    step = pl.program_id(0)
    heads = steps * per
    tokens = bt_ref.shape[2]
    groups = []
    for _ in range(4):
        groups.append(refs[: len(sizes)])
        refs = refs[len(sizes) :]
    outs, dqs, gws, dvts = groups
    out_ref, dq_ref, dv_ref, gw_ref, out_all = refs
    grads = [jnp.where(step < steps // 2, recv_ref[0, s], own_ref[0, s]) for s in range(per)]
    moved = [dot3(grads[s], bt_ref[s]) for s in range(per)]
    places = []
    for s in range(per):
        head = head_at(step * per + s, sides_ref[0], heads)
        places.append((head, pl.ds(head, tokens, stride=heads)))
    start = 0
    for p, size in enumerate(sizes):

        @pl.when((step >= start // per) & (step < (start + size) // per))
        def _(p=p):
            for s, (head, place) in enumerate(places):
                out_all[place, :] = outs[p][s]
                dq_ref[place, :] = dqs[p][s]
                dv_ref[place, :] = jnp.transpose(dvts[p][s] + moved[s])
                for l in range(gw_ref.shape[0]):
                    gw_ref[l, pl.ds(head, 1), :] = gws[p][s, l : l + 1, :]

        start += size

    @pl.when(step == steps - 1)
    def _():
        out_ref[...] = out_all[...].reshape(out_ref.shape).astype(BF16)


def pick(flag, a, b):
    return jnp.where(flag, a, b)


def stored(side, h, count, mine_ref, other_ref, write):
    if other_ref is None:
        write(mine_ref, h)
        return
    half = count // 2

    @pl.when(side == h // half)
    def _():
        write(mine_ref, h % half)

    @pl.when(side != h // half)
    def _():
        write(other_ref, h % half)


def read_half(side, h, own_ref, recv_ref, level):
    if recv_ref is None:
        return own_ref[level, h]
    half = own_ref.shape[1]
    return pick(side == h // half, own_ref[level, h % half], recv_ref[level, h % half])


def up_kernel(r, last, splits, sides_ref, mine_ref, recv_ref, low_m, up_m, low_s, *nexts):
    count = mine_ref.shape[1]
    up = sides_ref[r] == 1
    next_mine, next_other = nexts if splits else (nexts[0], None)
    pairs, s_ups = [], []
    for h in range(count):
        m_low = pick(up, recv_ref[0, h], mine_ref[0, h])
        m_up = pick(up, mine_ref[0, h], recv_ref[0, h])
        s_low = pick(up, recv_ref[1, h], mine_ref[1, h])
        s_ups.append(pick(up, mine_ref[1, h], recv_ref[1, h]))
        low_m[h] = m_low
        up_m[h] = m_up
        low_s[h] = s_low
        parts = split(m_up)
        pairs.append((parts, split(s_low)))
        if not last:
            pairs.append((parts, split(m_low)))
    products = batch_parts(pairs)
    for h in range(count):
        value = products[h : h + 1] if last else products[2 * h : 2 * h + 2]

        def write(ref, place):
            ref[-1 % ref.shape[0], place] = value[0] + s_ups[h]
            if not last:
                ref[0, place] = value[1]

        stored(sides_ref[min(r + 1, sides_ref.shape[0] - 1)], h, count, next_mine, next_other, write)


def down_kernel(r, top, split_in, splits, sides_ref, low_m, low_s, *refs):
    own_ref, *refs = refs
    recv_ref = None
    if split_in or top:
        recv_ref, *refs = refs
    out_own, out_send = refs if splits else (refs[0], None)
    count = low_m.shape[0]
    levels = own_ref.shape[0]
    up = sides_ref[r] == 1
    values, pairs = [], []
    for h in range(count):
        m_parts = split(low_m[h])
        for l in range(levels):
            if top:
                x = pick(sides_ref[r + 1] == 1, recv_ref[0, h], own_ref[0, h])
            else:
                x = read_half(sides_ref[r + 1], h, own_ref, recv_ref, l)
            values.append(x)
            pairs.append((m_parts, split(x)))
    products = batch_parts(pairs)
    for h in range(count):
        out_own[0, h] = low_s[h]
        if out_send is not None:
            out_send[0, h] = low_s[h]
        for l in range(levels):
            x, moved = values[h * levels + l], products[h * levels + l]
            out_own[l + 1, h] = pick(up, moved, x)
            if out_send is not None:
                out_send[l + 1, h] = pick(up, x, moved)


def adjoint_up_kernel(r, sizes, splits, sides_ref, low_m, recv_ref, *refs):
    parts, refs = refs[: len(sizes)], refs[len(sizes) :]
    run_ref, next_mine, *rest = refs
    next_other = rest[0] if splits else None
    count, levels = low_m.shape[0], recv_ref.shape[0]
    up = sides_ref[r] == 1
    pairs, bases = [], []
    for h in range(count):
        p, place = 0, h
        while place >= sizes[p]:
            place -= sizes[p]
            p += 1
        mine_ref = parts[p]
        run_ref[h] = pick(up, mine_ref[0, place], recv_ref[0, h])
        m_parts = split(low_m[h])
        highs = []
        for l in range(1, levels):
            mine, received = mine_ref[l, place], recv_ref[l, h]
            highs.append(pick(up, mine, received))
            bases.append(pick(up, received, mine))
        pairs.append((split(piled(highs)), m_parts))
    products = batch_parts(pairs)
    for h in range(count):
        for l in range(1, levels):
            value = bases[h * (levels - 1) + l - 1] + products[h][rows_of(l - 1)]

            def write(ref, at):
                ref[l - 1, at] = value

            stored(sides_ref[min(r + 1, sides_ref.shape[0] - 1)], h, count, next_mine, next_other, write)


def adjoint_down_kernel(r, top, split_in, splits, sides_ref, run_ref, up_m, *refs):
    own_ref, *refs = refs
    recv_ref = None
    if split_in:
        recv_ref, *refs = refs
    out_own, out_send = refs if splits else (refs[0], None)
    up = sides_ref[r] == 1
    span = range(run_ref.shape[0])
    grads = [read_half(sides_ref[r + 1], h, own_ref, recv_ref, 0) for h in span]
    if top:
        grads = [pick(sides_ref[r + 1] == 1, 0.0, g) for g in grads]
    products = batch_parts([(split(grads[h]), split(up_m[h])) for h in span])
    for h in span:
        low = run_ref[h] + products[h]
        out_own[0, h] = pick(up, grads[h], low)
        if out_send is not None:
            out_send[0, h] = pick(up, low, grads[h])


def whole(shape):
    return pl.BlockSpec(shape, lambda p: (0,) * len(shape))


def headed(*shape, start=0):
    return pl.BlockSpec(
        (pl.Squeezed(),) + shape, lambda p: (p + start,) + (0,) * len(shape)
    )


def second(first, *shape, start=0):
    return pl.BlockSpec(
        (first, pl.Squeezed()) + shape, lambda p: (0, p + start) + (0,) * len(shape)
    )


def struct(*shape, dtype=F32):
    return jax.ShapeDtypeStruct(shape, dtype)


SMEM = pl.BlockSpec(memory_space=pltpu.SMEM)
VMEM = pl.BlockSpec(memory_space=pltpu.VMEM)


def params(mib):
    return pltpu.CompilerParams(
        dimension_semantics=("arbitrary",), vmem_limit_bytes=mib * 1024 * 1024
    )


def cost(micros, size=1 << 20):
    return pl.CostEstimate(flops=int(micros * 1.1e9), bytes_accessed=size, transcendentals=0)


def small(kernel, name, sides, inputs, outputs):
    return pl.pallas_call(
        kernel,
        in_specs=[SMEM] + [VMEM] * len(inputs),
        out_specs=[VMEM] * len(outputs),
        out_shape=[struct(*o) for o in outputs],
        cost_estimate=cost(1.0),
        compiler_params=pltpu.CompilerParams(vmem_limit_bytes=24 * 1024 * 1024),
        name=name,
    )(sides, *inputs)


def swap(x, round_bit):
    size = lax.axis_size("ctx")
    return lax.ppermute(x, "ctx", [(i, i ^ 1 << round_bit) for i in range(size)])


def to_upper(x, round_bit):
    size = lax.axis_size("ctx")
    bit = 1 << round_bit
    return lax.ppermute(x, "ctx", [(i, i ^ bit) for i in range(size) if not i & bit])


def to_lower(x, round_bit):
    size = lax.axis_size("ctx")
    bit = 1 << round_bit
    return lax.ppermute(x, "ctx", [(i, i ^ bit) for i in range(size) if i & bit])


def after(values, marker):
    return lax.optimization_barrier((values, marker))[0]


PARTS = (4, 2, 2)


def shards(
    queries, key_vectors, values, gate_rates, log_decay, level_weights, block_levels, grad_out
):
    levels = lax.axis_size("ctx").bit_length() - 1
    position = lax.axis_index("ctx")
    tokens, heads, width = key_vectors.shape
    half = heads // 2
    ids = jnp.arange(levels, dtype=jnp.int32)
    sides = jnp.right_shift(position, ids) % 2
    sees = sides * (ids < block_levels[0]).astype(jnp.int32)
    per = 2
    state_per = 4
    aux_rows = (levels + 3 + 7) // 8 * 8
    mat = (width, width)
    splits = [heads >> r > 1 for r in range(levels + 1)]
    held = [max(heads >> r, 1) for r in range(levels + 1)]
    packed = whole((tokens, heads, width))
    rows = whole((heads, tokens))
    flat = pltpu.VMEM((tokens * heads, width), F32)

    def grouped(*shape, size=per):
        return pl.BlockSpec((size,) + shape, lambda p: (p,) + (0,) * len(shape))

    def stated(*shape):
        return grouped(*shape, size=state_per)

    tok = struct(heads, tokens, width, dtype=BF16)
    q, k, v, d, aux, a_full, bt, other, mine = pl.pallas_call(
        state_kernel,
        grid=(heads // state_per,),
        in_specs=[SMEM, packed, packed, packed, packed, rows, rows, whole(level_weights.shape)],
        out_specs=[
            stated(tokens, width), stated(tokens, width), stated(tokens, width),
            stated(tokens, width), stated(aux_rows, tokens), stated(tokens, tokens),
            stated(width, tokens), whole((2, half) + mat), whole((2, half) + mat),
        ],
        out_shape=[
            tok, tok, tok, tok, struct(heads, aux_rows, tokens), struct(heads, tokens, tokens),
            struct(heads, width, tokens), struct(2, half, *mat), struct(2, half, *mat),
        ],
        scratch_shapes=[flat] * 4 + [pltpu.VMEM((heads, tokens), F32)],
        compiler_params=params(56),
        cost_estimate=cost(20),
        name="state",
    )(sides, queries, key_vectors, values, grad_out, gate_rates, log_decay, level_weights)

    def early(start, size, q):
        return pl.pallas_call(
            early_kernel,
            grid=(size,),
            in_specs=[
                SMEM, headed(tokens, width, start=start), headed(tokens, width, start=start),
                headed(tokens, width, start=start), headed(aux_rows, tokens, start=start),
                headed(tokens, tokens, start=start),
            ],
            out_specs=[headed(tokens, width), headed(tokens, width), second(levels, *mat)],
            out_shape=[
                struct(size, tokens, width), struct(size, tokens, width),
                struct(levels, size, *mat),
            ],
            compiler_params=params(32),
            cost_estimate=cost(1.2 * size),
            name="early",
        )(sees, q, k, d, aux, a_full)

    def late(start, size, q):
        return pl.pallas_call(
            late_kernel,
            grid=(size,),
            in_specs=[headed(tokens, width, start=start)] * 4
            + [headed(aux_rows, tokens, start=start), headed(tokens, tokens, start=start)],
            out_specs=[
                headed(tokens, width), headed(tokens, width), headed(width, tokens),
                headed(1, tokens),
            ],
            out_shape=[
                struct(size, tokens, width), struct(size, tokens, width),
                struct(size, width, tokens), struct(size, 1, tokens),
            ],
            compiler_params=params(32),
            cost_estimate=cost(1.5 * size),
            name="late",
        )(q, k, v, d, aux, a_full)

    def cross(start, size, x, x_start, early_out, late_out, marker):
        carried, w_keys, _ = early_out
        local, dq, _, gw = late_out
        return pl.pallas_call(
            cross_kernel,
            grid=(size,),
            in_specs=[
                SMEM, headed(tokens, width, start=start), headed(tokens, width, start=start),
                headed(aux_rows, tokens, start=start), second(levels, *mat, start=x_start),
                headed(tokens, width), headed(tokens, width), headed(tokens, width),
                headed(tokens, width), headed(1, tokens),
            ],
            out_specs=[
                headed(tokens, width), headed(tokens, width), headed(levels + 1, tokens),
            ],
            out_shape=[
                struct(size, tokens, width), struct(size, tokens, width),
                struct(size, levels + 1, tokens),
            ],
            compiler_params=params(32),
            cost_estimate=cost(2.5 * size),
            name="cross",
        )(sees, after(k, marker), d, aux, x, carried, w_keys, local, dq, gw)

    lows, ups, low_states = [], [], []

    def up_round(r, mine, received):
        last = r + 1 == levels - 1
        n, many = held[r + 1], splits[r + 1]
        payload = (1 if last else 2, held[r + 2]) + mat
        low_m, up_m, low_s, *following = small(
            functools.partial(up_kernel, r, last, many), f"up{r}", sides, [mine, received],
            [(n, *mat)] * 3 + [payload] * (2 if many else 1),
        )
        lows.append(low_m)
        ups.append(up_m)
        low_states.append(low_s)
        return following[0], following[-1]

    def adjoint_round(r, parts, received):
        many = splits[r + 1]
        following = (levels - r - 1, held[r + 2]) + mat
        run, *rest = small(
            functools.partial(
                adjoint_up_kernel, r, [p.shape[1] for p in parts], many
            ),
            f"adjoint_up{r}", sides, [lows[r], received, *parts],
            [(held[r + 1], *mat)] + [following] * (2 if many else 1),
        )
        return run, rest[0], rest[-1]

    def down_round(r, own, received):
        top = r == levels - 2
        split_in = splits[r + 1]
        many = splits[r]
        inputs = [lows[r], low_states[r], own] + ([received] if split_in or top else [])
        shape = (levels - r, held[r + 1]) + mat
        outs = small(
            functools.partial(down_kernel, r, top, split_in, many), f"down{r}", sides, inputs,
            [shape] * (2 if many else 1),
        )
        return outs[0], outs[-1]

    def adjoint_down_round(r, run, own, received):
        top = r == levels - 2
        split_in = splits[r + 1]
        many = splits[r]
        inputs = [run, ups[r], own] + ([received] if split_in else [])
        outs = small(
            functools.partial(adjoint_down_kernel, r, top, split_in, many), f"adjoint_down{r}",
            sides, inputs, [(1, held[r + 1], *mat)] * (2 if many else 1),
        )
        return outs[0], outs[-1]

    starts = [sum(PARTS[:i]) for i in range(len(PARTS))]
    early_outs, late_outs = [], []
    received = swap(other, 0)
    early_outs.append(early(starts[0], PARTS[0], q))
    mine, other = up_round(0, mine, received)
    for r in range(1, levels):
        received = to_upper(other, r) if r == levels - 1 else swap(other, r)
        if r < len(PARTS):
            early_outs.append(early(starts[r], PARTS[r], after(q, other)))
        if r < levels - 1:
            mine, other = up_round(r, mine, received)
    top_own, top_received = mine, received

    adj_other = early_outs[0][2]
    adj_received = swap(adj_other, 0)
    own, send = down_round(levels - 2, top_own, top_received)
    state_received = None
    runs = []
    adj_parts = [e[2] for e in early_outs[1:]]
    late_outs.append(late(starts[0], PARTS[0], after(q, send)))
    run, adj_mine, adj_other = adjoint_round(0, adj_parts, adj_received)
    runs.append(run)
    for r in reversed(range(levels - 2)):
        if splits[r + 1]:
            state_received = swap(send, r + 1)
        own, send = down_round(r, own, state_received)
        if len(late_outs) < len(PARTS):
            i = len(late_outs)
            late_outs.append(late(starts[i], PARTS[i], after(q, send)))
    state_received = swap(send, 0)
    for r in range(1, levels):
        adj_received = to_lower(adj_other, r) if r == levels - 1 else swap(adj_other, r)
        if r < levels - 1:
            run, adj_mine, adj_other = adjoint_round(r, [adj_mine], adj_received)
            runs.append(run)
    cross_outs = [None] * len(PARTS)
    order = list(range(1, len(PARTS))) + [0]
    grad_own, grad_received = adj_received[:1], None
    marker = send
    for r in reversed(range(levels - 1)):
        grad_own, grad_send = adjoint_down_round(r, runs[r], grad_own, grad_received)
        grad_received = swap(grad_send, r) if splits[r] else None
    for i in order:
        x, x_start = (state_received, 0) if i == 0 else (own, starts[i] - half)
        cross_outs[i] = cross(starts[i], PARTS[i], x, x_start, early_outs[i], late_outs[i], marker)

    def part_spec(i, *shape):
        first, size = starts[i] // per, PARTS[i] // per
        return pl.BlockSpec(
            (per,) + shape, lambda p: (jnp.clip(p - first, 0, size - 1),) + (0,) * len(shape)
        )

    indices = range(len(PARTS))
    layer_out, grad_queries, grad_values, grad_level_weights = pl.pallas_call(
        functools.partial(value_kernel, PARTS, per),
        grid=(heads // per,),
        in_specs=[
            SMEM, grouped(width, tokens),
            pl.BlockSpec((1, per) + mat, lambda p: (0, jnp.minimum(p, half // per - 1), 0, 0)),
            pl.BlockSpec((1, per) + mat, lambda p: (0, jnp.maximum(p - half // per, 0), 0, 0)),
        ]
        + [part_spec(i, tokens, width) for i in indices]
        + [part_spec(i, tokens, width) for i in indices]
        + [part_spec(i, levels + 1, tokens) for i in indices]
        + [part_spec(i, width, tokens) for i in indices],
        out_specs=[
            packed, whole((tokens * heads, width)), whole((tokens * heads, width)),
            whole((levels + 1, heads, tokens)),
        ],
        out_shape=[
            struct(tokens, heads, width, dtype=BF16), struct(tokens * heads, width),
            struct(tokens * heads, width), struct(levels + 1, heads, tokens),
        ],
        scratch_shapes=[flat],
        compiler_params=params(40),
        cost_estimate=cost(5),
        name="value",
    )(
        sides, bt, grad_received, grad_own,
        *[c[0] for c in cross_outs], *[c[1] for c in cross_outs], *[c[2] for c in cross_outs],
        *[l[2] for l in late_outs],
    )
    shape = (tokens, heads, width)
    return (
        layer_out, grad_queries.reshape(shape), grad_values.reshape(shape), grad_level_weights
    )


def solution(mesh):
    tokens = P(("groups", "ctx"), None, None)
    rows = P(None, ("groups", "ctx"))
    weights = P(None, None, ("groups", "ctx"))
    return jax.shard_map(
        shards,
        mesh=mesh,
        in_specs=(tokens, tokens, tokens, rows, rows, weights, P(("groups", "ctx")), tokens),
        out_specs=(tokens, tokens, tokens, weights),
        check_vma=False,
    )
```

```python
import functools

import jax
import jax.numpy as jnp
from jax import lax
from jax.experimental import pallas as pl
from jax.experimental.pallas import tpu as pltpu
from jax.sharding import PartitionSpec as P

F32 = jnp.float32
BF16 = jnp.bfloat16
TILE = 128
SUB = 16
NN = (((1,), (0,)), ((), ()))
NT = (((1,), (1,)), ((), ()))


def split(x):
    high = x.astype(BF16)
    return high, (x - high.astype(F32)).astype(BF16)


def dot(a, b, dims=NN):
    return lax.dot_general(a, b, dims, preferred_element_type=F32)


def dot_left(a, b, dims=NN):
    high, low = split(a)
    return dot(high, b, dims) + dot(low, b, dims)


def free_axis(dims):
    return 1 - dims[0][1][0]


def fold(x):
    half = x.shape[1] // 2
    return x[:, :half] + x[:, half:]


def dot_right(a, b, dims=NN):
    high, low = split(b)
    axis = free_axis(dims)
    if b.shape[axis] <= TILE:
        return fold(dot(a, jnp.concatenate([high, low], axis=axis), dims))
    return dot(a, high, dims) + dot(a, low, dims)


def dot_parts(a, b, dims=NN):
    ah, al = a
    bh, bl = b
    axis = free_axis(dims)
    if bh.shape[axis] <= TILE:
        return fold(dot(ah, jnp.concatenate([bh, bl], axis=axis), dims)) + dot(al, bh, dims)
    return dot(ah, bh, dims) + (dot(ah, bl, dims) + dot(al, bh, dims))


def dot3(a, b, dims=NN):
    return dot_parts(split(a), split(b), dims)


def batch_parts(pairs, dims=NN):
    axis = free_axis(dims)
    first = [dot(a[0], jnp.concatenate(b, axis=axis), dims) for a, b in pairs]
    second = [dot(a[1], b[0], dims) for a, b in pairs]
    return [fold(f) + g for f, g in zip(first, second)]


def column(row):
    return [
        jnp.transpose(jnp.broadcast_to(row[:, s : s + TILE], (TILE, TILE)))
        for s in range(0, row.shape[1], TILE)
    ]


def wide(tile, width):
    return jnp.concatenate([tile] * (width // TILE), axis=1) if width > TILE else tile


def rows_of(i):
    return slice(i * TILE, (i + 1) * TILE)


def key_norms(keys):
    k32 = keys.astype(F32)
    scale = 1.0 / jnp.sqrt(jnp.sum(k32 * k32, axis=1, keepdims=True) + 1e-06)
    cols = [
        jnp.broadcast_to(scale[rows_of(i)], (TILE, TILE)) for i in range(keys.shape[0] // TILE)
    ]
    row = jnp.concatenate([jnp.transpose(c)[0:1] for c in cols], axis=1)
    return cols, row


def causal(i, strict):
    width = (i + 1) * TILE
    r = lax.broadcasted_iota(jnp.int32, (TILE, width), 0) + i * TILE
    c = lax.broadcasted_iota(jnp.int32, (TILE, width), 1)
    return r > c if strict else r >= c


def decay_ratio(c_cols, c_row, i):
    width = (i + 1) * TILE
    keep = causal(i, False)
    spread = wide(c_cols[i], width) - c_row[:, :width]
    return jnp.where(keep, jnp.exp(jnp.where(keep, spread, 0.0)), 0.0)


def small_inverses(blocks):
    lane = lax.broadcasted_iota(jnp.int32, (8, TILE), 1)
    sub_row = lax.broadcasted_iota(jnp.int32, (8, TILE), 0)
    owner = lane // SUB
    within = lane - owner * SUB
    first = owner * SUB
    tiles = SUB // 8
    coefs, sols = [], []
    for block in blocks:
        packed, unit = [], []
        for q in range(tiles):
            piece = jnp.zeros((8, TILE), F32)
            for b in range(TILE // SUB):
                start = b * SUB + q * 8
                piece = jnp.where(owner == b, block[start : start + 8], piece)
            packed.append(piece)
            unit.append(jnp.where(within == sub_row + q * 8, 1.0, 0.0).astype(F32))
        coefs.append(packed)
        sols.append(unit)
    for j in range(SUB - 1):
        index = first + j
        for coef, sol in zip(coefs, sols):
            row = jnp.broadcast_to(sol[j // 8][j % 8 : j % 8 + 1], (8, TILE))
            for q in range((j + 1) // 8, tiles):
                factor = jnp.take_along_axis(coef[q], index, axis=1, mode="promise_in_bounds")
                sol[q] = sol[q] - factor * row
    out = []
    for sol in sols:
        pieces = []
        for b in range(TILE // SUB):
            for q in range(tiles):
                pieces.append(jnp.where(owner == b, sol[q], 0.0))
        out.append(jnp.concatenate(pieces, axis=0))
    return out


def tile_inverses(blocks):
    r = lax.broadcasted_iota(jnp.int32, (TILE, TILE), 0)
    c = lax.broadcasted_iota(jnp.int32, (TILE, TILE), 1)
    inverses = small_inverses(blocks)
    size = SUB
    while size < TILE:
        below_half = (r // size == c // size + 1) & (r // (2 * size) == c // (2 * size))
        parts = [split(x) for x in inverses]
        inner = batch_parts(
            [(split(jnp.where(below_half, t, 0.0)), x) for t, x in zip(blocks, parts)]
        )
        outer = batch_parts([(x, split(y)) for x, y in zip(parts, inner)])
        inverses = [x - y for x, y in zip(inverses, outer)]
        size *= 2
    return inverses


def piled(parts):
    return jnp.concatenate(parts, axis=0) if len(parts) > 1 else parts[0]


def below(rows, j):
    return piled([rows[i][:, rows_of(j)] for i in range(j, len(rows))])


def head_at(position, side, heads):
    return (position + (1 - side) * (heads // 2)) % heads


def state_kernel(
    sides_ref, q_in, k_in, v_in, d_in, beta_ref, decay_ref, w_ref,
    q_ref, k_ref, v_ref, d_ref, aux_ref, a_ref, bt_ref, other_ref, mine_ref,
    q_all, k_all, v_all, d_all, c_all, packed_all, beta_all, decay_all, w_all, sems,
):
    tokens, heads, width = k_in.shape
    per = k_ref.shape[0]
    half = heads // 2
    step = pl.program_id(0)
    count = tokens // TILE

    @pl.when(step == 0)
    def _():
        sources = (decay_ref, beta_ref, w_ref, k_in, v_in, q_in, d_in)
        targets = (decay_all, beta_all, w_all, *(packed_all.at[i] for i in range(4)))
        copies = [
            pltpu.make_async_copy(source, target, sems.at[i])
            for i, (source, target) in enumerate(zip(sources, targets))
        ]
        for copy in copies:
            copy.start()
        for copy in copies:
            copy.wait()
        for i, target in enumerate((k_all, v_all, q_all, d_all)):
            target[...] = packed_all[i].astype(F32).reshape(tokens * heads, width)
        r = lax.broadcasted_iota(jnp.int32, (tokens, tokens), 0)
        c = lax.broadcasted_iota(jnp.int32, (tokens, tokens), 1)
        upper = jnp.where(r <= c, 1.0, 0.0).astype(BF16)
        decay = decay_all[...]
        high, rest = split(decay)
        low = (decay - high.astype(F32) - rest.astype(F32)).astype(BF16)
        c_all[...] = dot(high, upper) + (dot(rest, upper) + dot(low, upper))

    r = lax.broadcasted_iota(jnp.int32, (width, width), 0)
    c = lax.broadcasted_iota(jnp.int32, (width, width), 1)
    identity = jnp.where(r == c, 1.0, 0.0).astype(F32)
    k32s, keyss, norms, betas, c_rows, lowers, tiles = [], [], [], [], [], [], []
    for s in range(per):
        head = head_at(step * per + s, sides_ref[0], heads)
        mine = pl.ds(head, tokens, stride=heads)
        k32 = k_all[mine, :]
        keys = k32.astype(BF16)
        q_ref[s] = q_all[mine, :].astype(BF16)
        k_ref[s] = keys
        v_ref[s] = v_all[mine, :].astype(BF16)
        d_ref[s] = d_all[mine, :].astype(BF16)
        beta_row = beta_all[pl.ds(head, 1), :]
        c_row = c_all[pl.ds(head, 1), :]
        norm_cols, norm_row = key_norms(keys)
        aux = [c_row, norm_row] + [w_all[l, pl.ds(head, 1), :] for l in range(w_all.shape[0])]
        aux_ref[s, : len(aux)] = jnp.concatenate(aux, axis=0)
        beta_cols = column(beta_row)
        lower = []
        for i in range(count):
            n = (i + 1) * TILE
            gram = dot(keys[rows_of(i)], keys[:n], NT)
            scaled = wide(beta_cols[i] * norm_cols[i], n) * gram * norm_row[:, :n]
            lower.append(jnp.where(causal(i, True), scaled, 0.0))
        k32s.append(k32)
        keyss.append(keys)
        norms.append((norm_cols, norm_row))
        betas.append(beta_row)
        c_rows.append(c_row)
        lowers.append(lower)
        tiles += [lower[i][:, rows_of(i)] for i in range(count)]
    inverses = tile_inverses(tiles)
    diagonal = [split(x) for x in inverses]
    lower_parts = [[split(row) for row in lower] for lower in lowers]
    group = range(per)
    solved = [{(i, i): diagonal[s * count + i] for i in range(count)} for s in group]
    exact = [{(i, i): inverses[s * count + i] for i in range(count)} for s in group]
    for off in range(1, count):
        pairs = []
        for s in group:
            for i in range(off, count):
                j = i - off
                left = tuple(x[:, j * TILE : i * TILE] for x in lower_parts[s][i])
                right = tuple(piled([solved[s][k, j][z] for k in range(j, i)]) for z in range(2))
                pairs.append((left, right))
        inner = batch_parts(pairs)
        places = [(s, i) for s in group for i in range(off, count)]
        outer = batch_parts(
            [(diagonal[s * count + i], split(y)) for (s, i), y in zip(places, inner)]
        )
        for (s, i), y in zip(places, outer):
            exact[s][i, i - off] = -y
            solved[s][i, i - off] = split(-y)
    scaled_rows = []
    for s in group:
        norm_cols, beta_row = norms[s][0], betas[s]
        scaled = []
        for i in range(count):
            n = (i + 1) * TILE
            row = [exact[s][i, j] for j in range(i + 1)]
            a_row = (jnp.concatenate(row, axis=1) if i else row[0]) * beta_row[:, :n]
            a_ref[s, rows_of(i), :n] = a_row
            scaled.append(wide(norm_cols[i], n) * a_row)
        scaled_rows.append(scaled)
    keys_t = [jnp.transpose(k32).astype(BF16) for k32 in k32s]
    bts = [
        jnp.concatenate(
            [
                dot_right(keys_t[s][:, j * TILE :], below(scaled_rows[s], j))
                for j in range(count)
            ],
            axis=1,
        )
        for s in group
    ]
    totals = [c_rows[s][:, tokens - 1 :] for s in group]
    fadeds = [bts[s] * jnp.exp(totals[s] - c_rows[s]) for s in group]
    overlaps = [dot_left(bts[s] * norms[s][1], keyss[s]) for s in group]
    states = [dot_left(fadeds[s], v_ref[s]) for s in group]
    for s in group:
        bt_ref[s] = fadeds[s]
        moved = jnp.exp(totals[s]) * (identity - overlaps[s])
        position = step * per + s

        @pl.when(position < half)
        def _():
            other_ref[0, position] = moved
            other_ref[1, position] = states[s]

        @pl.when(position >= half)
        def _():
            mine_ref[0, position - half] = moved
            mine_ref[1, position - half] = states[s]


GROUP = 2


def pick_head(ref, s):
    return ref.at[s] if len(ref.shape) == 3 else ref.at[:, s]


def interleaved(head_body):
    def kernel(scalars_ref, *refs):
        running = [
            head_body(scalars_ref, *[pick_head(ref, s) for ref in refs]) for s in range(GROUP)
        ]
        while running:
            running = [body for body in running if next(body, None) is not None]

    return kernel


def early_kernel(sees_ref, q_ref, k_ref, d_ref, aux_ref, a_ref, carried_ref, w_keys_ref, adj_ref):
    tokens, width = q_ref.shape
    count = tokens // TILE
    levels = adj_ref.shape[0]
    queries, keys = q_ref[...], k_ref[...]
    c_row, norm_row = aux_ref[0:1, :], aux_ref[1:2, :]
    gains = [jnp.exp(t) for t in column(c_row)]
    delta_t = jnp.transpose(d_ref[...].astype(F32)).astype(BF16)
    weight_cols = [column(aux_ref[3 + l : 4 + l, :]) for l in range(levels)]
    span = range(count)
    sizes = [(i + 1) * TILE for i in span]
    wy_keys = [
        dot_left(a_ref[rows_of(i), : sizes[i]] * norm_row[:, : sizes[i]], keys[: sizes[i]])
        for i in span
    ]
    scores = [dot(queries[rows_of(i)], keys[: sizes[i]], NT) for i in span]
    yield 1
    query_key = [jnp.where(causal(i, False), scores[i] * norm_row[:, : sizes[i]], 0.0) for i in span]
    keys_w = piled(wy_keys)
    w_keys_ref[...] = keys_w
    keys_h, keys_l = split(keys_w)
    inner = [
        dot_parts(split(query_key[i]), (keys_h[: sizes[i]], keys_l[: sizes[i]])) for i in span
    ]
    yield 1
    carried = [gains[i] * (queries[rows_of(i)].astype(F32) - inner[i]) for i in span]
    for i in span:
        carried_ref[rows_of(i), :] = carried[i]
    for l in range(levels):
        scaled = piled([weight_cols[l][i] * carried[i] for i in range(count)])
        adj_ref[l] = jnp.where(sees_ref[l] == 1, dot_right(delta_t, scaled), 0.0)


def late_kernel(sides_ref, q_ref, k_ref, v_ref, d_ref, aux_ref, a_ref, local_ref, dq_ref, dvt_ref, gw_ref):
    tokens, width = q_ref.shape
    count = tokens // TILE
    queries, keys, values, delta = q_ref[...], k_ref[...], v_ref[...], d_ref[...]
    d32 = delta.astype(F32)
    c_row, norm_row = aux_ref[0:1, :], aux_ref[1:2, :]
    c_cols = column(c_row)
    w_cols = column(aux_ref[2:3, :])
    wy_values, ratios, faded_a = [], [], []
    for i in range(count):
        n = (i + 1) * TILE
        ratios.append(decay_ratio(c_cols, c_row, i))
        faded_a.append(ratios[i] * a_ref[rows_of(i), :n])
        wy_values.append(dot_left(faded_a[i], values[:n]))
    yield 1
    values_h, values_l = split(piled(wy_values))
    span = range(count)
    sizes = [(i + 1) * TILE for i in span]
    scores = [dot(queries[rows_of(i)], keys[: sizes[i]], NT) for i in span]
    outers = [
        dot(delta[rows_of(i)], values_h[: sizes[i]], NT)
        + dot(delta[rows_of(i)], values_l[: sizes[i]], NT)
        for i in span
    ]
    yield 1
    scales = [ratios[i] * norm_row[:, : sizes[i]] for i in span]
    pqs = [scales[i] * scores[i] for i in span]
    weights = [wide(w_cols[i], sizes[i]) for i in span]
    weighted_pq = [weights[i] * pqs[i] for i in span]
    locals_ = [
        dot_parts(split(pqs[i]), (values_h[: sizes[i]], values_l[: sizes[i]])) for i in span
    ]
    yield 1
    for i in span:
        dq_ref[rows_of(i), :] = dot_left(scales[i] * weights[i] * outers[i], keys[: sizes[i]])
        local_ref[rows_of(i), :] = w_cols[i] * locals_[i]
    dots = [d32[rows_of(i)] * locals_[i] for i in span]
    ones = jnp.ones((8, width), BF16)
    gw_ref[...] = dot_right(ones, piled(dots), NT)[0:1]
    delta_t = jnp.transpose(d32).astype(BF16)
    adjoint_u = jnp.concatenate(
        [dot_right(delta_t[:, j * TILE :], below(weighted_pq, j)) for j in range(count)], axis=1
    )
    yield 1
    u_h, u_l = split(adjoint_u)
    for j in range(count):
        part = (u_h[:, j * TILE :], u_l[:, j * TILE :])
        dvt_ref[:, rows_of(j)] = dot_parts(part, split(below(faded_a, j)))


def cross_kernel(
    sees_ref, k_ref, d_ref, aux_ref, x_ref, carried_ref, w_keys_ref, local_ref, dq_in_ref, gw_in_ref,
    out_ref, dq_ref, gw_ref,
):
    tokens, width = k_ref.shape
    count = tokens // TILE
    levels = x_ref.shape[0]
    keys, delta = k_ref[...], d_ref[...]
    norm_row = aux_ref[1:2, :]
    gains = [jnp.exp(t) for t in column(aux_ref[0:1, :])]
    weight_cols = [column(aux_ref[3 + l : 4 + l, :]) for l in range(levels)]
    states = piled([jnp.where(sees_ref[l] == 1, x_ref[l], 0.0) for l in range(levels)])
    states_h, states_l = split(states)
    keys_h, keys_l = split(w_keys_ref[...])
    ones = jnp.ones((8, width), BF16)
    span = range(count)
    pulled = [
        dot(delta[rows_of(i)], states_h, NT) + dot(delta[rows_of(i)], states_l, NT) for i in span
    ]
    yield 1
    carried = [carried_ref[rows_of(i), :] for i in span]
    lefts = [
        split(jnp.concatenate([weight_cols[l][i] * carried[i] for l in range(levels)], axis=1))
        for i in span
    ]
    crosses = [dot_parts(lefts[i], (states_h, states_l)) for i in span]
    yield 1
    scaled = []
    for i in span:
        terms = [weight_cols[l][i] * pulled[i][:, rows_of(l)] for l in range(levels)]
        scaled.append(gains[i] * functools.reduce(jnp.add, terms))
    scores = [
        dot_parts(split(scaled[i]), (keys_h[: (i + 1) * TILE], keys_l[: (i + 1) * TILE]), NT)
        for i in span
    ]
    weight_rows = [
        [dot_right(ones, carried[i] * pulled[i][:, rows_of(l)], NT)[0:1] for i in span]
        for l in range(levels)
    ]
    yield 1
    for i in span:
        n = (i + 1) * TILE
        kept = jnp.where(causal(i, False), scores[i], 0.0) * norm_row[:, :n]
        dq_ref[rows_of(i), :] = dq_in_ref[rows_of(i), :] + scaled[i] - dot_left(kept, keys[:n])
        out_ref[rows_of(i), :] = local_ref[rows_of(i), :] + crosses[i]
    rows = [gw_in_ref[...]] + [jnp.concatenate(weight_rows[l], axis=1) for l in range(levels)]
    gw_ref[...] = jnp.concatenate(rows, axis=0)


def value_kernel(sizes, per, sides_ref, bt_ref, recv_ref, own_ref, *refs):
    steps = pl.num_programs(0)
    step = pl.program_id(0)
    heads = steps * per
    tokens = bt_ref.shape[2]
    groups = []
    for _ in range(4):
        groups.append(refs[: len(sizes)])
        refs = refs[len(sizes) :]
    outs, dqs, gws, dvts = groups
    out_ref, dq_ref, dv_ref, gw_ref, out_all = refs
    grads = [jnp.where(step < steps // 2, recv_ref[0, s], own_ref[0, s]) for s in range(per)]
    moved = [dot3(grads[s], bt_ref[s]) for s in range(per)]
    places = []
    for s in range(per):
        head = head_at(step * per + s, sides_ref[0], heads)
        places.append((head, pl.ds(head, tokens, stride=heads)))
    start = 0
    for p, size in enumerate(sizes):

        @pl.when((step >= start // per) & (step < (start + size) // per))
        def _(p=p):
            for s, (head, place) in enumerate(places):
                out_all[place, :] = outs[p][s]
                dq_ref[place, :] = dqs[p][s]
                dv_ref[place, :] = jnp.transpose(dvts[p][s] + moved[s])
                for l in range(gw_ref.shape[0]):
                    gw_ref[l, pl.ds(head, 1), :] = gws[p][s, l : l + 1, :]

        start += size

    @pl.when(step == steps - 1)
    def _():
        out_ref[...] = out_all[...].reshape(out_ref.shape).astype(BF16)


def pick(flag, a, b):
    return jnp.where(flag, a, b)


def stored(side, h, count, mine_ref, other_ref, write):
    if other_ref is None:
        write(mine_ref, h)
        return
    half = count // 2

    @pl.when(side == h // half)
    def _():
        write(mine_ref, h % half)

    @pl.when(side != h // half)
    def _():
        write(other_ref, h % half)


def read_half(side, h, own_ref, recv_ref, level):
    if recv_ref is None:
        return own_ref[level, h]
    half = own_ref.shape[1]
    return pick(side == h // half, own_ref[level, h % half], recv_ref[level, h % half])


def up_kernel(r, last, splits, sides_ref, mine_ref, recv_ref, low_m, up_m, low_s, *nexts):
    count = mine_ref.shape[1]
    up = sides_ref[r] == 1
    next_mine, next_other = nexts if splits else (nexts[0], None)
    pairs, s_ups = [], []
    for h in range(count):
        m_low = pick(up, recv_ref[0, h], mine_ref[0, h])
        m_up = pick(up, mine_ref[0, h], recv_ref[0, h])
        s_low = pick(up, recv_ref[1, h], mine_ref[1, h])
        s_ups.append(pick(up, mine_ref[1, h], recv_ref[1, h]))
        low_m[h] = m_low
        up_m[h] = m_up
        low_s[h] = s_low
        parts = split(m_up)
        pairs.append((parts, split(s_low)))
        if not last:
            pairs.append((parts, split(m_low)))
    products = batch_parts(pairs)
    for h in range(count):
        value = products[h : h + 1] if last else products[2 * h : 2 * h + 2]

        def write(ref, place):
            ref[-1 % ref.shape[0], place] = value[0] + s_ups[h]
            if not last:
                ref[0, place] = value[1]

        stored(sides_ref[min(r + 1, sides_ref.shape[0] - 1)], h, count, next_mine, next_other, write)


def down_kernel(r, top, split_in, splits, sides_ref, low_m, low_s, *refs):
    own_ref, *refs = refs
    recv_ref = None
    if split_in or top:
        recv_ref, *refs = refs
    out_own, out_send = refs if splits else (refs[0], None)
    count = low_m.shape[0]
    levels = own_ref.shape[0]
    up = sides_ref[r] == 1
    values, pairs = [], []
    for h in range(count):
        m_parts = split(low_m[h])
        for l in range(levels):
            if top:
                x = pick(sides_ref[r + 1] == 1, recv_ref[0, h], own_ref[0, h])
            else:
                x = read_half(sides_ref[r + 1], h, own_ref, recv_ref, l)
            values.append(x)
            pairs.append((m_parts, split(x)))
    products = batch_parts(pairs)
    for h in range(count):
        out_own[0, h] = low_s[h]
        if out_send is not None:
            out_send[0, h] = low_s[h]
        for l in range(levels):
            x, moved = values[h * levels + l], products[h * levels + l]
            out_own[l + 1, h] = pick(up, moved, x)
            if out_send is not None:
                out_send[l + 1, h] = pick(up, x, moved)


def adjoint_up_kernel(r, sizes, splits, sides_ref, low_m, recv_ref, *refs):
    parts, refs = refs[: len(sizes)], refs[len(sizes) :]
    run_ref, next_mine, *rest = refs
    next_other = rest[0] if splits else None
    count, levels = low_m.shape[0], recv_ref.shape[0]
    up = sides_ref[r] == 1
    pairs, bases = [], []
    for h in range(count):
        p, place = 0, h
        while place >= sizes[p]:
            place -= sizes[p]
            p += 1
        mine_ref = parts[p]
        run_ref[h] = pick(up, mine_ref[0, place], recv_ref[0, h])
        m_parts = split(low_m[h])
        highs = []
        for l in range(1, levels):
            mine, received = mine_ref[l, place], recv_ref[l, h]
            highs.append(pick(up, mine, received))
            bases.append(pick(up, received, mine))
        pairs.append((split(piled(highs)), m_parts))
    products = batch_parts(pairs)
    for h in range(count):
        for l in range(1, levels):
            value = bases[h * (levels - 1) + l - 1] + products[h][rows_of(l - 1)]

            def write(ref, at):
                ref[l - 1, at] = value

            stored(sides_ref[min(r + 1, sides_ref.shape[0] - 1)], h, count, next_mine, next_other, write)


def adjoint_down_kernel(r, top, split_in, splits, sides_ref, run_ref, up_m, *refs):
    own_ref, *refs = refs
    recv_ref = None
    if split_in:
        recv_ref, *refs = refs
    out_own, out_send = refs if splits else (refs[0], None)
    up = sides_ref[r] == 1
    span = range(run_ref.shape[0])
    grads = [read_half(sides_ref[r + 1], h, own_ref, recv_ref, 0) for h in span]
    if top:
        grads = [pick(sides_ref[r + 1] == 1, 0.0, g) for g in grads]
    products = batch_parts([(split(grads[h]), split(up_m[h])) for h in span])
    for h in span:
        low = run_ref[h] + products[h]
        out_own[0, h] = pick(up, grads[h], low)
        if out_send is not None:
            out_send[0, h] = pick(up, low, grads[h])


def whole(shape):
    return pl.BlockSpec(shape, lambda p: (0,) * len(shape))


def headed(*shape, start=0):
    return pl.BlockSpec(
        (GROUP,) + shape, lambda p: (p + start // GROUP,) + (0,) * len(shape)
    )


def second(first, *shape, start=0):
    return pl.BlockSpec(
        (first, GROUP) + shape, lambda p: (0, p + start // GROUP) + (0,) * len(shape)
    )


def struct(*shape, dtype=F32):
    return jax.ShapeDtypeStruct(shape, dtype)


SMEM = pl.BlockSpec(memory_space=pltpu.SMEM)
VMEM = pl.BlockSpec(memory_space=pltpu.VMEM)
HBM = pl.BlockSpec(memory_space=pltpu.HBM)


BIG, MID, LOW = 36, 20, 12


def params(mib):
    return pltpu.CompilerParams(
        dimension_semantics=("arbitrary",), vmem_limit_bytes=mib * 1024 * 1024
    )


def cost(micros, size=1 << 20):
    return pl.CostEstimate(flops=int(micros * 1.1e9), bytes_accessed=size, transcendentals=0)


def small(kernel, name, sides, inputs, outputs):
    return pl.pallas_call(
        kernel,
        in_specs=[SMEM] + [VMEM] * len(inputs),
        out_specs=[VMEM] * len(outputs),
        out_shape=[struct(*o) for o in outputs],
        cost_estimate=cost(1.0),
        compiler_params=pltpu.CompilerParams(vmem_limit_bytes=LOW * 1024 * 1024),
        name=name,
    )(sides, *inputs)


def swap(x, round_bit):
    size = lax.axis_size("ctx")
    return lax.ppermute(x, "ctx", [(i, i ^ 1 << round_bit) for i in range(size)])


class Order:
    def __init__(self):
        self.last = None

    def start(self, scalars):
        if self.last is None:
            return scalars
        return lax.optimization_barrier((scalars, self.last))[0]

    def end(self, outputs):
        self.last = outputs[-1]
        return outputs


EARLY = {"e_o": (0, 4), "e_m1": (4, 2), "e_m2": (6, 2)}
PARTS = ((0, 2), (2, 2), (4, 2), (6, 2))
FOUR_LEVELS = "e_m2 up0 e_o e_m1 up1 l2 ad0 up2 l0 ad1 dn2 l3 ad2 dn1 l1 ed2 dn0 c2 c0 ed1 c3 ed0 c1"


RELEASE = "up1"


def call_order(levels):
    if levels == 4:
        return FOUR_LEVELS.split()
    last = levels - 2
    names = ["e_o", "up0", "e_m1"]
    for r in range(1, last + 1):
        names += [f"up{r}"] + (["e_m2"] if r == 1 else []) + [f"ad{r - 1}"]
    names += ["l2", f"dn{last}", "l3", f"ad{last}", "l0"]
    for r in reversed(range(last)):
        names += [f"dn{r}", f"ed{r + 1}"] + (["l1"] if r == last - 1 else [])
    return names + ["c2", "c3", "ed0", "c0", "c1"]


def shards(
    queries, key_vectors, values, gate_rates, log_decay, level_weights, block_levels, grad_out
):
    levels = lax.axis_size("ctx").bit_length() - 1
    position = lax.axis_index("ctx")
    tokens, heads, width = key_vectors.shape
    half = heads // 2
    ids = jnp.arange(levels, dtype=jnp.int32)
    sides = jnp.right_shift(position, ids) % 2
    sees = sides * (ids < block_levels[0]).astype(jnp.int32)
    per = 2
    state_per = 4
    aux_rows = (levels + 3 + 7) // 8 * 8
    mat = (width, width)
    splits = [heads >> r > 1 for r in range(levels + 1)]
    held = [max(heads >> r, 1) for r in range(levels + 1)]
    packed = whole((tokens, heads, width))
    rows = whole((heads, tokens))
    flat = pltpu.VMEM((tokens * heads, width), F32)

    def grouped(*shape, size=per):
        return pl.BlockSpec((size,) + shape, lambda p: (p,) + (0,) * len(shape))

    def stated(*shape):
        return grouped(*shape, size=state_per)

    tok = struct(heads, tokens, width, dtype=BF16)
    q, k, v, d, aux, a_full, bt, other, mine = pl.pallas_call(
        state_kernel,
        grid=(heads // state_per,),
        in_specs=[SMEM] + [HBM] * 7,
        out_specs=[
            stated(tokens, width), stated(tokens, width), stated(tokens, width),
            stated(tokens, width), stated(aux_rows, tokens), stated(tokens, tokens),
            stated(width, tokens), whole((2, half) + mat), whole((2, half) + mat),
        ],
        out_shape=[
            tok, tok, tok, tok, struct(heads, aux_rows, tokens), struct(heads, tokens, tokens),
            struct(heads, width, tokens), struct(2, half, *mat), struct(2, half, *mat),
        ],
        scratch_shapes=[flat] * 4
        + [
            pltpu.VMEM((heads, tokens), F32),
            pltpu.VMEM((4, tokens, heads, width), BF16),
            pltpu.VMEM((heads, tokens), F32),
            pltpu.VMEM((heads, tokens), F32),
            pltpu.VMEM(level_weights.shape, F32),
            pltpu.SemaphoreType.DMA((7,)),
        ],
        compiler_params=params(BIG),
        cost_estimate=cost(20),
        name="state",
    )(
        sides,
        *[
            pltpu.with_memory_space_constraint(x, pltpu.HBM)
            for x in (
                queries, key_vectors, values, grad_out, gate_rates, log_decay, level_weights
            )
        ],
    )

    order = Order()
    early_outs, late_outs, cross_outs = [{} for _ in range(3)]

    def early(i):
        start, size = EARLY[i]
        early_outs[i] = order.end(pl.pallas_call(
            interleaved(early_kernel),
            grid=(size // GROUP,),
            in_specs=[
                SMEM, headed(tokens, width, start=start), headed(tokens, width, start=start),
                headed(tokens, width, start=start), headed(aux_rows, tokens, start=start),
                headed(tokens, tokens, start=start),
            ],
            out_specs=[headed(tokens, width), headed(tokens, width), second(levels, *mat)],
            out_shape=[
                struct(size, tokens, width), struct(size, tokens, width),
                struct(levels, size, *mat),
            ],
            compiler_params=params(MID),
            cost_estimate=cost(1.1 * size),
            name="early",
        )(order.start(sees), q, k, d, aux, a_full))

    def late(i):
        start, size = PARTS[i]
        late_outs[i] = order.end(pl.pallas_call(
            interleaved(late_kernel),
            grid=(size // GROUP,),
            in_specs=[SMEM] + [headed(tokens, width, start=start)] * 4
            + [headed(aux_rows, tokens, start=start), headed(tokens, tokens, start=start)],
            out_specs=[
                headed(tokens, width), headed(tokens, width), headed(width, tokens),
                headed(1, tokens),
            ],
            out_shape=[
                struct(size, tokens, width), struct(size, tokens, width),
                struct(size, width, tokens), struct(size, 1, tokens),
            ],
            compiler_params=params(MID),
            cost_estimate=cost(1.2 * size),
            name="late",
        )(order.start(sides), q, k, v, d, aux, a_full))

    def cross(i, x, x_start):
        start, size = PARTS[i]
        name = next(e for e, (s, n) in EARLY.items() if s <= start < s + n)
        skip = start - EARLY[name][0]
        carried, w_keys, _ = early_outs[name]
        local, dq, _, gw = late_outs[i]
        cross_outs[i] = order.end(pl.pallas_call(
            interleaved(cross_kernel),
            grid=(size // GROUP,),
            in_specs=[
                SMEM, headed(tokens, width, start=start), headed(tokens, width, start=start),
                headed(aux_rows, tokens, start=start), second(levels, *mat, start=x_start),
                headed(tokens, width, start=skip), headed(tokens, width, start=skip),
                headed(tokens, width), headed(tokens, width), headed(1, tokens),
            ],
            out_specs=[
                headed(tokens, width), headed(tokens, width), headed(levels + 1, tokens),
            ],
            out_shape=[
                struct(size, tokens, width), struct(size, tokens, width),
                struct(size, levels + 1, tokens),
            ],
            compiler_params=params(MID),
            cost_estimate=cost(1.4 * size),
            name="cross",
        )(order.start(sees), k, d, aux, x, carried, w_keys, local, dq, gw))

    lows, ups, low_states, runs = [], [], [], []

    def short(kernel, name, inputs, outputs):
        return order.end(small(kernel, name, order.start(sides), inputs, outputs))

    def up_round(r, mine, received):
        last = r + 1 == levels - 1
        n, many = held[r + 1], splits[r + 1]
        payload = (1 if last else 2, held[r + 2]) + mat
        low_m, up_m, low_s, *following = short(
            functools.partial(up_kernel, r, last, many), f"up{r}", [mine, received],
            [(n, *mat)] * 3 + [payload] * (2 if many else 1),
        )
        lows.append(low_m)
        ups.append(up_m)
        low_states.append(low_s)
        return following[0], following[-1]

    def adjoint_round(r, parts, received):
        many = splits[r + 1]
        following = (levels - r - 1, held[r + 2]) + mat
        run, *rest = short(
            functools.partial(adjoint_up_kernel, r, [p.shape[1] for p in parts], many),
            f"adjoint_up{r}", [lows[r], received, *parts],
            [(held[r + 1], *mat)] + [following] * (2 if many else 1),
        )
        runs.append(run)
        return rest[0], rest[-1]

    def down_round(r, own, received):
        top = r == levels - 2
        split_in = splits[r + 1]
        many = splits[r]
        inputs = [lows[r], low_states[r], own] + ([received] if split_in or top else [])
        shape = (levels - r, held[r + 1]) + mat
        outs = short(
            functools.partial(down_kernel, r, top, split_in, many), f"down{r}", inputs,
            [shape] * (2 if many else 1),
        )
        return outs[0], outs[-1]

    def adjoint_down_round(r, own, received):
        top = r == levels - 2
        split_in = splits[r + 1]
        many = splits[r]
        inputs = [runs[r], ups[r], own] + ([received] if split_in else [])
        outs = short(
            functools.partial(adjoint_down_kernel, r, top, split_in, many), f"adjoint_down{r}",
            inputs, [(1, held[r + 1], *mat)] * (2 if many else 1),
        )
        return outs[0], outs[-1]

    moves = {}

    def adjoint_send(x, r):
        moves["adjoint", r] = swap(x, r)

    def step(kind, r):
        if kind == "up":
            mine, send = up_round(r, moves["mine", r], moves["pair", r])
            moves["mine", r + 1] = mine
            moves["pair", r + 1] = swap(send, r + 1)
        elif kind == "ad":
            parts = moves["adjoint_mine", r] if r else [early_outs["e_m1"][2], early_outs["e_m2"][2]]
            mine, send = adjoint_round(r, parts, moves["adjoint", r])
            moves["adjoint_mine", r + 1] = [mine]
            adjoint_send(send, r + 1)
        elif kind == "dn":
            top = r == levels - 2
            own = moves["mine", r + 1] if top else moves["own", r + 1]
            received = moves["pair", r + 1] if top else moves.get(("state", r + 1))
            own, send = down_round(r, own, received)
            moves["own", r] = own
            if splits[r]:
                moves["state", r] = swap(send, r)
        else:
            top = r == levels - 2
            own = moves["adjoint", r + 1][:1] if top else moves["grad_own", r + 1]
            own, send = adjoint_down_round(r, own, moves.get(("grad", r + 1)))
            moves["grad_own", r] = own
            if splits[r]:
                moves["grad", r] = swap(send, r)

    def cover(name):
        kind, i = name[0], name[1:]
        if kind == "e":
            early(name)
        elif kind == "l":
            late(int(i))
        else:
            i = int(i)
            start = PARTS[i][0]
            if start < half:
                cross(i, moves["state", 0], start)
            else:
                cross(i, moves["own", 0], start - half)

    moves["mine", 0] = mine
    moves["pair", 0] = swap(other, 0)
    for name in call_order(levels):
        if name[:2] in ("up", "ad", "dn", "ed"):
            step(name[:2], int(name[2:]))
            if name == RELEASE:
                adjoint_send(order.start(early_outs["e_o"][2]), 0)
        else:
            cover(name)
    grad_own, grad_received = moves["grad_own", 0], moves["grad", 0]

    def part_spec(i, *shape):
        first, size = (n // per for n in PARTS[i])
        return pl.BlockSpec(
            (per,) + shape, lambda p: (jnp.clip(p - first, 0, size - 1),) + (0,) * len(shape)
        )

    indices = range(len(PARTS))
    layer_out, grad_queries, grad_values, grad_level_weights = pl.pallas_call(
        functools.partial(value_kernel, [n for _, n in PARTS], per),
        grid=(heads // per,),
        in_specs=[
            SMEM, grouped(width, tokens),
            pl.BlockSpec((1, per) + mat, lambda p: (0, jnp.minimum(p, half // per - 1), 0, 0)),
            pl.BlockSpec((1, per) + mat, lambda p: (0, jnp.maximum(p - half // per, 0), 0, 0)),
        ]
        + [part_spec(i, tokens, width) for i in indices]
        + [part_spec(i, tokens, width) for i in indices]
        + [part_spec(i, levels + 1, tokens) for i in indices]
        + [part_spec(i, width, tokens) for i in indices],
        out_specs=[
            packed, whole((tokens * heads, width)), whole((tokens * heads, width)),
            whole((levels + 1, heads, tokens)),
        ],
        out_shape=[
            struct(tokens, heads, width, dtype=BF16), struct(tokens * heads, width),
            struct(tokens * heads, width), struct(levels + 1, heads, tokens),
        ],
        scratch_shapes=[flat],
        compiler_params=params(BIG),
        cost_estimate=cost(5),
        name="value",
    )(
        order.start(sides), bt, grad_received, grad_own,
        *[cross_outs[i][0] for i in indices], *[cross_outs[i][1] for i in indices],
        *[cross_outs[i][2] for i in indices], *[late_outs[i][2] for i in indices],
    )
    shape = (tokens, heads, width)
    return (
        layer_out, grad_queries.reshape(shape), grad_values.reshape(shape), grad_level_weights
    )


def solution(mesh):
    tokens = P(("groups", "ctx"), None, None)
    rows = P(None, ("groups", "ctx"))
    weights = P(None, None, ("groups", "ctx"))
    return jax.shard_map(
        shards,
        mesh=mesh,
        in_specs=(tokens, tokens, tokens, rows, rows, weights, P(("groups", "ctx")), tokens),
        out_specs=(tokens, tokens, tokens, weights),
        check_vma=False,
    )
```

```python
import functools

import jax
import jax.numpy as jnp
from jax import lax
from jax.experimental import pallas as pl
from jax.experimental.pallas import tpu as pltpu
from jax.sharding import PartitionSpec as P

F32 = jnp.float32
BF16 = jnp.bfloat16
TILE = 128
SUB = 16
NN = (((1,), (0,)), ((), ()))
NT = (((1,), (1,)), ((), ()))


def split(x):
    high = x.astype(BF16)
    return high, (x - high.astype(F32)).astype(BF16)


def dot(a, b, dims=NN):
    return lax.dot_general(a, b, dims, preferred_element_type=F32)


def dot_left(a, b, dims=NN):
    return dot(beside(split(a), 1), beside((b, b), dims[0][1][0]), dims)


def beside(parts, axis):
    return jnp.concatenate(parts, axis=axis)


def fold(x):
    half = x.shape[1] // 2
    return x[:, :half] + x[:, half:]


def dot_right_parts(a, b, dims=NN):
    depth = dims[0][1][0]
    if a.shape[1] <= TILE:
        return dot(beside((a, a), 1), beside(b, depth), dims)
    if b[0].shape[1 - depth] <= TILE:
        return fold(dot(a, beside(b, 1 - depth), dims))
    return dot(a, b[0], dims) + dot(a, b[1], dims)


def dot_right(a, b, dims=NN):
    return dot_right_parts(a, split(b), dims)


def dot_parts(a, b, dims=NN):
    depth = dims[0][1][0]
    left = beside(a, 1)
    if b[0].shape[1 - depth] <= TILE:
        both = beside(b, 1 - depth)
        return fold(dot(left, beside((both, both), depth), dims))
    return dot(left, beside((b[0], b[0]), depth), dims) + dot(a[0], b[1], dims)


def dot3(a, b, dims=NN):
    return dot_parts(split(a), split(b), dims)


def batch_parts(pairs, dims=NN):
    return [dot_parts(a, b, dims) for a, b in pairs]


def column(row):
    return [
        jnp.transpose(jnp.broadcast_to(row[:, s : s + TILE], (TILE, TILE)))
        for s in range(0, row.shape[1], TILE)
    ]


def wide(tile, width):
    return jnp.concatenate([tile] * (width // TILE), axis=1) if width > TILE else tile


def rows_of(i):
    return slice(i * TILE, (i + 1) * TILE)


def key_norms(keys):
    k32 = keys.astype(F32)
    scale = 1.0 / jnp.sqrt(jnp.sum(k32 * k32, axis=1, keepdims=True) + 1e-06)
    cols = [
        jnp.broadcast_to(scale[rows_of(i)], (TILE, TILE)) for i in range(keys.shape[0] // TILE)
    ]
    row = jnp.concatenate([jnp.transpose(c)[0:1] for c in cols], axis=1)
    return cols, row


def causal(i, strict):
    width = (i + 1) * TILE
    r = lax.broadcasted_iota(jnp.int32, (TILE, width), 0) + i * TILE
    c = lax.broadcasted_iota(jnp.int32, (TILE, width), 1)
    return r > c if strict else r >= c


def decay_ratio(c_cols, c_row, i):
    width = (i + 1) * TILE
    keep = causal(i, False)
    spread = wide(c_cols[i], width) - c_row[:, :width]
    return jnp.where(keep, jnp.exp(jnp.where(keep, spread, 0.0)), 0.0)


def small_inverses(blocks):
    lane = lax.broadcasted_iota(jnp.int32, (8, TILE), 1)
    sub_row = lax.broadcasted_iota(jnp.int32, (8, TILE), 0)
    owner = lane // SUB
    within = lane - owner * SUB
    first = owner * SUB
    tiles = SUB // 8
    coefs, sols = [], []
    for block in blocks:
        packed, unit = [], []
        for q in range(tiles):
            piece = jnp.zeros((8, TILE), F32)
            for b in range(TILE // SUB):
                start = b * SUB + q * 8
                piece = jnp.where(owner == b, block[start : start + 8], piece)
            packed.append(piece)
            unit.append(jnp.where(within == sub_row + q * 8, 1.0, 0.0).astype(F32))
        coefs.append(packed)
        sols.append(unit)
    for j in range(SUB - 1):
        index = first + j
        for coef, sol in zip(coefs, sols):
            row = jnp.broadcast_to(sol[j // 8][j % 8 : j % 8 + 1], (8, TILE))
            for q in range((j + 1) // 8, tiles):
                factor = jnp.take_along_axis(coef[q], index, axis=1, mode="promise_in_bounds")
                sol[q] = sol[q] - factor * row
    out = []
    for sol in sols:
        pieces = []
        for b in range(TILE // SUB):
            for q in range(tiles):
                pieces.append(jnp.where(owner == b, sol[q], 0.0))
        out.append(jnp.concatenate(pieces, axis=0))
    return out


def tile_inverses(blocks):
    r = lax.broadcasted_iota(jnp.int32, (TILE, TILE), 0)
    c = lax.broadcasted_iota(jnp.int32, (TILE, TILE), 1)
    inverses = small_inverses(blocks)
    size = SUB
    while size < TILE:
        below_half = (r // size == c // size + 1) & (r // (2 * size) == c // (2 * size))
        parts = [split(x) for x in inverses]
        inner = batch_parts(
            [(split(jnp.where(below_half, t, 0.0)), x) for t, x in zip(blocks, parts)]
        )
        outer = batch_parts([(x, split(y)) for x, y in zip(parts, inner)])
        inverses = [x - y for x, y in zip(inverses, outer)]
        size *= 2
    return inverses


def piled(parts):
    return jnp.concatenate(parts, axis=0) if len(parts) > 1 else parts[0]


def below(rows, j):
    return piled([rows[i][:, rows_of(j)] for i in range(j, len(rows))])


def head_at(position, side, heads):
    return (position + (1 - side) * (heads // 2)) % heads


def state_kernel(
    sides_ref, q_in, k_in, v_in, d_in, beta_ref, decay_ref, w_ref,
    q_ref, k_ref, v_ref, d_ref, aux_ref, a_ref, bt_ref, other_ref, mine_ref,
    q_all, k_all, v_all, d_all, c_all, packed_all, beta_all, decay_all, w_all, sems,
):
    tokens, heads, width = k_in.shape
    per = k_ref.shape[0]
    half = heads // 2
    step = pl.program_id(0)
    count = tokens // TILE

    @pl.when(step == 0)
    def _():
        sources = (decay_ref, beta_ref, w_ref, k_in, v_in, q_in, d_in)
        targets = (decay_all, beta_all, w_all, *(packed_all.at[i] for i in range(4)))
        copies = [
            pltpu.make_async_copy(source, target, sems.at[i])
            for i, (source, target) in enumerate(zip(sources, targets))
        ]
        for copy in copies:
            copy.start()
        for copy in copies:
            copy.wait()
        for i, target in enumerate((k_all, v_all, q_all, d_all)):
            target[...] = packed_all[i].astype(F32).reshape(tokens * heads, width)
        r = lax.broadcasted_iota(jnp.int32, (tokens, tokens), 0)
        c = lax.broadcasted_iota(jnp.int32, (tokens, tokens), 1)
        upper = jnp.where(r <= c, 1.0, 0.0).astype(BF16)
        decay = decay_all[...]
        high, rest = split(decay)
        low = (decay - high.astype(F32) - rest.astype(F32)).astype(BF16)
        c_all[...] = dot(high, upper) + (dot(rest, upper) + dot(low, upper))

    r = lax.broadcasted_iota(jnp.int32, (width, width), 0)
    c = lax.broadcasted_iota(jnp.int32, (width, width), 1)
    identity = jnp.where(r == c, 1.0, 0.0).astype(F32)
    k32s, keyss, norms, betas, c_rows, lowers, tiles = [], [], [], [], [], [], []
    for s in range(per):
        head = head_at(step * per + s, sides_ref[0], heads)
        mine = pl.ds(head, tokens, stride=heads)
        k32 = k_all[mine, :]
        keys = k32.astype(BF16)
        q_ref[s] = q_all[mine, :].astype(BF16)
        k_ref[s] = keys
        v_ref[s] = v_all[mine, :].astype(BF16)
        d_ref[s] = d_all[mine, :].astype(BF16)
        beta_row = beta_all[pl.ds(head, 1), :]
        c_row = c_all[pl.ds(head, 1), :]
        norm_cols, norm_row = key_norms(keys)
        aux = [c_row, norm_row] + [w_all[l, pl.ds(head, 1), :] for l in range(w_all.shape[0])]
        aux_ref[s, : len(aux)] = jnp.concatenate(aux, axis=0)
        beta_cols = column(beta_row)
        lower = []
        for i in range(count):
            n = (i + 1) * TILE
            gram = dot(keys[rows_of(i)], keys[:n], NT)
            scaled = wide(beta_cols[i] * norm_cols[i], n) * gram * norm_row[:, :n]
            lower.append(jnp.where(causal(i, True), scaled, 0.0))
        k32s.append(k32)
        keyss.append(keys)
        norms.append((norm_cols, norm_row))
        betas.append(beta_row)
        c_rows.append(c_row)
        lowers.append(lower)
        tiles += [lower[i][:, rows_of(i)] for i in range(count)]
    inverses = tile_inverses(tiles)
    diagonal = [split(x) for x in inverses]
    lower_parts = [[split(row) for row in lower] for lower in lowers]
    group = range(per)
    solved = [{(i, i): diagonal[s * count + i] for i in range(count)} for s in group]
    exact = [{(i, i): inverses[s * count + i] for i in range(count)} for s in group]
    for off in range(1, count):
        pairs = []
        for s in group:
            for i in range(off, count):
                j = i - off
                left = tuple(x[:, j * TILE : i * TILE] for x in lower_parts[s][i])
                right = tuple(piled([solved[s][k, j][z] for k in range(j, i)]) for z in range(2))
                pairs.append((left, right))
        inner = batch_parts(pairs)
        places = [(s, i) for s in group for i in range(off, count)]
        outer = batch_parts(
            [(diagonal[s * count + i], split(y)) for (s, i), y in zip(places, inner)]
        )
        for (s, i), y in zip(places, outer):
            exact[s][i, i - off] = -y
            solved[s][i, i - off] = split(-y)
    scaled_rows = []
    for s in group:
        norm_cols, beta_row = norms[s][0], betas[s]
        scaled = []
        for i in range(count):
            n = (i + 1) * TILE
            row = [exact[s][i, j] for j in range(i + 1)]
            a_row = (jnp.concatenate(row, axis=1) if i else row[0]) * beta_row[:, :n]
            a_ref[s, rows_of(i), :n] = a_row
            scaled.append(wide(norm_cols[i], n) * a_row)
        scaled_rows.append(scaled)
    keys_t = [jnp.transpose(k32).astype(BF16) for k32 in k32s]
    bts = [
        jnp.concatenate(
            [
                dot_right(keys_t[s][:, j * TILE :], below(scaled_rows[s], j))
                for j in range(count)
            ],
            axis=1,
        )
        for s in group
    ]
    totals = [c_rows[s][:, tokens - 1 :] for s in group]
    fadeds = [bts[s] * jnp.exp(totals[s] - c_rows[s]) for s in group]
    overlaps = [dot_left(bts[s] * norms[s][1], keyss[s]) for s in group]
    states = [dot_left(fadeds[s], v_ref[s]) for s in group]
    for s in group:
        bt_ref[s] = fadeds[s]
        moved = jnp.exp(totals[s]) * (identity - overlaps[s])
        position = step * per + s

        @pl.when(position < half)
        def _():
            other_ref[0, position] = moved
            other_ref[1, position] = states[s]

        @pl.when(position >= half)
        def _():
            mine_ref[0, position - half] = moved
            mine_ref[1, position - half] = states[s]


GROUP = 2


def pick_head(ref, s):
    return ref.at[s] if len(ref.shape) == 3 else ref.at[:, s]


def interleaved(head_body):
    def kernel(scalars_ref, *refs):
        running = [
            head_body(scalars_ref, *[pick_head(ref, s) for ref in refs]) for s in range(GROUP)
        ]
        while running:
            running = [body for body in running if next(body, None) is not None]

    return kernel


def early_kernel(sees_ref, q_ref, k_ref, d_ref, aux_ref, a_ref, carried_ref, w_keys_ref, adj_ref):
    tokens, width = q_ref.shape
    count = tokens // TILE
    levels = adj_ref.shape[0]
    queries, keys = q_ref[...], k_ref[...]
    c_row, norm_row = aux_ref[0:1, :], aux_ref[1:2, :]
    gains = [jnp.exp(t) for t in column(c_row)]
    delta_t = jnp.transpose(d_ref[...].astype(F32)).astype(BF16)
    weight_cols = [column(aux_ref[3 + l : 4 + l, :]) for l in range(levels)]
    span = range(count)
    sizes = [(i + 1) * TILE for i in span]
    wy_keys = [
        dot_left(a_ref[rows_of(i), : sizes[i]] * norm_row[:, : sizes[i]], keys[: sizes[i]])
        for i in span
    ]
    scores = [dot(queries[rows_of(i)], keys[: sizes[i]], NT) for i in span]
    yield 1
    query_key = [jnp.where(causal(i, False), scores[i] * norm_row[:, : sizes[i]], 0.0) for i in span]
    keys_w = piled(wy_keys)
    w_keys_ref[...] = keys_w
    keys_h, keys_l = split(keys_w)
    inner = [
        dot_parts(split(query_key[i]), (keys_h[: sizes[i]], keys_l[: sizes[i]])) for i in span
    ]
    yield 1
    carried = [gains[i] * (queries[rows_of(i)].astype(F32) - inner[i]) for i in span]
    for i in span:
        carried_ref[rows_of(i), :] = carried[i]
    for l in range(levels):
        scaled = piled([weight_cols[l][i] * carried[i] for i in range(count)])
        adj_ref[l] = jnp.where(sees_ref[l] == 1, dot_right(delta_t, scaled), 0.0)


def late_kernel(sides_ref, q_ref, k_ref, v_ref, d_ref, aux_ref, a_ref, local_ref, dq_ref, dvt_ref, gw_ref):
    tokens, width = q_ref.shape
    count = tokens // TILE
    queries, keys, values, delta = q_ref[...], k_ref[...], v_ref[...], d_ref[...]
    d32 = delta.astype(F32)
    c_row, norm_row = aux_ref[0:1, :], aux_ref[1:2, :]
    c_cols = column(c_row)
    w_cols = column(aux_ref[2:3, :])
    wy_values, ratios, faded_a = [], [], []
    for i in range(count):
        n = (i + 1) * TILE
        ratios.append(decay_ratio(c_cols, c_row, i))
        faded_a.append(ratios[i] * a_ref[rows_of(i), :n])
        wy_values.append(dot_left(faded_a[i], values[:n]))
    yield 1
    values_h, values_l = split(piled(wy_values))
    span = range(count)
    sizes = [(i + 1) * TILE for i in span]
    scores = [dot(queries[rows_of(i)], keys[: sizes[i]], NT) for i in span]
    outers = [
        dot_right_parts(delta[rows_of(i)], (values_h[: sizes[i]], values_l[: sizes[i]]), NT)
        for i in span
    ]
    yield 1
    scales = [ratios[i] * norm_row[:, : sizes[i]] for i in span]
    pqs = [scales[i] * scores[i] for i in span]
    weights = [wide(w_cols[i], sizes[i]) for i in span]
    weighted_pq = [weights[i] * pqs[i] for i in span]
    locals_ = [
        dot_parts(split(pqs[i]), (values_h[: sizes[i]], values_l[: sizes[i]])) for i in span
    ]
    yield 1
    for i in span:
        dq_ref[rows_of(i), :] = dot_left(scales[i] * weights[i] * outers[i], keys[: sizes[i]])
        local_ref[rows_of(i), :] = w_cols[i] * locals_[i]
    dots = [d32[rows_of(i)] * locals_[i] for i in span]
    ones = jnp.ones((8, width), BF16)
    gw_ref[...] = dot_right(ones, piled(dots), NT)[0:1]
    delta_t = jnp.transpose(d32).astype(BF16)
    adjoint_u = jnp.concatenate(
        [dot_right(delta_t[:, j * TILE :], below(weighted_pq, j)) for j in range(count)], axis=1
    )
    yield 1
    u_h, u_l = split(adjoint_u)
    for j in range(count):
        part = (u_h[:, j * TILE :], u_l[:, j * TILE :])
        dvt_ref[:, rows_of(j)] = dot_parts(part, split(below(faded_a, j)))


def cross_kernel(
    sees_ref, k_ref, d_ref, aux_ref, x_ref, carried_ref, w_keys_ref, local_ref, dq_in_ref, gw_in_ref,
    out_ref, dq_ref, gw_ref,
):
    tokens, width = k_ref.shape
    count = tokens // TILE
    levels = x_ref.shape[0]
    keys, delta = k_ref[...], d_ref[...]
    norm_row = aux_ref[1:2, :]
    gains = [jnp.exp(t) for t in column(aux_ref[0:1, :])]
    weight_cols = [column(aux_ref[3 + l : 4 + l, :]) for l in range(levels)]
    states = piled([jnp.where(sees_ref[l] == 1, x_ref[l], 0.0) for l in range(levels)])
    states_h, states_l = split(states)
    keys_h, keys_l = split(w_keys_ref[...])
    ones = jnp.ones((8, width), BF16)
    span = range(count)
    pulled = [
        dot_right_parts(delta[rows_of(i)], (states_h, states_l), NT) for i in span
    ]
    yield 1
    carried = [carried_ref[rows_of(i), :] for i in span]
    lefts = [
        split(jnp.concatenate([weight_cols[l][i] * carried[i] for l in range(levels)], axis=1))
        for i in span
    ]
    crosses = [dot_parts(lefts[i], (states_h, states_l)) for i in span]
    yield 1
    scaled = []
    for i in span:
        terms = [weight_cols[l][i] * pulled[i][:, rows_of(l)] for l in range(levels)]
        scaled.append(gains[i] * functools.reduce(jnp.add, terms))
    scores = [
        dot_parts(split(scaled[i]), (keys_h[: (i + 1) * TILE], keys_l[: (i + 1) * TILE]), NT)
        for i in span
    ]
    weight_rows = [
        [dot_right(ones, carried[i] * pulled[i][:, rows_of(l)], NT)[0:1] for i in span]
        for l in range(levels)
    ]
    yield 1
    for i in span:
        n = (i + 1) * TILE
        kept = jnp.where(causal(i, False), scores[i], 0.0) * norm_row[:, :n]
        dq_ref[rows_of(i), :] = dq_in_ref[rows_of(i), :] + scaled[i] - dot_left(kept, keys[:n])
        out_ref[rows_of(i), :] = local_ref[rows_of(i), :] + crosses[i]
    rows = [gw_in_ref[...]] + [jnp.concatenate(weight_rows[l], axis=1) for l in range(levels)]
    gw_ref[...] = jnp.concatenate(rows, axis=0)


def value_kernel(sizes, per, sides_ref, bt_ref, recv_ref, own_ref, *refs):
    steps = pl.num_programs(0)
    step = pl.program_id(0)
    heads = steps * per
    tokens = bt_ref.shape[2]
    groups = []
    for _ in range(4):
        groups.append(refs[: len(sizes)])
        refs = refs[len(sizes) :]
    outs, dqs, gws, dvts = groups
    out_ref, dq_ref, dv_ref, gw_ref, out_all = refs
    grads = [jnp.where(step < steps // 2, recv_ref[0, s], own_ref[0, s]) for s in range(per)]
    moved = [dot3(grads[s], bt_ref[s]) for s in range(per)]
    places = []
    for s in range(per):
        head = head_at(step * per + s, sides_ref[0], heads)
        places.append((head, pl.ds(head, tokens, stride=heads)))
    start = 0
    for p, size in enumerate(sizes):

        @pl.when((step >= start // per) & (step < (start + size) // per))
        def _(p=p):
            for s, (head, place) in enumerate(places):
                out_all[place, :] = outs[p][s]
                dq_ref[place, :] = dqs[p][s]
                dv_ref[place, :] = jnp.transpose(dvts[p][s] + moved[s])
                for l in range(gw_ref.shape[0]):
                    gw_ref[l, pl.ds(head, 1), :] = gws[p][s, l : l + 1, :]

        start += size

    @pl.when(step == steps - 1)
    def _():
        out_ref[...] = out_all[...].reshape(out_ref.shape).astype(BF16)


def pick(flag, a, b):
    return jnp.where(flag, a, b)


def stored(side, h, count, mine_ref, other_ref, write):
    if other_ref is None:
        write(mine_ref, h)
        return
    half = count // 2

    @pl.when(side == h // half)
    def _():
        write(mine_ref, h % half)

    @pl.when(side != h // half)
    def _():
        write(other_ref, h % half)


def read_half(side, h, own_ref, recv_ref, level):
    if recv_ref is None:
        return own_ref[level, h]
    half = own_ref.shape[1]
    return pick(side == h // half, own_ref[level, h % half], recv_ref[level, h % half])


def up_kernel(r, last, splits, sides_ref, mine_ref, recv_ref, low_m, up_m, low_s, *nexts):
    count = mine_ref.shape[1]
    up = sides_ref[r] == 1
    next_mine, next_other = nexts if splits else (nexts[0], None)
    pairs, s_ups = [], []
    for h in range(count):
        m_low = pick(up, recv_ref[0, h], mine_ref[0, h])
        m_up = pick(up, mine_ref[0, h], recv_ref[0, h])
        s_low = pick(up, recv_ref[1, h], mine_ref[1, h])
        s_ups.append(pick(up, mine_ref[1, h], recv_ref[1, h]))
        low_m[h] = m_low
        up_m[h] = m_up
        low_s[h] = s_low
        parts = split(m_up)
        pairs.append((parts, split(s_low)))
        if not last:
            pairs.append((parts, split(m_low)))
    products = batch_parts(pairs)
    for h in range(count):
        value = products[h : h + 1] if last else products[2 * h : 2 * h + 2]

        def write(ref, place):
            ref[-1 % ref.shape[0], place] = value[0] + s_ups[h]
            if not last:
                ref[0, place] = value[1]

        stored(sides_ref[min(r + 1, sides_ref.shape[0] - 1)], h, count, next_mine, next_other, write)


def down_kernel(r, top, split_in, splits, sides_ref, low_m, low_s, *refs):
    own_ref, *refs = refs
    recv_ref = None
    if split_in or top:
        recv_ref, *refs = refs
    out_own, out_send = refs if splits else (refs[0], None)
    count = low_m.shape[0]
    levels = own_ref.shape[0]
    up = sides_ref[r] == 1
    values, pairs = [], []
    for h in range(count):
        m_parts = split(low_m[h])
        for l in range(levels):
            if top:
                x = pick(sides_ref[r + 1] == 1, recv_ref[0, h], own_ref[0, h])
            else:
                x = read_half(sides_ref[r + 1], h, own_ref, recv_ref, l)
            values.append(x)
            pairs.append((m_parts, split(x)))
    products = batch_parts(pairs)
    for h in range(count):
        out_own[0, h] = low_s[h]
        if out_send is not None:
            out_send[0, h] = low_s[h]
        for l in range(levels):
            x, moved = values[h * levels + l], products[h * levels + l]
            out_own[l + 1, h] = pick(up, moved, x)
            if out_send is not None:
                out_send[l + 1, h] = pick(up, x, moved)


def adjoint_up_kernel(r, sizes, splits, sides_ref, low_m, recv_ref, *refs):
    parts, refs = refs[: len(sizes)], refs[len(sizes) :]
    run_ref, next_mine, *rest = refs
    next_other = rest[0] if splits else None
    count, levels = low_m.shape[0], recv_ref.shape[0]
    up = sides_ref[r] == 1
    pairs, bases = [], []
    for h in range(count):
        p, place = 0, h
        while place >= sizes[p]:
            place -= sizes[p]
            p += 1
        mine_ref = parts[p]
        run_ref[h] = pick(up, mine_ref[0, place], recv_ref[0, h])
        m_parts = split(low_m[h])
        highs = []
        for l in range(1, levels):
            mine, received = mine_ref[l, place], recv_ref[l, h]
            highs.append(pick(up, mine, received))
            bases.append(pick(up, received, mine))
        pairs.append((split(piled(highs)), m_parts))
    products = batch_parts(pairs)
    for h in range(count):
        for l in range(1, levels):
            value = bases[h * (levels - 1) + l - 1] + products[h][rows_of(l - 1)]

            def write(ref, at):
                ref[l - 1, at] = value

            stored(sides_ref[min(r + 1, sides_ref.shape[0] - 1)], h, count, next_mine, next_other, write)


def adjoint_down_kernel(r, top, split_in, splits, sides_ref, run_ref, up_m, *refs):
    own_ref, *refs = refs
    recv_ref = None
    if split_in:
        recv_ref, *refs = refs
    out_own, out_send = refs if splits else (refs[0], None)
    up = sides_ref[r] == 1
    span = range(run_ref.shape[0])
    grads = [read_half(sides_ref[r + 1], h, own_ref, recv_ref, 0) for h in span]
    if top:
        grads = [pick(sides_ref[r + 1] == 1, 0.0, g) for g in grads]
    products = batch_parts([(split(grads[h]), split(up_m[h])) for h in span])
    for h in span:
        low = run_ref[h] + products[h]
        out_own[0, h] = pick(up, grads[h], low)
        if out_send is not None:
            out_send[0, h] = pick(up, low, grads[h])


def whole(shape):
    return pl.BlockSpec(shape, lambda p: (0,) * len(shape))


def headed(*shape, start=0):
    return pl.BlockSpec(
        (GROUP,) + shape, lambda p: (p + start // GROUP,) + (0,) * len(shape)
    )


def second(first, *shape, start=0):
    return pl.BlockSpec(
        (first, GROUP) + shape, lambda p: (0, p + start // GROUP) + (0,) * len(shape)
    )


def struct(*shape, dtype=F32):
    return jax.ShapeDtypeStruct(shape, dtype)


SMEM = pl.BlockSpec(memory_space=pltpu.SMEM)
VMEM = pl.BlockSpec(memory_space=pltpu.VMEM)
HBM = pl.BlockSpec(memory_space=pltpu.HBM)


BIG, MID, LOW = 36, 20, 12


def params(mib):
    return pltpu.CompilerParams(
        dimension_semantics=("arbitrary",), vmem_limit_bytes=mib * 1024 * 1024
    )


def cost(micros, size=1 << 20):
    return pl.CostEstimate(flops=int(micros * 1.1e9), bytes_accessed=size, transcendentals=0)


def small(kernel, name, sides, inputs, outputs):
    return pl.pallas_call(
        kernel,
        in_specs=[SMEM] + [VMEM] * len(inputs),
        out_specs=[VMEM] * len(outputs),
        out_shape=[struct(*o) for o in outputs],
        cost_estimate=cost(1.0),
        compiler_params=pltpu.CompilerParams(vmem_limit_bytes=LOW * 1024 * 1024),
        name=name,
    )(sides, *inputs)


def swap(x, round_bit):
    size = lax.axis_size("ctx")
    return lax.ppermute(x, "ctx", [(i, i ^ 1 << round_bit) for i in range(size)])


class Order:
    def __init__(self):
        self.last = None

    def start(self, scalars):
        if self.last is None:
            return scalars
        return lax.optimization_barrier((scalars, self.last))[0]

    def end(self, outputs):
        self.last = outputs[-1]
        return outputs


EARLY = {"e_o": (0, 4), "e_m1": (4, 2), "e_m2": (6, 2)}
PARTS = ((0, 2), (2, 2), (4, 2), (6, 2))
FOUR_LEVELS = "e_m2 up0 e_o e_m1 up1 ad0 up2 l2 l0 dn2 ad1 l3 dn1 ad2 l1 ed2 dn0 c2 c0 ed1 c3 ed0 c1"


RELEASE = "up1"


def call_order(levels):
    if levels == 4:
        return FOUR_LEVELS.split()
    last = levels - 2
    names = ["e_o", "up0", "e_m1"]
    for r in range(1, last + 1):
        names += [f"up{r}"] + (["e_m2"] if r == 1 else []) + [f"ad{r - 1}"]
    names += ["l2", f"dn{last}", "l3", f"ad{last}", "l0"]
    for r in reversed(range(last)):
        names += [f"dn{r}", f"ed{r + 1}"] + (["l1"] if r == last - 1 else [])
    return names + ["c2", "c3", "ed0", "c0", "c1"]


def shards(
    queries, key_vectors, values, gate_rates, log_decay, level_weights, block_levels, grad_out
):
    levels = lax.axis_size("ctx").bit_length() - 1
    position = lax.axis_index("ctx")
    tokens, heads, width = key_vectors.shape
    half = heads // 2
    ids = jnp.arange(levels, dtype=jnp.int32)
    sides = jnp.right_shift(position, ids) % 2
    sees = sides * (ids < block_levels[0]).astype(jnp.int32)
    per = 2
    state_per = 4
    aux_rows = (levels + 3 + 7) // 8 * 8
    mat = (width, width)
    splits = [heads >> r > 1 for r in range(levels + 1)]
    held = [max(heads >> r, 1) for r in range(levels + 1)]
    packed = whole((tokens, heads, width))
    rows = whole((heads, tokens))
    flat = pltpu.VMEM((tokens * heads, width), F32)

    def grouped(*shape, size=per):
        return pl.BlockSpec((size,) + shape, lambda p: (p,) + (0,) * len(shape))

    def stated(*shape):
        return grouped(*shape, size=state_per)

    tok = struct(heads, tokens, width, dtype=BF16)
    q, k, v, d, aux, a_full, bt, other, mine = pl.pallas_call(
        state_kernel,
        grid=(heads // state_per,),
        in_specs=[SMEM] + [HBM] * 7,
        out_specs=[
            stated(tokens, width), stated(tokens, width), stated(tokens, width),
            stated(tokens, width), stated(aux_rows, tokens), stated(tokens, tokens),
            stated(width, tokens), whole((2, half) + mat), whole((2, half) + mat),
        ],
        out_shape=[
            tok, tok, tok, tok, struct(heads, aux_rows, tokens), struct(heads, tokens, tokens),
            struct(heads, width, tokens), struct(2, half, *mat), struct(2, half, *mat),
        ],
        scratch_shapes=[flat] * 4
        + [
            pltpu.VMEM((heads, tokens), F32),
            pltpu.VMEM((4, tokens, heads, width), BF16),
            pltpu.VMEM((heads, tokens), F32),
            pltpu.VMEM((heads, tokens), F32),
            pltpu.VMEM(level_weights.shape, F32),
            pltpu.SemaphoreType.DMA((7,)),
        ],
        compiler_params=params(BIG),
        cost_estimate=cost(20),
        name="state",
    )(
        sides,
        *[
            pltpu.with_memory_space_constraint(x, pltpu.HBM)
            for x in (
                queries, key_vectors, values, grad_out, gate_rates, log_decay, level_weights
            )
        ],
    )

    order = Order()
    early_outs, late_outs, cross_outs = [{} for _ in range(3)]

    def early(i):
        start, size = EARLY[i]
        early_outs[i] = order.end(pl.pallas_call(
            interleaved(early_kernel),
            grid=(size // GROUP,),
            in_specs=[
                SMEM, headed(tokens, width, start=start), headed(tokens, width, start=start),
                headed(tokens, width, start=start), headed(aux_rows, tokens, start=start),
                headed(tokens, tokens, start=start),
            ],
            out_specs=[headed(tokens, width), headed(tokens, width), second(levels, *mat)],
            out_shape=[
                struct(size, tokens, width), struct(size, tokens, width),
                struct(levels, size, *mat),
            ],
            compiler_params=params(MID),
            cost_estimate=cost(1.1 * size),
            name="early",
        )(order.start(sees), q, k, d, aux, a_full))

    def late(i):
        start, size = PARTS[i]
        late_outs[i] = order.end(pl.pallas_call(
            interleaved(late_kernel),
            grid=(size // GROUP,),
            in_specs=[SMEM] + [headed(tokens, width, start=start)] * 4
            + [headed(aux_rows, tokens, start=start), headed(tokens, tokens, start=start)],
            out_specs=[
                headed(tokens, width), headed(tokens, width), headed(width, tokens),
                headed(1, tokens),
            ],
            out_shape=[
                struct(size, tokens, width), struct(size, tokens, width),
                struct(size, width, tokens), struct(size, 1, tokens),
            ],
            compiler_params=params(MID),
            cost_estimate=cost(1.2 * size),
            name="late",
        )(order.start(sides), q, k, v, d, aux, a_full))

    def cross(i, x, x_start):
        start, size = PARTS[i]
        name = next(e for e, (s, n) in EARLY.items() if s <= start < s + n)
        skip = start - EARLY[name][0]
        carried, w_keys, _ = early_outs[name]
        local, dq, _, gw = late_outs[i]
        cross_outs[i] = order.end(pl.pallas_call(
            interleaved(cross_kernel),
            grid=(size // GROUP,),
            in_specs=[
                SMEM, headed(tokens, width, start=start), headed(tokens, width, start=start),
                headed(aux_rows, tokens, start=start), second(levels, *mat, start=x_start),
                headed(tokens, width, start=skip), headed(tokens, width, start=skip),
                headed(tokens, width), headed(tokens, width), headed(1, tokens),
            ],
            out_specs=[
                headed(tokens, width), headed(tokens, width), headed(levels + 1, tokens),
            ],
            out_shape=[
                struct(size, tokens, width), struct(size, tokens, width),
                struct(size, levels + 1, tokens),
            ],
            compiler_params=params(MID),
            cost_estimate=cost(1.4 * size),
            name="cross",
        )(order.start(sees), k, d, aux, x, carried, w_keys, local, dq, gw))

    lows, ups, low_states, runs = [], [], [], []

    def short(kernel, name, inputs, outputs):
        return order.end(small(kernel, name, order.start(sides), inputs, outputs))

    def up_round(r, mine, received):
        last = r + 1 == levels - 1
        n, many = held[r + 1], splits[r + 1]
        payload = (1 if last else 2, held[r + 2]) + mat
        low_m, up_m, low_s, *following = short(
            functools.partial(up_kernel, r, last, many), f"up{r}", [mine, received],
            [(n, *mat)] * 3 + [payload] * (2 if many else 1),
        )
        lows.append(low_m)
        ups.append(up_m)
        low_states.append(low_s)
        return following[0], following[-1]

    def adjoint_round(r, parts, received):
        many = splits[r + 1]
        following = (levels - r - 1, held[r + 2]) + mat
        run, *rest = short(
            functools.partial(adjoint_up_kernel, r, [p.shape[1] for p in parts], many),
            f"adjoint_up{r}", [lows[r], received, *parts],
            [(held[r + 1], *mat)] + [following] * (2 if many else 1),
        )
        runs.append(run)
        return rest[0], rest[-1]

    def down_round(r, own, received):
        top = r == levels - 2
        split_in = splits[r + 1]
        many = splits[r]
        inputs = [lows[r], low_states[r], own] + ([received] if split_in or top else [])
        shape = (levels - r, held[r + 1]) + mat
        outs = short(
            functools.partial(down_kernel, r, top, split_in, many), f"down{r}", inputs,
            [shape] * (2 if many else 1),
        )
        return outs[0], outs[-1]

    def adjoint_down_round(r, own, received):
        top = r == levels - 2
        split_in = splits[r + 1]
        many = splits[r]
        inputs = [runs[r], ups[r], own] + ([received] if split_in else [])
        outs = short(
            functools.partial(adjoint_down_kernel, r, top, split_in, many), f"adjoint_down{r}",
            inputs, [(1, held[r + 1], *mat)] * (2 if many else 1),
        )
        return outs[0], outs[-1]

    moves = {}

    def adjoint_send(x, r):
        moves["adjoint", r] = swap(x, r)

    def step(kind, r):
        if kind == "up":
            mine, send = up_round(r, moves["mine", r], moves["pair", r])
            moves["mine", r + 1] = mine
            moves["pair", r + 1] = swap(send, r + 1)
        elif kind == "ad":
            parts = moves["adjoint_mine", r] if r else [early_outs["e_m1"][2], early_outs["e_m2"][2]]
            mine, send = adjoint_round(r, parts, moves["adjoint", r])
            moves["adjoint_mine", r + 1] = [mine]
            adjoint_send(send, r + 1)
        elif kind == "dn":
            top = r == levels - 2
            own = moves["mine", r + 1] if top else moves["own", r + 1]
            received = moves["pair", r + 1] if top else moves.get(("state", r + 1))
            own, send = down_round(r, own, received)
            moves["own", r] = own
            if splits[r]:
                moves["state", r] = swap(send, r)
        else:
            top = r == levels - 2
            own = moves["adjoint", r + 1][:1] if top else moves["grad_own", r + 1]
            own, send = adjoint_down_round(r, own, moves.get(("grad", r + 1)))
            moves["grad_own", r] = own
            if splits[r]:
                moves["grad", r] = swap(send, r)

    def cover(name):
        kind, i = name[0], name[1:]
        if kind == "e":
            early(name)
        elif kind == "l":
            late(int(i))
        else:
            i = int(i)
            start = PARTS[i][0]
            if start < half:
                cross(i, moves["state", 0], start)
            else:
                cross(i, moves["own", 0], start - half)

    moves["mine", 0] = mine
    moves["pair", 0] = swap(other, 0)
    for name in call_order(levels):
        if name[:2] in ("up", "ad", "dn", "ed"):
            step(name[:2], int(name[2:]))
            if name == RELEASE:
                adjoint_send(order.start(early_outs["e_o"][2]), 0)
        else:
            cover(name)
    grad_own, grad_received = moves["grad_own", 0], moves["grad", 0]

    def part_spec(i, *shape):
        first, size = (n // per for n in PARTS[i])
        return pl.BlockSpec(
            (per,) + shape, lambda p: (jnp.clip(p - first, 0, size - 1),) + (0,) * len(shape)
        )

    indices = range(len(PARTS))
    layer_out, grad_queries, grad_values, grad_level_weights = pl.pallas_call(
        functools.partial(value_kernel, [n for _, n in PARTS], per),
        grid=(heads // per,),
        in_specs=[
            SMEM, grouped(width, tokens),
            pl.BlockSpec((1, per) + mat, lambda p: (0, jnp.minimum(p, half // per - 1), 0, 0)),
            pl.BlockSpec((1, per) + mat, lambda p: (0, jnp.maximum(p - half // per, 0), 0, 0)),
        ]
        + [part_spec(i, tokens, width) for i in indices]
        + [part_spec(i, tokens, width) for i in indices]
        + [part_spec(i, levels + 1, tokens) for i in indices]
        + [part_spec(i, width, tokens) for i in indices],
        out_specs=[
            packed, whole((tokens * heads, width)), whole((tokens * heads, width)),
            whole((levels + 1, heads, tokens)),
        ],
        out_shape=[
            struct(tokens, heads, width, dtype=BF16), struct(tokens * heads, width),
            struct(tokens * heads, width), struct(levels + 1, heads, tokens),
        ],
        scratch_shapes=[flat],
        compiler_params=params(BIG),
        cost_estimate=cost(5),
        name="value",
    )(
        order.start(sides), bt, grad_received, grad_own,
        *[cross_outs[i][0] for i in indices], *[cross_outs[i][1] for i in indices],
        *[cross_outs[i][2] for i in indices], *[late_outs[i][2] for i in indices],
    )
    shape = (tokens, heads, width)
    return (
        layer_out, grad_queries.reshape(shape), grad_values.reshape(shape), grad_level_weights
    )


def solution(mesh):
    tokens = P(("groups", "ctx"), None, None)
    rows = P(None, ("groups", "ctx"))
    weights = P(None, None, ("groups", "ctx"))
    return jax.shard_map(
        shards,
        mesh=mesh,
        in_specs=(tokens, tokens, tokens, rows, rows, weights, P(("groups", "ctx")), tokens),
        out_specs=(tokens, tokens, tokens, weights),
        check_vma=False,
    )
```

```python
import functools

import jax
import jax.numpy as jnp
from jax import lax
from jax.experimental import pallas as pl
from jax.experimental.pallas import tpu as pltpu
from jax.sharding import PartitionSpec as P

F32 = jnp.float32
BF16 = jnp.bfloat16
TILE = 128
SUB = 16
NN = (((1,), (0,)), ((), ()))
NT = (((1,), (1,)), ((), ()))


def split(x):
    high = x.astype(BF16)
    return high, (x - high.astype(F32)).astype(BF16)


def dot(a, b, dims=NN):
    return lax.dot_general(a, b, dims, preferred_element_type=F32)


def dot_left(a, b, dims=NN):
    return dot(beside(split(a), 1), beside((b, b), dims[0][1][0]), dims)


def beside(parts, axis):
    return jnp.concatenate(parts, axis=axis)


def fold(x):
    half = x.shape[1] // 2
    return x[:, :half] + x[:, half:]


def dot_right_parts(a, b, dims=NN):
    depth = dims[0][1][0]
    if a.shape[1] <= TILE:
        return dot(beside((a, a), 1), beside(b, depth), dims)
    if b[0].shape[1 - depth] <= TILE:
        return fold(dot(a, beside(b, 1 - depth), dims))
    return dot(a, b[0], dims) + dot(a, b[1], dims)


def dot_right(a, b, dims=NN):
    return dot_right_parts(a, split(b), dims)


def dot_parts(a, b, dims=NN):
    depth = dims[0][1][0]
    left = beside(a, 1)
    if b[0].shape[1 - depth] <= TILE:
        both = beside(b, 1 - depth)
        return fold(dot(left, beside((both, both), depth), dims))
    return dot(left, beside((b[0], b[0]), depth), dims) + dot(a[0], b[1], dims)


def dot3(a, b, dims=NN):
    return dot_parts(split(a), split(b), dims)


def batch_parts(pairs, dims=NN):
    return [dot_parts(a, b, dims) for a, b in pairs]


def column(row):
    return [
        jnp.transpose(jnp.broadcast_to(row[:, s : s + TILE], (TILE, TILE)))
        for s in range(0, row.shape[1], TILE)
    ]


def wide(tile, width):
    return jnp.concatenate([tile] * (width // TILE), axis=1) if width > TILE else tile


def rows_of(i):
    return slice(i * TILE, (i + 1) * TILE)


def key_norms(keys):
    k32 = keys.astype(F32)
    scale = 1.0 / jnp.sqrt(jnp.sum(k32 * k32, axis=1, keepdims=True) + 1e-06)
    cols = [
        jnp.broadcast_to(scale[rows_of(i)], (TILE, TILE)) for i in range(keys.shape[0] // TILE)
    ]
    row = jnp.concatenate([jnp.transpose(c)[0:1] for c in cols], axis=1)
    return cols, row


def causal(i, strict):
    width = (i + 1) * TILE
    r = lax.broadcasted_iota(jnp.int32, (TILE, width), 0) + i * TILE
    c = lax.broadcasted_iota(jnp.int32, (TILE, width), 1)
    return r > c if strict else r >= c


def decay_ratio(c_cols, c_row, i):
    width = (i + 1) * TILE
    keep = causal(i, False)
    spread = wide(c_cols[i], width) - c_row[:, :width]
    return jnp.where(keep, jnp.exp(jnp.where(keep, spread, 0.0)), 0.0)


def small_inverses(blocks):
    lane = lax.broadcasted_iota(jnp.int32, (8, TILE), 1)
    sub_row = lax.broadcasted_iota(jnp.int32, (8, TILE), 0)
    owner = lane // SUB
    within = lane - owner * SUB
    first = owner * SUB
    tiles = SUB // 8
    coefs, sols = [], []
    for block in blocks:
        packed, unit = [], []
        for q in range(tiles):
            piece = jnp.zeros((8, TILE), F32)
            for b in range(TILE // SUB):
                start = b * SUB + q * 8
                piece = jnp.where(owner == b, block[start : start + 8], piece)
            packed.append(piece)
            unit.append(jnp.where(within == sub_row + q * 8, 1.0, 0.0).astype(F32))
        coefs.append(packed)
        sols.append(unit)
    for j in range(SUB - 1):
        index = first + j
        for coef, sol in zip(coefs, sols):
            row = jnp.broadcast_to(sol[j // 8][j % 8 : j % 8 + 1], (8, TILE))
            for q in range((j + 1) // 8, tiles):
                factor = jnp.take_along_axis(coef[q], index, axis=1, mode="promise_in_bounds")
                sol[q] = sol[q] - factor * row
    out = []
    for sol in sols:
        pieces = []
        for b in range(TILE // SUB):
            for q in range(tiles):
                pieces.append(jnp.where(owner == b, sol[q], 0.0))
        out.append(jnp.concatenate(pieces, axis=0))
    return out


def tile_inverses(blocks):
    r = lax.broadcasted_iota(jnp.int32, (TILE, TILE), 0)
    c = lax.broadcasted_iota(jnp.int32, (TILE, TILE), 1)
    inverses = small_inverses(blocks)
    size = SUB
    while size < TILE:
        below_half = (r // size == c // size + 1) & (r // (2 * size) == c // (2 * size))
        parts = [split(x) for x in inverses]
        inner = batch_parts(
            [(split(jnp.where(below_half, t, 0.0)), x) for t, x in zip(blocks, parts)]
        )
        outer = batch_parts([(x, split(y)) for x, y in zip(parts, inner)])
        inverses = [x - y for x, y in zip(inverses, outer)]
        size *= 2
    return inverses


def piled(parts):
    return jnp.concatenate(parts, axis=0) if len(parts) > 1 else parts[0]


def below(rows, j):
    return piled([rows[i][:, rows_of(j)] for i in range(j, len(rows))])


def head_at(position, side, heads):
    return (position + (1 - side) * (heads // 2)) % heads


def state_kernel(
    sides_ref, q_in, k_in, v_in, d_in, beta_ref, decay_ref, w_ref,
    q_ref, k_ref, v_ref, d_ref, aux_ref, a_ref, bt_ref, other_ref, mine_ref,
    q_all, k_all, v_all, d_all, c_all, packed_all, beta_all, decay_all, w_all, sems,
):
    tokens, heads, width = k_in.shape
    per = k_ref.shape[0]
    half = heads // 2
    step = pl.program_id(0)
    count = tokens // TILE

    @pl.when(step == 0)
    def _():
        sources = (decay_ref, beta_ref, w_ref, k_in, v_in, q_in, d_in)
        targets = (decay_all, beta_all, w_all, *(packed_all.at[i] for i in range(4)))
        copies = [
            pltpu.make_async_copy(source, target, sems.at[i])
            for i, (source, target) in enumerate(zip(sources, targets))
        ]
        for copy in copies:
            copy.start()
        for copy in copies:
            copy.wait()
        for i, target in enumerate((k_all, v_all, q_all, d_all)):
            target[...] = packed_all[i].astype(F32).reshape(tokens * heads, width)
        r = lax.broadcasted_iota(jnp.int32, (tokens, tokens), 0)
        c = lax.broadcasted_iota(jnp.int32, (tokens, tokens), 1)
        upper = jnp.where(r <= c, 1.0, 0.0).astype(BF16)
        decay = decay_all[...]
        high, rest = split(decay)
        low = (decay - high.astype(F32) - rest.astype(F32)).astype(BF16)
        c_all[...] = dot(high, upper) + (dot(rest, upper) + dot(low, upper))

    r = lax.broadcasted_iota(jnp.int32, (width, width), 0)
    c = lax.broadcasted_iota(jnp.int32, (width, width), 1)
    identity = jnp.where(r == c, 1.0, 0.0).astype(F32)
    k32s, keyss, norms, betas, c_rows, lowers, tiles = [], [], [], [], [], [], []
    for s in range(per):
        head = head_at(step * per + s, sides_ref[0], heads)
        mine = pl.ds(head, tokens, stride=heads)
        k32 = k_all[mine, :]
        keys = k32.astype(BF16)
        q_ref[s] = q_all[mine, :].astype(BF16)
        k_ref[s] = keys
        v_ref[s] = v_all[mine, :].astype(BF16)
        d_ref[s] = d_all[mine, :].astype(BF16)
        beta_row = beta_all[pl.ds(head, 1), :]
        c_row = c_all[pl.ds(head, 1), :]
        norm_cols, norm_row = key_norms(keys)
        aux = [c_row, norm_row] + [w_all[l, pl.ds(head, 1), :] for l in range(w_all.shape[0])]
        aux_ref[s, : len(aux)] = jnp.concatenate(aux, axis=0)
        beta_cols = column(beta_row)
        lower = []
        for i in range(count):
            n = (i + 1) * TILE
            gram = dot(keys[rows_of(i)], keys[:n], NT)
            scaled = wide(beta_cols[i] * norm_cols[i], n) * gram * norm_row[:, :n]
            lower.append(jnp.where(causal(i, True), scaled, 0.0))
        k32s.append(k32)
        keyss.append(keys)
        norms.append((norm_cols, norm_row))
        betas.append(beta_row)
        c_rows.append(c_row)
        lowers.append(lower)
        tiles += [lower[i][:, rows_of(i)] for i in range(count)]
    inverses = tile_inverses(tiles)
    diagonal = [split(x) for x in inverses]
    lower_parts = [[split(row) for row in lower] for lower in lowers]
    group = range(per)
    solved = [{(i, i): diagonal[s * count + i] for i in range(count)} for s in group]
    exact = [{(i, i): inverses[s * count + i] for i in range(count)} for s in group]
    for off in range(1, count):
        pairs = []
        for s in group:
            for i in range(off, count):
                j = i - off
                left = tuple(x[:, j * TILE : i * TILE] for x in lower_parts[s][i])
                right = tuple(piled([solved[s][k, j][z] for k in range(j, i)]) for z in range(2))
                pairs.append((left, right))
        inner = batch_parts(pairs)
        places = [(s, i) for s in group for i in range(off, count)]
        outer = batch_parts(
            [(diagonal[s * count + i], split(y)) for (s, i), y in zip(places, inner)]
        )
        for (s, i), y in zip(places, outer):
            exact[s][i, i - off] = -y
            solved[s][i, i - off] = split(-y)
    scaled_rows = []
    for s in group:
        norm_cols, beta_row = norms[s][0], betas[s]
        scaled = []
        for i in range(count):
            n = (i + 1) * TILE
            row = [exact[s][i, j] for j in range(i + 1)]
            a_row = (jnp.concatenate(row, axis=1) if i else row[0]) * beta_row[:, :n]
            a_ref[s, rows_of(i), :n] = a_row
            scaled.append(wide(norm_cols[i], n) * a_row)
        scaled_rows.append(scaled)
    keys_t = [jnp.transpose(k32).astype(BF16) for k32 in k32s]
    bts = [
        jnp.concatenate(
            [
                dot_right(keys_t[s][:, j * TILE :], below(scaled_rows[s], j))
                for j in range(count)
            ],
            axis=1,
        )
        for s in group
    ]
    totals = [c_rows[s][:, tokens - 1 :] for s in group]
    fadeds = [bts[s] * jnp.exp(totals[s] - c_rows[s]) for s in group]
    overlaps = [dot_left(bts[s] * norms[s][1], keyss[s]) for s in group]
    states = [dot_left(fadeds[s], v_ref[s]) for s in group]
    for s in group:
        bt_ref[s] = fadeds[s]
        moved = jnp.exp(totals[s]) * (identity - overlaps[s])
        position = step * per + s

        @pl.when(position < half)
        def _():
            other_ref[0, position] = moved
            other_ref[1, position] = states[s]

        @pl.when(position >= half)
        def _():
            mine_ref[0, position - half] = moved
            mine_ref[1, position - half] = states[s]


GROUP = 2


def pick_head(ref, s):
    return ref.at[s] if len(ref.shape) == 3 else ref.at[:, s]


def interleaved(head_body):
    def kernel(scalars_ref, *refs):
        running = [
            head_body(scalars_ref, *[pick_head(ref, s) for ref in refs]) for s in range(GROUP)
        ]
        while running:
            running = [body for body in running if next(body, None) is not None]

    return kernel


def early_kernel(sees_ref, q_ref, k_ref, d_ref, aux_ref, a_ref, carried_ref, w_keys_ref, adj_ref):
    tokens, width = q_ref.shape
    count = tokens // TILE
    levels = adj_ref.shape[0]
    queries, keys = q_ref[...], k_ref[...]
    c_row, norm_row = aux_ref[0:1, :], aux_ref[1:2, :]
    gains = [jnp.exp(t) for t in column(c_row)]
    delta_t = jnp.transpose(d_ref[...].astype(F32)).astype(BF16)
    weight_cols = [column(aux_ref[3 + l : 4 + l, :]) for l in range(levels)]
    span = range(count)
    sizes = [(i + 1) * TILE for i in span]
    wy_keys = [
        dot_left(a_ref[rows_of(i), : sizes[i]] * norm_row[:, : sizes[i]], keys[: sizes[i]])
        for i in span
    ]
    scores = [dot(queries[rows_of(i)], keys[: sizes[i]], NT) for i in span]
    yield 1
    query_key = [jnp.where(causal(i, False), scores[i] * norm_row[:, : sizes[i]], 0.0) for i in span]
    keys_w = piled(wy_keys)
    w_keys_ref[...] = keys_w
    keys_h, keys_l = split(keys_w)
    inner = [
        dot_parts(split(query_key[i]), (keys_h[: sizes[i]], keys_l[: sizes[i]])) for i in span
    ]
    yield 1
    carried = [gains[i] * (queries[rows_of(i)].astype(F32) - inner[i]) for i in span]
    for i in span:
        carried_ref[rows_of(i), :] = carried[i]
    for l in range(levels):
        scaled = piled([weight_cols[l][i] * carried[i] for i in range(count)])
        adj_ref[l] = jnp.where(sees_ref[l] == 1, dot_right(delta_t, scaled), 0.0)


def late_kernel(sides_ref, q_ref, k_ref, v_ref, d_ref, aux_ref, a_ref, local_ref, dq_ref, dvt_ref, gw_ref):
    tokens, width = q_ref.shape
    count = tokens // TILE
    queries, keys, values, delta = q_ref[...], k_ref[...], v_ref[...], d_ref[...]
    d32 = delta.astype(F32)
    c_row, norm_row = aux_ref[0:1, :], aux_ref[1:2, :]
    c_cols = column(c_row)
    w_cols = column(aux_ref[2:3, :])
    wy_values, ratios, faded_a = [], [], []
    for i in range(count):
        n = (i + 1) * TILE
        ratios.append(decay_ratio(c_cols, c_row, i))
        faded_a.append(ratios[i] * a_ref[rows_of(i), :n])
        wy_values.append(dot_left(faded_a[i], values[:n]))
    yield 1
    values_h, values_l = split(piled(wy_values))
    span = range(count)
    sizes = [(i + 1) * TILE for i in span]
    scores = [dot(queries[rows_of(i)], keys[: sizes[i]], NT) for i in span]
    outers = [
        dot_right_parts(delta[rows_of(i)], (values_h[: sizes[i]], values_l[: sizes[i]]), NT)
        for i in span
    ]
    yield 1
    scales = [ratios[i] * norm_row[:, : sizes[i]] for i in span]
    pqs = [scales[i] * scores[i] for i in span]
    weights = [wide(w_cols[i], sizes[i]) for i in span]
    weighted_pq = [weights[i] * pqs[i] for i in span]
    locals_ = [
        dot_parts(split(pqs[i]), (values_h[: sizes[i]], values_l[: sizes[i]])) for i in span
    ]
    yield 1
    for i in span:
        dq_ref[rows_of(i), :] = dot_left(scales[i] * weights[i] * outers[i], keys[: sizes[i]])
        local_ref[rows_of(i), :] = w_cols[i] * locals_[i]
    dots = [d32[rows_of(i)] * locals_[i] for i in span]
    ones = jnp.ones((8, width), BF16)
    gw_ref[...] = dot_right(ones, piled(dots), NT)[0:1]
    delta_t = jnp.transpose(d32).astype(BF16)
    adjoint_u = jnp.concatenate(
        [dot_right(delta_t[:, j * TILE :], below(weighted_pq, j)) for j in range(count)], axis=1
    )
    yield 1
    u_h, u_l = split(adjoint_u)
    for j in range(count):
        part = (u_h[:, j * TILE :], u_l[:, j * TILE :])
        dvt_ref[:, rows_of(j)] = dot_parts(part, split(below(faded_a, j)))


def cross_kernel(
    sees_ref, k_ref, d_ref, aux_ref, x_ref, carried_ref, w_keys_ref, local_ref, dq_in_ref, gw_in_ref,
    out_ref, dq_ref, gw_ref,
):
    tokens, width = k_ref.shape
    count = tokens // TILE
    levels = x_ref.shape[0]
    keys, delta = k_ref[...], d_ref[...]
    norm_row = aux_ref[1:2, :]
    gains = [jnp.exp(t) for t in column(aux_ref[0:1, :])]
    weight_cols = [column(aux_ref[3 + l : 4 + l, :]) for l in range(levels)]
    states = piled([jnp.where(sees_ref[l] == 1, x_ref[l], 0.0) for l in range(levels)])
    states_h, states_l = split(states)
    keys_h, keys_l = split(w_keys_ref[...])
    ones = jnp.ones((8, width), BF16)
    span = range(count)
    pulled = [
        dot_right_parts(delta[rows_of(i)], (states_h, states_l), NT) for i in span
    ]
    yield 1
    carried = [carried_ref[rows_of(i), :] for i in span]
    lefts = [
        split(jnp.concatenate([weight_cols[l][i] * carried[i] for l in range(levels)], axis=1))
        for i in span
    ]
    crosses = [dot_parts(lefts[i], (states_h, states_l)) for i in span]
    yield 1
    scaled = []
    for i in span:
        terms = [weight_cols[l][i] * pulled[i][:, rows_of(l)] for l in range(levels)]
        scaled.append(gains[i] * functools.reduce(jnp.add, terms))
    scores = [
        dot_parts(split(scaled[i]), (keys_h[: (i + 1) * TILE], keys_l[: (i + 1) * TILE]), NT)
        for i in span
    ]
    weight_rows = [
        [dot_right(ones, carried[i] * pulled[i][:, rows_of(l)], NT)[0:1] for i in span]
        for l in range(levels)
    ]
    yield 1
    for i in span:
        n = (i + 1) * TILE
        kept = jnp.where(causal(i, False), scores[i], 0.0) * norm_row[:, :n]
        dq_ref[rows_of(i), :] = dq_in_ref[rows_of(i), :] + scaled[i] - dot_left(kept, keys[:n])
        out_ref[rows_of(i), :] = local_ref[rows_of(i), :] + crosses[i]
    rows = [gw_in_ref[...]] + [jnp.concatenate(weight_rows[l], axis=1) for l in range(levels)]
    gw_ref[...] = jnp.concatenate(rows, axis=0)


def value_kernel(sizes, per, sides_ref, bt_ref, recv_ref, own_ref, *refs):
    steps = pl.num_programs(0)
    step = pl.program_id(0)
    heads = steps * per
    tokens = bt_ref.shape[2]
    groups = []
    for _ in range(4):
        groups.append(refs[: len(sizes)])
        refs = refs[len(sizes) :]
    outs, dqs, gws, dvts = groups
    out_ref, dq_ref, dv_ref, gw_ref, out_all = refs
    grads = [jnp.where(step < steps // 2, recv_ref[0, s], own_ref[0, s]) for s in range(per)]
    moved = [dot3(grads[s], bt_ref[s]) for s in range(per)]
    places = []
    for s in range(per):
        head = head_at(step * per + s, sides_ref[0], heads)
        places.append((head, pl.ds(head, tokens, stride=heads)))
    start = 0
    for p, size in enumerate(sizes):

        @pl.when((step >= start // per) & (step < (start + size) // per))
        def _(p=p):
            for s, (head, place) in enumerate(places):
                out_all[place, :] = outs[p][s]
                dq_ref[place, :] = dqs[p][s]
                dv_ref[place, :] = jnp.transpose(dvts[p][s] + moved[s])
                for l in range(gw_ref.shape[0]):
                    gw_ref[l, pl.ds(head, 1), :] = gws[p][s, l : l + 1, :]

        start += size

    @pl.when(step == steps - 1)
    def _():
        out_ref[...] = out_all[...].reshape(out_ref.shape).astype(BF16)


def pick(flag, a, b):
    return jnp.where(flag, a, b)


def stored(side, h, count, mine_ref, other_ref, write):
    if other_ref is None:
        write(mine_ref, h)
        return
    half = count // 2

    @pl.when(side == h // half)
    def _():
        write(mine_ref, h % half)

    @pl.when(side != h // half)
    def _():
        write(other_ref, h % half)


def read_half(side, h, own_ref, recv_ref, level):
    if recv_ref is None:
        return own_ref[level, h]
    half = own_ref.shape[1]
    return pick(side == h // half, own_ref[level, h % half], recv_ref[level, h % half])


def up_kernel(r, last, splits, sides_ref, mine_ref, recv_ref, low_m, up_m, low_s, *nexts):
    count = mine_ref.shape[1]
    up = sides_ref[r] == 1
    next_mine, next_other = nexts if splits else (nexts[0], None)
    pairs, s_ups = [], []
    for h in range(count):
        m_low = pick(up, recv_ref[0, h], mine_ref[0, h])
        m_up = pick(up, mine_ref[0, h], recv_ref[0, h])
        s_low = pick(up, recv_ref[1, h], mine_ref[1, h])
        s_ups.append(pick(up, mine_ref[1, h], recv_ref[1, h]))
        low_m[h] = m_low
        up_m[h] = m_up
        low_s[h] = s_low
        parts = split(m_up)
        pairs.append((parts, split(s_low)))
        if not last:
            pairs.append((parts, split(m_low)))
    products = batch_parts(pairs)
    for h in range(count):
        value = products[h : h + 1] if last else products[2 * h : 2 * h + 2]

        def write(ref, place):
            ref[-1 % ref.shape[0], place] = value[0] + s_ups[h]
            if not last:
                ref[0, place] = value[1]

        stored(sides_ref[min(r + 1, sides_ref.shape[0] - 1)], h, count, next_mine, next_other, write)


def down_kernel(r, top, split_in, splits, sides_ref, low_m, low_s, *refs):
    own_ref, *refs = refs
    recv_ref = None
    if split_in or top:
        recv_ref, *refs = refs
    out_own, out_send = refs if splits else (refs[0], None)
    count = low_m.shape[0]
    levels = own_ref.shape[0]
    up = sides_ref[r] == 1
    values, pairs = [], []
    for h in range(count):
        m_parts = split(low_m[h])
        for l in range(levels):
            if top:
                x = pick(sides_ref[r + 1] == 1, recv_ref[0, h], own_ref[0, h])
            else:
                x = read_half(sides_ref[r + 1], h, own_ref, recv_ref, l)
            values.append(x)
            pairs.append((m_parts, split(x)))
    products = batch_parts(pairs)
    for h in range(count):
        out_own[0, h] = low_s[h]
        if out_send is not None:
            out_send[0, h] = low_s[h]
        for l in range(levels):
            x, moved = values[h * levels + l], products[h * levels + l]
            out_own[l + 1, h] = pick(up, moved, x)
            if out_send is not None:
                out_send[l + 1, h] = pick(up, x, moved)


def adjoint_up_kernel(r, sizes, splits, sides_ref, low_m, recv_ref, *refs):
    parts, refs = refs[: len(sizes)], refs[len(sizes) :]
    run_ref, next_mine, *rest = refs
    next_other = rest[0] if splits else None
    count, levels = low_m.shape[0], recv_ref.shape[0]
    up = sides_ref[r] == 1
    pairs, bases = [], []
    for h in range(count):
        p, place = 0, h
        while place >= sizes[p]:
            place -= sizes[p]
            p += 1
        mine_ref = parts[p]
        run_ref[h] = pick(up, mine_ref[0, place], recv_ref[0, h])
        m_parts = split(low_m[h])
        highs = []
        for l in range(1, levels):
            mine, received = mine_ref[l, place], recv_ref[l, h]
            highs.append(pick(up, mine, received))
            bases.append(pick(up, received, mine))
        pairs.append((split(piled(highs)), m_parts))
    products = batch_parts(pairs)
    for h in range(count):
        for l in range(1, levels):
            value = bases[h * (levels - 1) + l - 1] + products[h][rows_of(l - 1)]

            def write(ref, at):
                ref[l - 1, at] = value

            stored(sides_ref[min(r + 1, sides_ref.shape[0] - 1)], h, count, next_mine, next_other, write)


def adjoint_down_kernel(r, top, split_in, splits, sides_ref, run_ref, up_m, *refs):
    own_ref, *refs = refs
    recv_ref = None
    if split_in:
        recv_ref, *refs = refs
    out_own, out_send = refs if splits else (refs[0], None)
    up = sides_ref[r] == 1
    span = range(run_ref.shape[0])
    grads = [read_half(sides_ref[r + 1], h, own_ref, recv_ref, 0) for h in span]
    if top:
        grads = [pick(sides_ref[r + 1] == 1, 0.0, g) for g in grads]
    products = batch_parts([(split(grads[h]), split(up_m[h])) for h in span])
    for h in span:
        low = run_ref[h] + products[h]
        out_own[0, h] = pick(up, grads[h], low)
        if out_send is not None:
            out_send[0, h] = pick(up, low, grads[h])


def whole(shape):
    return pl.BlockSpec(shape, lambda p: (0,) * len(shape))


def headed(*shape, start=0):
    return pl.BlockSpec(
        (GROUP,) + shape, lambda p: (p + start // GROUP,) + (0,) * len(shape)
    )


def second(first, *shape, start=0):
    return pl.BlockSpec(
        (first, GROUP) + shape, lambda p: (0, p + start // GROUP) + (0,) * len(shape)
    )


def struct(*shape, dtype=F32):
    return jax.ShapeDtypeStruct(shape, dtype)


SMEM = pl.BlockSpec(memory_space=pltpu.SMEM)
VMEM = pl.BlockSpec(memory_space=pltpu.VMEM)
HBM = pl.BlockSpec(memory_space=pltpu.HBM)


BIG, MID, LOW = 36, 20, 12


def params(mib):
    return pltpu.CompilerParams(
        dimension_semantics=("arbitrary",), vmem_limit_bytes=mib * 1024 * 1024
    )


def cost(micros, size=1 << 20):
    return pl.CostEstimate(flops=int(micros * 1.1e9), bytes_accessed=size, transcendentals=0)


def small(kernel, name, sides, inputs, outputs):
    return pl.pallas_call(
        kernel,
        in_specs=[SMEM] + [VMEM] * len(inputs),
        out_specs=[VMEM] * len(outputs),
        out_shape=[struct(*o) for o in outputs],
        cost_estimate=cost(1.0),
        compiler_params=pltpu.CompilerParams(vmem_limit_bytes=LOW * 1024 * 1024),
        name=name,
    )(sides, *inputs)


def swap(x, round_bit):
    size = lax.axis_size("ctx")
    return lax.ppermute(x, "ctx", [(i, i ^ 1 << round_bit) for i in range(size)])


class Order:
    def __init__(self):
        self.last = None

    def start(self, scalars):
        if self.last is None:
            return scalars
        return lax.optimization_barrier((scalars, self.last))[0]

    def end(self, outputs):
        self.last = outputs[-1]
        return outputs


EARLY = {"e_o": (0, 4), "e_m1": (4, 2), "e_m2": (6, 2)}
PARTS = ((0, 2), (2, 2), (4, 2), (6, 2))
FOUR_LEVELS = "e_m2 up0 e_o e_m1 up1 ad0 l2 up2 l0 dn2 ad1 l3 dn1 ad2 l1 ed2 dn0 c2 c0 ed1 c3 ed0 c1"


RELEASE = "up1"


def call_order(levels):
    if levels == 4:
        return FOUR_LEVELS.split()
    last = levels - 2
    names = ["e_o", "up0", "e_m1"]
    for r in range(1, last + 1):
        names += [f"up{r}"] + (["e_m2"] if r == 1 else []) + [f"ad{r - 1}"]
    names += ["l2", f"dn{last}", "l3", f"ad{last}", "l0"]
    for r in reversed(range(last)):
        names += [f"dn{r}", f"ed{r + 1}"] + (["l1"] if r == last - 1 else [])
    return names + ["c2", "c3", "ed0", "c0", "c1"]


def shards(
    queries, key_vectors, values, gate_rates, log_decay, level_weights, block_levels, grad_out
):
    levels = lax.axis_size("ctx").bit_length() - 1
    position = lax.axis_index("ctx")
    tokens, heads, width = key_vectors.shape
    half = heads // 2
    ids = jnp.arange(levels, dtype=jnp.int32)
    sides = jnp.right_shift(position, ids) % 2
    sees = sides * (ids < block_levels[0]).astype(jnp.int32)
    per = 2
    state_per = 4
    aux_rows = (levels + 3 + 7) // 8 * 8
    mat = (width, width)
    splits = [heads >> r > 1 for r in range(levels + 1)]
    held = [max(heads >> r, 1) for r in range(levels + 1)]
    packed = whole((tokens, heads, width))
    rows = whole((heads, tokens))
    flat = pltpu.VMEM((tokens * heads, width), F32)

    def grouped(*shape, size=per):
        return pl.BlockSpec((size,) + shape, lambda p: (p,) + (0,) * len(shape))

    def stated(*shape):
        return grouped(*shape, size=state_per)

    tok = struct(heads, tokens, width, dtype=BF16)
    q, k, v, d, aux, a_full, bt, other, mine = pl.pallas_call(
        state_kernel,
        grid=(heads // state_per,),
        in_specs=[SMEM] + [HBM] * 7,
        out_specs=[
            stated(tokens, width), stated(tokens, width), stated(tokens, width),
            stated(tokens, width), stated(aux_rows, tokens), stated(tokens, tokens),
            stated(width, tokens), whole((2, half) + mat), whole((2, half) + mat),
        ],
        out_shape=[
            tok, tok, tok, tok, struct(heads, aux_rows, tokens), struct(heads, tokens, tokens),
            struct(heads, width, tokens), struct(2, half, *mat), struct(2, half, *mat),
        ],
        scratch_shapes=[flat] * 4
        + [
            pltpu.VMEM((heads, tokens), F32),
            pltpu.VMEM((4, tokens, heads, width), BF16),
            pltpu.VMEM((heads, tokens), F32),
            pltpu.VMEM((heads, tokens), F32),
            pltpu.VMEM(level_weights.shape, F32),
            pltpu.SemaphoreType.DMA((7,)),
        ],
        compiler_params=params(BIG),
        cost_estimate=cost(20),
        name="state",
    )(
        sides,
        *[
            pltpu.with_memory_space_constraint(x, pltpu.HBM)
            for x in (
                queries, key_vectors, values, grad_out, gate_rates, log_decay, level_weights
            )
        ],
    )

    order = Order()
    early_outs, late_outs, cross_outs = [{} for _ in range(3)]

    def early(i):
        start, size = EARLY[i]
        early_outs[i] = order.end(pl.pallas_call(
            interleaved(early_kernel),
            grid=(size // GROUP,),
            in_specs=[
                SMEM, headed(tokens, width, start=start), headed(tokens, width, start=start),
                headed(tokens, width, start=start), headed(aux_rows, tokens, start=start),
                headed(tokens, tokens, start=start),
            ],
            out_specs=[headed(tokens, width), headed(tokens, width), second(levels, *mat)],
            out_shape=[
                struct(size, tokens, width), struct(size, tokens, width),
                struct(levels, size, *mat),
            ],
            compiler_params=params(MID),
            cost_estimate=cost(1.1 * size),
            name="early",
        )(order.start(sees), q, k, d, aux, a_full))

    def late(i):
        start, size = PARTS[i]
        late_outs[i] = order.end(pl.pallas_call(
            interleaved(late_kernel),
            grid=(size // GROUP,),
            in_specs=[SMEM] + [headed(tokens, width, start=start)] * 4
            + [headed(aux_rows, tokens, start=start), headed(tokens, tokens, start=start)],
            out_specs=[
                headed(tokens, width), headed(tokens, width), headed(width, tokens),
                headed(1, tokens),
            ],
            out_shape=[
                struct(size, tokens, width), struct(size, tokens, width),
                struct(size, width, tokens), struct(size, 1, tokens),
            ],
            compiler_params=params(MID),
            cost_estimate=cost(1.2 * size),
            name="late",
        )(order.start(sides), q, k, v, d, aux, a_full))

    def cross(i, x, x_start):
        start, size = PARTS[i]
        name = next(e for e, (s, n) in EARLY.items() if s <= start < s + n)
        skip = start - EARLY[name][0]
        carried, w_keys, _ = early_outs[name]
        local, dq, _, gw = late_outs[i]
        cross_outs[i] = order.end(pl.pallas_call(
            interleaved(cross_kernel),
            grid=(size // GROUP,),
            in_specs=[
                SMEM, headed(tokens, width, start=start), headed(tokens, width, start=start),
                headed(aux_rows, tokens, start=start), second(levels, *mat, start=x_start),
                headed(tokens, width, start=skip), headed(tokens, width, start=skip),
                headed(tokens, width), headed(tokens, width), headed(1, tokens),
            ],
            out_specs=[
                headed(tokens, width), headed(tokens, width), headed(levels + 1, tokens),
            ],
            out_shape=[
                struct(size, tokens, width), struct(size, tokens, width),
                struct(size, levels + 1, tokens),
            ],
            compiler_params=params(MID),
            cost_estimate=cost(1.4 * size),
            name="cross",
        )(order.start(sees), k, d, aux, x, carried, w_keys, local, dq, gw))

    lows, ups, low_states, runs = [], [], [], []

    def short(kernel, name, inputs, outputs):
        return order.end(small(kernel, name, order.start(sides), inputs, outputs))

    def up_round(r, mine, received):
        last = r + 1 == levels - 1
        n, many = held[r + 1], splits[r + 1]
        payload = (1 if last else 2, held[r + 2]) + mat
        low_m, up_m, low_s, *following = short(
            functools.partial(up_kernel, r, last, many), f"up{r}", [mine, received],
            [(n, *mat)] * 3 + [payload] * (2 if many else 1),
        )
        lows.append(low_m)
        ups.append(up_m)
        low_states.append(low_s)
        return following[0], following[-1]

    def adjoint_round(r, parts, received):
        many = splits[r + 1]
        following = (levels - r - 1, held[r + 2]) + mat
        run, *rest = short(
            functools.partial(adjoint_up_kernel, r, [p.shape[1] for p in parts], many),
            f"adjoint_up{r}", [lows[r], received, *parts],
            [(held[r + 1], *mat)] + [following] * (2 if many else 1),
        )
        runs.append(run)
        return rest[0], rest[-1]

    def down_round(r, own, received):
        top = r == levels - 2
        split_in = splits[r + 1]
        many = splits[r]
        inputs = [lows[r], low_states[r], own] + ([received] if split_in or top else [])
        shape = (levels - r, held[r + 1]) + mat
        outs = short(
            functools.partial(down_kernel, r, top, split_in, many), f"down{r}", inputs,
            [shape] * (2 if many else 1),
        )
        return outs[0], outs[-1]

    def adjoint_down_round(r, own, received):
        top = r == levels - 2
        split_in = splits[r + 1]
        many = splits[r]
        inputs = [runs[r], ups[r], own] + ([received] if split_in else [])
        outs = short(
            functools.partial(adjoint_down_kernel, r, top, split_in, many), f"adjoint_down{r}",
            inputs, [(1, held[r + 1], *mat)] * (2 if many else 1),
        )
        return outs[0], outs[-1]

    moves = {}

    def adjoint_send(x, r):
        moves["adjoint", r] = swap(x, r)

    def step(kind, r):
        if kind == "up":
            mine, send = up_round(r, moves["mine", r], moves["pair", r])
            moves["mine", r + 1] = mine
            moves["pair", r + 1] = swap(send, r + 1)
        elif kind == "ad":
            parts = moves["adjoint_mine", r] if r else [early_outs["e_m1"][2], early_outs["e_m2"][2]]
            mine, send = adjoint_round(r, parts, moves["adjoint", r])
            moves["adjoint_mine", r + 1] = [mine]
            adjoint_send(send, r + 1)
        elif kind == "dn":
            top = r == levels - 2
            own = moves["mine", r + 1] if top else moves["own", r + 1]
            received = moves["pair", r + 1] if top else moves.get(("state", r + 1))
            own, send = down_round(r, own, received)
            moves["own", r] = own
            if splits[r]:
                moves["state", r] = swap(send, r)
        else:
            top = r == levels - 2
            own = moves["adjoint", r + 1][:1] if top else moves["grad_own", r + 1]
            own, send = adjoint_down_round(r, own, moves.get(("grad", r + 1)))
            moves["grad_own", r] = own
            if splits[r]:
                moves["grad", r] = swap(send, r)

    def cover(name):
        kind, i = name[0], name[1:]
        if kind == "e":
            early(name)
        elif kind == "l":
            late(int(i))
        else:
            i = int(i)
            start = PARTS[i][0]
            if start < half:
                cross(i, moves["state", 0], start)
            else:
                cross(i, moves["own", 0], start - half)

    moves["mine", 0] = mine
    moves["pair", 0] = swap(other, 0)
    for name in call_order(levels):
        if name[:2] in ("up", "ad", "dn", "ed"):
            step(name[:2], int(name[2:]))
            if name == RELEASE:
                adjoint_send(order.start(early_outs["e_o"][2]), 0)
        else:
            cover(name)
    grad_own, grad_received = moves["grad_own", 0], moves["grad", 0]

    def part_spec(i, *shape):
        first, size = (n // per for n in PARTS[i])
        return pl.BlockSpec(
            (per,) + shape, lambda p: (jnp.clip(p - first, 0, size - 1),) + (0,) * len(shape)
        )

    indices = range(len(PARTS))
    layer_out, grad_queries, grad_values, grad_level_weights = pl.pallas_call(
        functools.partial(value_kernel, [n for _, n in PARTS], per),
        grid=(heads // per,),
        in_specs=[
            SMEM, grouped(width, tokens),
            pl.BlockSpec((1, per) + mat, lambda p: (0, jnp.minimum(p, half // per - 1), 0, 0)),
            pl.BlockSpec((1, per) + mat, lambda p: (0, jnp.maximum(p - half // per, 0), 0, 0)),
        ]
        + [part_spec(i, tokens, width) for i in indices]
        + [part_spec(i, tokens, width) for i in indices]
        + [part_spec(i, levels + 1, tokens) for i in indices]
        + [part_spec(i, width, tokens) for i in indices],
        out_specs=[
            packed, whole((tokens * heads, width)), whole((tokens * heads, width)),
            whole((levels + 1, heads, tokens)),
        ],
        out_shape=[
            struct(tokens, heads, width, dtype=BF16), struct(tokens * heads, width),
            struct(tokens * heads, width), struct(levels + 1, heads, tokens),
        ],
        scratch_shapes=[flat],
        compiler_params=params(BIG),
        cost_estimate=cost(5),
        name="value",
    )(
        order.start(sides), bt, grad_received, grad_own,
        *[cross_outs[i][0] for i in indices], *[cross_outs[i][1] for i in indices],
        *[cross_outs[i][2] for i in indices], *[late_outs[i][2] for i in indices],
    )
    shape = (tokens, heads, width)
    return (
        layer_out, grad_queries.reshape(shape), grad_values.reshape(shape), grad_level_weights
    )


def solution(mesh):
    tokens = P(("groups", "ctx"), None, None)
    rows = P(None, ("groups", "ctx"))
    weights = P(None, None, ("groups", "ctx"))
    return jax.shard_map(
        shards,
        mesh=mesh,
        in_specs=(tokens, tokens, tokens, rows, rows, weights, P(("groups", "ctx")), tokens),
        out_specs=(tokens, tokens, tokens, weights),
        check_vma=False,
    )
```

```python
import functools

import jax
import jax.numpy as jnp
from jax import lax
from jax.experimental import pallas as pl
from jax.experimental.pallas import tpu as pltpu
from jax.sharding import PartitionSpec as P

F32 = jnp.float32
BF16 = jnp.bfloat16
TILE = 128
SUB = 16
NN = (((1,), (0,)), ((), ()))
NT = (((1,), (1,)), ((), ()))


def split(x):
    high = x.astype(BF16)
    return high, (x - high.astype(F32)).astype(BF16)


def dot(a, b, dims=NN):
    return lax.dot_general(a, b, dims, preferred_element_type=F32)


def dot_left(a, b, dims=NN):
    return dot(beside(split(a), 1), beside((b, b), dims[0][1][0]), dims)


def beside(parts, axis):
    return jnp.concatenate(parts, axis=axis)


def fold(x):
    half = x.shape[1] // 2
    return x[:, :half] + x[:, half:]


def dot_right_parts(a, b, dims=NN):
    depth = dims[0][1][0]
    if a.shape[1] <= TILE:
        return dot(beside((a, a), 1), beside(b, depth), dims)
    if b[0].shape[1 - depth] <= TILE:
        return fold(dot(a, beside(b, 1 - depth), dims))
    return dot(a, b[0], dims) + dot(a, b[1], dims)


def dot_right(a, b, dims=NN):
    return dot_right_parts(a, split(b), dims)


def dot_parts(a, b, dims=NN):
    depth = dims[0][1][0]
    left = beside(a, 1)
    if b[0].shape[1 - depth] <= TILE:
        both = beside(b, 1 - depth)
        return fold(dot(left, beside((both, both), depth), dims))
    return dot(left, beside((b[0], b[0]), depth), dims) + dot(a[0], b[1], dims)


def dot_apart(a, b):
    return fold(dot(a[0], beside(b, 1))) + dot(a[1], b[0])


def dot3(a, b, dims=NN):
    return dot_parts(split(a), split(b), dims)


def batch_parts(pairs, dims=NN):
    return [dot_parts(a, b, dims) for a, b in pairs]


def column(row):
    return [
        jnp.transpose(jnp.broadcast_to(row[:, s : s + TILE], (TILE, TILE)))
        for s in range(0, row.shape[1], TILE)
    ]


def wide(tile, width):
    return jnp.concatenate([tile] * (width // TILE), axis=1) if width > TILE else tile


def rows_of(i):
    return slice(i * TILE, (i + 1) * TILE)


def key_norms(keys):
    k32 = keys.astype(F32)
    scale = 1.0 / jnp.sqrt(jnp.sum(k32 * k32, axis=1, keepdims=True) + 1e-06)
    cols = [
        jnp.broadcast_to(scale[rows_of(i)], (TILE, TILE)) for i in range(keys.shape[0] // TILE)
    ]
    row = jnp.concatenate([jnp.transpose(c)[0:1] for c in cols], axis=1)
    return cols, row


def causal(i, strict):
    width = (i + 1) * TILE
    r = lax.broadcasted_iota(jnp.int32, (TILE, width), 0) + i * TILE
    c = lax.broadcasted_iota(jnp.int32, (TILE, width), 1)
    return r > c if strict else r >= c


def decay_ratio(c_cols, c_row, i):
    width = (i + 1) * TILE
    keep = causal(i, False)
    spread = wide(c_cols[i], width) - c_row[:, :width]
    return jnp.where(keep, jnp.exp(jnp.where(keep, spread, 0.0)), 0.0)


def small_inverses(blocks):
    lane = lax.broadcasted_iota(jnp.int32, (8, TILE), 1)
    sub_row = lax.broadcasted_iota(jnp.int32, (8, TILE), 0)
    owner = lane // SUB
    within = lane - owner * SUB
    first = owner * SUB
    tiles = SUB // 8
    coefs, sols = [], []
    for block in blocks:
        packed, unit = [], []
        for q in range(tiles):
            piece = jnp.zeros((8, TILE), F32)
            for b in range(TILE // SUB):
                start = b * SUB + q * 8
                piece = jnp.where(owner == b, block[start : start + 8], piece)
            packed.append(piece)
            unit.append(jnp.where(within == sub_row + q * 8, 1.0, 0.0).astype(F32))
        coefs.append(packed)
        sols.append(unit)
    for j in range(SUB - 1):
        index = first + j
        for coef, sol in zip(coefs, sols):
            row = jnp.broadcast_to(sol[j // 8][j % 8 : j % 8 + 1], (8, TILE))
            for q in range((j + 1) // 8, tiles):
                factor = jnp.take_along_axis(coef[q], index, axis=1, mode="promise_in_bounds")
                sol[q] = sol[q] - factor * row
    out = []
    for sol in sols:
        pieces = []
        for b in range(TILE // SUB):
            for q in range(tiles):
                pieces.append(jnp.where(owner == b, sol[q], 0.0))
        out.append(jnp.concatenate(pieces, axis=0))
    return out


def tile_inverses(blocks):
    r = lax.broadcasted_iota(jnp.int32, (TILE, TILE), 0)
    c = lax.broadcasted_iota(jnp.int32, (TILE, TILE), 1)
    inverses = small_inverses(blocks)
    size = SUB
    while size < TILE:
        below_half = (r // size == c // size + 1) & (r // (2 * size) == c // (2 * size))
        parts = [split(x) for x in inverses]
        inner = batch_parts(
            [(split(jnp.where(below_half, t, 0.0)), x) for t, x in zip(blocks, parts)]
        )
        outer = batch_parts([(x, split(y)) for x, y in zip(parts, inner)])
        inverses = [x - y for x, y in zip(inverses, outer)]
        size *= 2
    return inverses


def piled(parts):
    return jnp.concatenate(parts, axis=0) if len(parts) > 1 else parts[0]


def below(rows, j):
    return piled([rows[i][:, rows_of(j)] for i in range(j, len(rows))])


def head_at(position, side, heads):
    return (position + (1 - side) * (heads // 2)) % heads


def state_kernel(
    sides_ref, q_in, k_in, v_in, d_in, beta_ref, decay_ref, w_ref,
    q_ref, k_ref, v_ref, d_ref, aux_ref, a_ref, bt_ref, other_ref, mine_ref,
    q_all, k_all, v_all, d_all, c_all, packed_all, beta_all, decay_all, w_all, sems,
):
    tokens, heads, width = k_in.shape
    per = k_ref.shape[0]
    half = heads // 2
    step = pl.program_id(0)
    count = tokens // TILE

    @pl.when(step == 0)
    def _():
        sources = (decay_ref, beta_ref, w_ref, k_in, v_in, q_in, d_in)
        targets = (decay_all, beta_all, w_all, *(packed_all.at[i] for i in range(4)))
        copies = [
            pltpu.make_async_copy(source, target, sems.at[i])
            for i, (source, target) in enumerate(zip(sources, targets))
        ]
        for copy in copies:
            copy.start()
        for copy in copies:
            copy.wait()
        for i, target in enumerate((k_all, v_all, q_all, d_all)):
            target[...] = packed_all[i].astype(F32).reshape(tokens * heads, width)
        r = lax.broadcasted_iota(jnp.int32, (tokens, tokens), 0)
        c = lax.broadcasted_iota(jnp.int32, (tokens, tokens), 1)
        upper = jnp.where(r <= c, 1.0, 0.0).astype(BF16)
        decay = decay_all[...]
        high, rest = split(decay)
        low = (decay - high.astype(F32) - rest.astype(F32)).astype(BF16)
        c_all[...] = dot(high, upper) + (dot(rest, upper) + dot(low, upper))

    r = lax.broadcasted_iota(jnp.int32, (width, width), 0)
    c = lax.broadcasted_iota(jnp.int32, (width, width), 1)
    identity = jnp.where(r == c, 1.0, 0.0).astype(F32)
    k32s, keyss, norms, betas, c_rows, lowers, tiles = [], [], [], [], [], [], []
    for s in range(per):
        head = head_at(step * per + s, sides_ref[0], heads)
        mine = pl.ds(head, tokens, stride=heads)
        k32 = k_all[mine, :]
        keys = k32.astype(BF16)
        q_ref[s] = q_all[mine, :].astype(BF16)
        k_ref[s] = keys
        v_ref[s] = v_all[mine, :].astype(BF16)
        d_ref[s] = d_all[mine, :].astype(BF16)
        beta_row = beta_all[pl.ds(head, 1), :]
        c_row = c_all[pl.ds(head, 1), :]
        norm_cols, norm_row = key_norms(keys)
        aux = [c_row, norm_row] + [w_all[l, pl.ds(head, 1), :] for l in range(w_all.shape[0])]
        aux_ref[s, : len(aux)] = jnp.concatenate(aux, axis=0)
        beta_cols = column(beta_row)
        lower = []
        for i in range(count):
            n = (i + 1) * TILE
            gram = dot(keys[rows_of(i)], keys[:n], NT)
            scaled = wide(beta_cols[i] * norm_cols[i], n) * gram * norm_row[:, :n]
            lower.append(jnp.where(causal(i, True), scaled, 0.0))
        k32s.append(k32)
        keyss.append(keys)
        norms.append((norm_cols, norm_row))
        betas.append(beta_row)
        c_rows.append(c_row)
        lowers.append(lower)
        tiles += [lower[i][:, rows_of(i)] for i in range(count)]
    inverses = tile_inverses(tiles)
    diagonal = [split(x) for x in inverses]
    lower_parts = [[split(row) for row in lower] for lower in lowers]
    group = range(per)
    solved = [{(i, i): diagonal[s * count + i] for i in range(count)} for s in group]
    exact = [{(i, i): inverses[s * count + i] for i in range(count)} for s in group]
    for off in range(1, count):
        pairs = []
        for s in group:
            for i in range(off, count):
                j = i - off
                left = tuple(x[:, j * TILE : i * TILE] for x in lower_parts[s][i])
                right = tuple(piled([solved[s][k, j][z] for k in range(j, i)]) for z in range(2))
                pairs.append((left, right))
        inner = batch_parts(pairs)
        places = [(s, i) for s in group for i in range(off, count)]
        outer = batch_parts(
            [(diagonal[s * count + i], split(y)) for (s, i), y in zip(places, inner)]
        )
        for (s, i), y in zip(places, outer):
            exact[s][i, i - off] = -y
            solved[s][i, i - off] = split(-y)
    scaled_rows = []
    for s in group:
        norm_cols, beta_row = norms[s][0], betas[s]
        scaled = []
        for i in range(count):
            n = (i + 1) * TILE
            row = [exact[s][i, j] for j in range(i + 1)]
            a_row = (jnp.concatenate(row, axis=1) if i else row[0]) * beta_row[:, :n]
            a_ref[s, rows_of(i), :n] = a_row
            scaled.append(wide(norm_cols[i], n) * a_row)
        scaled_rows.append(scaled)
    keys_t = [jnp.transpose(k32).astype(BF16) for k32 in k32s]
    bts = [
        jnp.concatenate(
            [
                dot_right(keys_t[s][:, j * TILE :], below(scaled_rows[s], j))
                for j in range(count)
            ],
            axis=1,
        )
        for s in group
    ]
    totals = [c_rows[s][:, tokens - 1 :] for s in group]
    fadeds = [bts[s] * jnp.exp(totals[s] - c_rows[s]) for s in group]
    overlaps = [dot_left(bts[s] * norms[s][1], keyss[s]) for s in group]
    states = [dot_left(fadeds[s], v_ref[s]) for s in group]
    for s in group:
        bt_ref[s] = fadeds[s]
        moved = jnp.exp(totals[s]) * (identity - overlaps[s])
        position = step * per + s

        @pl.when(position < half)
        def _():
            other_ref[0, position] = moved
            other_ref[1, position] = states[s]

        @pl.when(position >= half)
        def _():
            mine_ref[0, position - half] = moved
            mine_ref[1, position - half] = states[s]


GROUP = 2


def pick_head(ref, s):
    return ref.at[s] if len(ref.shape) == 3 else ref.at[:, s]


def interleaved(head_body):
    def kernel(scalars_ref, *refs):
        running = [
            head_body(scalars_ref, *[pick_head(ref, s) for ref in refs]) for s in range(GROUP)
        ]
        while running:
            running = [body for body in running if next(body, None) is not None]

    return kernel


def early_kernel(sees_ref, q_ref, k_ref, d_ref, aux_ref, a_ref, carried_ref, w_keys_ref, adj_ref):
    tokens, width = q_ref.shape
    count = tokens // TILE
    levels = adj_ref.shape[0]
    queries, keys = q_ref[...], k_ref[...]
    c_row, norm_row = aux_ref[0:1, :], aux_ref[1:2, :]
    gains = [jnp.exp(t) for t in column(c_row)]
    delta_t = jnp.transpose(d_ref[...].astype(F32)).astype(BF16)
    weight_cols = [column(aux_ref[3 + l : 4 + l, :]) for l in range(levels)]
    span = range(count)
    sizes = [(i + 1) * TILE for i in span]
    wy_keys = [
        dot_left(a_ref[rows_of(i), : sizes[i]] * norm_row[:, : sizes[i]], keys[: sizes[i]])
        for i in span
    ]
    scores = [dot(queries[rows_of(i)], keys[: sizes[i]], NT) for i in span]
    yield 1
    query_key = [jnp.where(causal(i, False), scores[i] * norm_row[:, : sizes[i]], 0.0) for i in span]
    keys_w = piled(wy_keys)
    w_keys_ref[...] = keys_w
    keys_h, keys_l = split(keys_w)
    inner = [
        dot_parts(split(query_key[i]), (keys_h[: sizes[i]], keys_l[: sizes[i]])) for i in span
    ]
    yield 1
    carried = [gains[i] * (queries[rows_of(i)].astype(F32) - inner[i]) for i in span]
    for i in span:
        carried_ref[rows_of(i), :] = carried[i]
    for l in range(levels):
        scaled = piled([weight_cols[l][i] * carried[i] for i in range(count)])
        adj_ref[l] = jnp.where(sees_ref[l] == 1, dot_right(delta_t, scaled), 0.0)


def late_kernel(sides_ref, q_ref, k_ref, v_ref, d_ref, aux_ref, a_ref, local_ref, dq_ref, dvt_ref, gw_ref):
    tokens, width = q_ref.shape
    count = tokens // TILE
    queries, keys, values, delta = q_ref[...], k_ref[...], v_ref[...], d_ref[...]
    d32 = delta.astype(F32)
    c_row, norm_row = aux_ref[0:1, :], aux_ref[1:2, :]
    c_cols = column(c_row)
    w_cols = column(aux_ref[2:3, :])
    wy_values, ratios, faded_a = [], [], []
    for i in range(count):
        n = (i + 1) * TILE
        ratios.append(decay_ratio(c_cols, c_row, i))
        faded_a.append(ratios[i] * a_ref[rows_of(i), :n])
        wy_values.append(dot_left(faded_a[i], values[:n]))
    yield 1
    values_h, values_l = split(piled(wy_values))
    span = range(count)
    sizes = [(i + 1) * TILE for i in span]
    scores = [dot(queries[rows_of(i)], keys[: sizes[i]], NT) for i in span]
    outers = [
        dot_right_parts(delta[rows_of(i)], (values_h[: sizes[i]], values_l[: sizes[i]]), NT)
        for i in span
    ]
    yield 1
    scales = [ratios[i] * norm_row[:, : sizes[i]] for i in span]
    pqs = [scales[i] * scores[i] for i in span]
    weights = [wide(w_cols[i], sizes[i]) for i in span]
    weighted_pq = [weights[i] * pqs[i] for i in span]
    locals_ = [
        dot_parts(split(pqs[i]), (values_h[: sizes[i]], values_l[: sizes[i]])) for i in span
    ]
    yield 1
    for i in span:
        dq_ref[rows_of(i), :] = dot_left(scales[i] * weights[i] * outers[i], keys[: sizes[i]])
        local_ref[rows_of(i), :] = w_cols[i] * locals_[i]
    dots = [d32[rows_of(i)] * locals_[i] for i in span]
    ones = jnp.ones((8, width), BF16)
    gw_ref[...] = dot_right(ones, piled(dots), NT)[0:1]
    delta_t = jnp.transpose(d32).astype(BF16)
    adjoint_u = jnp.concatenate(
        [dot_right(delta_t[:, j * TILE :], below(weighted_pq, j)) for j in range(count)], axis=1
    )
    yield 1
    u_h, u_l = split(adjoint_u)
    for j in range(count):
        part = (u_h[:, j * TILE :], u_l[:, j * TILE :])
        dvt_ref[:, rows_of(j)] = dot_parts(part, split(below(faded_a, j)))


def cross_kernel(
    sees_ref, k_ref, d_ref, aux_ref, x_ref, carried_ref, w_keys_ref, local_ref, dq_in_ref, gw_in_ref,
    out_ref, dq_ref, gw_ref,
):
    tokens, width = k_ref.shape
    count = tokens // TILE
    levels = x_ref.shape[0]
    keys, delta = k_ref[...], d_ref[...]
    norm_row = aux_ref[1:2, :]
    gains = [jnp.exp(t) for t in column(aux_ref[0:1, :])]
    weight_cols = [column(aux_ref[3 + l : 4 + l, :]) for l in range(levels)]
    states = piled([jnp.where(sees_ref[l] == 1, x_ref[l], 0.0) for l in range(levels)])
    states_h, states_l = split(states)
    keys_h, keys_l = split(w_keys_ref[...])
    ones = jnp.ones((8, width), BF16)
    span = range(count)
    pulled = [
        dot(delta[rows_of(i)], states_h, NT) + dot(delta[rows_of(i)], states_l, NT) for i in span
    ]
    yield 1
    carried = [carried_ref[rows_of(i), :] for i in span]
    lefts = [
        split(jnp.concatenate([weight_cols[l][i] * carried[i] for l in range(levels)], axis=1))
        for i in span
    ]
    crosses = [dot_apart(lefts[i], (states_h, states_l)) for i in span]
    yield 1
    scaled = []
    for i in span:
        terms = [weight_cols[l][i] * pulled[i][:, rows_of(l)] for l in range(levels)]
        scaled.append(gains[i] * functools.reduce(jnp.add, terms))
    scores = [
        dot_parts(split(scaled[i]), (keys_h[: (i + 1) * TILE], keys_l[: (i + 1) * TILE]), NT)
        for i in span
    ]
    weight_rows = [
        [dot_right(ones, carried[i] * pulled[i][:, rows_of(l)], NT)[0:1] for i in span]
        for l in range(levels)
    ]
    yield 1
    for i in span:
        n = (i + 1) * TILE
        kept = jnp.where(causal(i, False), scores[i], 0.0) * norm_row[:, :n]
        dq_ref[rows_of(i), :] = dq_in_ref[rows_of(i), :] + scaled[i] - dot_left(kept, keys[:n])
        out_ref[rows_of(i), :] = local_ref[rows_of(i), :] + crosses[i]
    rows = [gw_in_ref[...]] + [jnp.concatenate(weight_rows[l], axis=1) for l in range(levels)]
    gw_ref[...] = jnp.concatenate(rows, axis=0)


def value_kernel(sizes, per, sides_ref, bt_ref, recv_ref, own_ref, *refs):
    steps = pl.num_programs(0)
    step = pl.program_id(0)
    heads = steps * per
    tokens = bt_ref.shape[2]
    groups = []
    for _ in range(4):
        groups.append(refs[: len(sizes)])
        refs = refs[len(sizes) :]
    outs, dqs, gws, dvts = groups
    out_ref, dq_ref, dv_ref, gw_ref, out_all = refs
    grads = [jnp.where(step < steps // 2, recv_ref[0, s], own_ref[0, s]) for s in range(per)]
    moved = [dot3(grads[s], bt_ref[s]) for s in range(per)]
    places = []
    for s in range(per):
        head = head_at(step * per + s, sides_ref[0], heads)
        places.append((head, pl.ds(head, tokens, stride=heads)))
    start = 0
    for p, size in enumerate(sizes):

        @pl.when((step >= start // per) & (step < (start + size) // per))
        def _(p=p):
            for s, (head, place) in enumerate(places):
                out_all[place, :] = outs[p][s]
                dq_ref[place, :] = dqs[p][s]
                dv_ref[place, :] = jnp.transpose(dvts[p][s] + moved[s])
                for l in range(gw_ref.shape[0]):
                    gw_ref[l, pl.ds(head, 1), :] = gws[p][s, l : l + 1, :]

        start += size

    @pl.when(step == steps - 1)
    def _():
        out_ref[...] = out_all[...].reshape(out_ref.shape).astype(BF16)


def pick(flag, a, b):
    return jnp.where(flag, a, b)


def stored(side, h, count, mine_ref, other_ref, write):
    if other_ref is None:
        write(mine_ref, h)
        return
    half = count // 2

    @pl.when(side == h // half)
    def _():
        write(mine_ref, h % half)

    @pl.when(side != h // half)
    def _():
        write(other_ref, h % half)


def read_half(side, h, own_ref, recv_ref, level):
    if recv_ref is None:
        return own_ref[level, h]
    half = own_ref.shape[1]
    return pick(side == h // half, own_ref[level, h % half], recv_ref[level, h % half])


def up_kernel(r, last, splits, sides_ref, mine_ref, recv_ref, low_m, up_m, low_s, *nexts):
    count = mine_ref.shape[1]
    up = sides_ref[r] == 1
    next_mine, next_other = nexts if splits else (nexts[0], None)
    pairs, s_ups = [], []
    for h in range(count):
        m_low = pick(up, recv_ref[0, h], mine_ref[0, h])
        m_up = pick(up, mine_ref[0, h], recv_ref[0, h])
        s_low = pick(up, recv_ref[1, h], mine_ref[1, h])
        s_ups.append(pick(up, mine_ref[1, h], recv_ref[1, h]))
        low_m[h] = m_low
        up_m[h] = m_up
        low_s[h] = s_low
        parts = split(m_up)
        pairs.append((parts, split(s_low)))
        if not last:
            pairs.append((parts, split(m_low)))
    products = batch_parts(pairs)
    for h in range(count):
        value = products[h : h + 1] if last else products[2 * h : 2 * h + 2]

        def write(ref, place):
            ref[-1 % ref.shape[0], place] = value[0] + s_ups[h]
            if not last:
                ref[0, place] = value[1]

        stored(sides_ref[min(r + 1, sides_ref.shape[0] - 1)], h, count, next_mine, next_other, write)


def down_kernel(r, top, split_in, splits, sides_ref, low_m, low_s, *refs):
    own_ref, *refs = refs
    recv_ref = None
    if split_in or top:
        recv_ref, *refs = refs
    out_own, out_send = refs if splits else (refs[0], None)
    count = low_m.shape[0]
    levels = own_ref.shape[0]
    up = sides_ref[r] == 1
    values, pairs = [], []
    for h in range(count):
        m_parts = split(low_m[h])
        for l in range(levels):
            if top:
                x = pick(sides_ref[r + 1] == 1, recv_ref[0, h], own_ref[0, h])
            else:
                x = read_half(sides_ref[r + 1], h, own_ref, recv_ref, l)
            values.append(x)
            pairs.append((m_parts, split(x)))
    products = batch_parts(pairs)
    for h in range(count):
        out_own[0, h] = low_s[h]
        if out_send is not None:
            out_send[0, h] = low_s[h]
        for l in range(levels):
            x, moved = values[h * levels + l], products[h * levels + l]
            out_own[l + 1, h] = pick(up, moved, x)
            if out_send is not None:
                out_send[l + 1, h] = pick(up, x, moved)


def adjoint_up_kernel(r, sizes, splits, sides_ref, low_m, recv_ref, *refs):
    parts, refs = refs[: len(sizes)], refs[len(sizes) :]
    run_ref, next_mine, *rest = refs
    next_other = rest[0] if splits else None
    count, levels = low_m.shape[0], recv_ref.shape[0]
    up = sides_ref[r] == 1
    pairs, bases = [], []
    for h in range(count):
        p, place = 0, h
        while place >= sizes[p]:
            place -= sizes[p]
            p += 1
        mine_ref = parts[p]
        run_ref[h] = pick(up, mine_ref[0, place], recv_ref[0, h])
        m_parts = split(low_m[h])
        highs = []
        for l in range(1, levels):
            mine, received = mine_ref[l, place], recv_ref[l, h]
            highs.append(pick(up, mine, received))
            bases.append(pick(up, received, mine))
        pairs.append((split(piled(highs)), m_parts))
    products = batch_parts(pairs)
    for h in range(count):
        for l in range(1, levels):
            value = bases[h * (levels - 1) + l - 1] + products[h][rows_of(l - 1)]

            def write(ref, at):
                ref[l - 1, at] = value

            stored(sides_ref[min(r + 1, sides_ref.shape[0] - 1)], h, count, next_mine, next_other, write)


def adjoint_down_kernel(r, top, split_in, splits, sides_ref, run_ref, up_m, *refs):
    own_ref, *refs = refs
    recv_ref = None
    if split_in:
        recv_ref, *refs = refs
    out_own, out_send = refs if splits else (refs[0], None)
    up = sides_ref[r] == 1
    span = range(run_ref.shape[0])
    grads = [read_half(sides_ref[r + 1], h, own_ref, recv_ref, 0) for h in span]
    if top:
        grads = [pick(sides_ref[r + 1] == 1, 0.0, g) for g in grads]
    products = batch_parts([(split(grads[h]), split(up_m[h])) for h in span])
    for h in span:
        low = run_ref[h] + products[h]
        out_own[0, h] = pick(up, grads[h], low)
        if out_send is not None:
            out_send[0, h] = pick(up, low, grads[h])


def whole(shape):
    return pl.BlockSpec(shape, lambda p: (0,) * len(shape))


def headed(*shape, start=0):
    return pl.BlockSpec(
        (GROUP,) + shape, lambda p: (p + start // GROUP,) + (0,) * len(shape)
    )


def second(first, *shape, start=0):
    return pl.BlockSpec(
        (first, GROUP) + shape, lambda p: (0, p + start // GROUP) + (0,) * len(shape)
    )


def struct(*shape, dtype=F32):
    return jax.ShapeDtypeStruct(shape, dtype)


SMEM = pl.BlockSpec(memory_space=pltpu.SMEM)
VMEM = pl.BlockSpec(memory_space=pltpu.VMEM)
HBM = pl.BlockSpec(memory_space=pltpu.HBM)


BIG, MID, LOW = 36, 20, 12


def params(mib):
    return pltpu.CompilerParams(
        dimension_semantics=("arbitrary",), vmem_limit_bytes=mib * 1024 * 1024
    )


def cost(micros, size=1 << 20):
    return pl.CostEstimate(flops=int(micros * 1.1e9), bytes_accessed=size, transcendentals=0)


def small(kernel, name, sides, inputs, outputs):
    return pl.pallas_call(
        kernel,
        in_specs=[SMEM] + [VMEM] * len(inputs),
        out_specs=[VMEM] * len(outputs),
        out_shape=[struct(*o) for o in outputs],
        cost_estimate=cost(1.0),
        compiler_params=pltpu.CompilerParams(vmem_limit_bytes=LOW * 1024 * 1024),
        name=name,
    )(sides, *inputs)


def swap(x, round_bit):
    size = lax.axis_size("ctx")
    return lax.ppermute(x, "ctx", [(i, i ^ 1 << round_bit) for i in range(size)])


class Order:
    def __init__(self):
        self.last = None

    def start(self, scalars):
        if self.last is None:
            return scalars
        return lax.optimization_barrier((scalars, self.last))[0]

    def end(self, outputs):
        self.last = outputs[-1]
        return outputs


EARLY = {"e_o": (0, 4), "e_m1": (4, 2), "e_m2": (6, 2)}
PARTS = ((0, 2), (2, 2), (4, 2), (6, 2))
FOUR_LEVELS = "e_m2 up0 e_o e_m1 up1 ad0 l2 up2 l0 dn2 ad1 l3 dn1 ad2 l1 ed2 dn0 c2 c0 ed1 c3 ed0 c1"


RELEASE = "up1"


def call_order(levels):
    if levels == 4:
        return FOUR_LEVELS.split()
    last = levels - 2
    names = ["e_o", "up0", "e_m1"]
    for r in range(1, last + 1):
        names += [f"up{r}"] + (["e_m2"] if r == 1 else []) + [f"ad{r - 1}"]
    names += ["l2", f"dn{last}", "l3", f"ad{last}", "l0"]
    for r in reversed(range(last)):
        names += [f"dn{r}", f"ed{r + 1}"] + (["l1"] if r == last - 1 else [])
    return names + ["c2", "c3", "ed0", "c0", "c1"]


def shards(
    queries, key_vectors, values, gate_rates, log_decay, level_weights, block_levels, grad_out
):
    levels = lax.axis_size("ctx").bit_length() - 1
    position = lax.axis_index("ctx")
    tokens, heads, width = key_vectors.shape
    half = heads // 2
    ids = jnp.arange(levels, dtype=jnp.int32)
    sides = jnp.right_shift(position, ids) % 2
    sees = sides * (ids < block_levels[0]).astype(jnp.int32)
    per = 2
    state_per = 4
    aux_rows = (levels + 3 + 7) // 8 * 8
    mat = (width, width)
    splits = [heads >> r > 1 for r in range(levels + 1)]
    held = [max(heads >> r, 1) for r in range(levels + 1)]
    packed = whole((tokens, heads, width))
    rows = whole((heads, tokens))
    flat = pltpu.VMEM((tokens * heads, width), F32)

    def grouped(*shape, size=per):
        return pl.BlockSpec((size,) + shape, lambda p: (p,) + (0,) * len(shape))

    def stated(*shape):
        return grouped(*shape, size=state_per)

    tok = struct(heads, tokens, width, dtype=BF16)
    q, k, v, d, aux, a_full, bt, other, mine = pl.pallas_call(
        state_kernel,
        grid=(heads // state_per,),
        in_specs=[SMEM] + [HBM] * 7,
        out_specs=[
            stated(tokens, width), stated(tokens, width), stated(tokens, width),
            stated(tokens, width), stated(aux_rows, tokens), stated(tokens, tokens),
            stated(width, tokens), whole((2, half) + mat), whole((2, half) + mat),
        ],
        out_shape=[
            tok, tok, tok, tok, struct(heads, aux_rows, tokens), struct(heads, tokens, tokens),
            struct(heads, width, tokens), struct(2, half, *mat), struct(2, half, *mat),
        ],
        scratch_shapes=[flat] * 4
        + [
            pltpu.VMEM((heads, tokens), F32),
            pltpu.VMEM((4, tokens, heads, width), BF16),
            pltpu.VMEM((heads, tokens), F32),
            pltpu.VMEM((heads, tokens), F32),
            pltpu.VMEM(level_weights.shape, F32),
            pltpu.SemaphoreType.DMA((7,)),
        ],
        compiler_params=params(BIG),
        cost_estimate=cost(20),
        name="state",
    )(
        sides,
        *[
            pltpu.with_memory_space_constraint(x, pltpu.HBM)
            for x in (
                queries, key_vectors, values, grad_out, gate_rates, log_decay, level_weights
            )
        ],
    )

    order = Order()
    early_outs, late_outs, cross_outs = [{} for _ in range(3)]

    def early(i):
        start, size = EARLY[i]
        early_outs[i] = order.end(pl.pallas_call(
            interleaved(early_kernel),
            grid=(size // GROUP,),
            in_specs=[
                SMEM, headed(tokens, width, start=start), headed(tokens, width, start=start),
                headed(tokens, width, start=start), headed(aux_rows, tokens, start=start),
                headed(tokens, tokens, start=start),
            ],
            out_specs=[headed(tokens, width), headed(tokens, width), second(levels, *mat)],
            out_shape=[
                struct(size, tokens, width), struct(size, tokens, width),
                struct(levels, size, *mat),
            ],
            compiler_params=params(MID),
            cost_estimate=cost(1.1 * size),
            name="early",
        )(order.start(sees), q, k, d, aux, a_full))

    def late(i):
        start, size = PARTS[i]
        late_outs[i] = order.end(pl.pallas_call(
            interleaved(late_kernel),
            grid=(size // GROUP,),
            in_specs=[SMEM] + [headed(tokens, width, start=start)] * 4
            + [headed(aux_rows, tokens, start=start), headed(tokens, tokens, start=start)],
            out_specs=[
                headed(tokens, width), headed(tokens, width), headed(width, tokens),
                headed(1, tokens),
            ],
            out_shape=[
                struct(size, tokens, width), struct(size, tokens, width),
                struct(size, width, tokens), struct(size, 1, tokens),
            ],
            compiler_params=params(MID),
            cost_estimate=cost(1.2 * size),
            name="late",
        )(order.start(sides), q, k, v, d, aux, a_full))

    def cross(i, x, x_start):
        start, size = PARTS[i]
        name = next(e for e, (s, n) in EARLY.items() if s <= start < s + n)
        skip = start - EARLY[name][0]
        carried, w_keys, _ = early_outs[name]
        local, dq, _, gw = late_outs[i]
        cross_outs[i] = order.end(pl.pallas_call(
            interleaved(cross_kernel),
            grid=(size // GROUP,),
            in_specs=[
                SMEM, headed(tokens, width, start=start), headed(tokens, width, start=start),
                headed(aux_rows, tokens, start=start), second(levels, *mat, start=x_start),
                headed(tokens, width, start=skip), headed(tokens, width, start=skip),
                headed(tokens, width), headed(tokens, width), headed(1, tokens),
            ],
            out_specs=[
                headed(tokens, width), headed(tokens, width), headed(levels + 1, tokens),
            ],
            out_shape=[
                struct(size, tokens, width), struct(size, tokens, width),
                struct(size, levels + 1, tokens),
            ],
            compiler_params=params(MID),
            cost_estimate=cost(1.4 * size),
            name="cross",
        )(order.start(sees), k, d, aux, x, carried, w_keys, local, dq, gw))

    lows, ups, low_states, runs = [], [], [], []

    def short(kernel, name, inputs, outputs):
        return order.end(small(kernel, name, order.start(sides), inputs, outputs))

    def up_round(r, mine, received):
        last = r + 1 == levels - 1
        n, many = held[r + 1], splits[r + 1]
        payload = (1 if last else 2, held[r + 2]) + mat
        low_m, up_m, low_s, *following = short(
            functools.partial(up_kernel, r, last, many), f"up{r}", [mine, received],
            [(n, *mat)] * 3 + [payload] * (2 if many else 1),
        )
        lows.append(low_m)
        ups.append(up_m)
        low_states.append(low_s)
        return following[0], following[-1]

    def adjoint_round(r, parts, received):
        many = splits[r + 1]
        following = (levels - r - 1, held[r + 2]) + mat
        run, *rest = short(
            functools.partial(adjoint_up_kernel, r, [p.shape[1] for p in parts], many),
            f"adjoint_up{r}", [lows[r], received, *parts],
            [(held[r + 1], *mat)] + [following] * (2 if many else 1),
        )
        runs.append(run)
        return rest[0], rest[-1]

    def down_round(r, own, received):
        top = r == levels - 2
        split_in = splits[r + 1]
        many = splits[r]
        inputs = [lows[r], low_states[r], own] + ([received] if split_in or top else [])
        shape = (levels - r, held[r + 1]) + mat
        outs = short(
            functools.partial(down_kernel, r, top, split_in, many), f"down{r}", inputs,
            [shape] * (2 if many else 1),
        )
        return outs[0], outs[-1]

    def adjoint_down_round(r, own, received):
        top = r == levels - 2
        split_in = splits[r + 1]
        many = splits[r]
        inputs = [runs[r], ups[r], own] + ([received] if split_in else [])
        outs = short(
            functools.partial(adjoint_down_kernel, r, top, split_in, many), f"adjoint_down{r}",
            inputs, [(1, held[r + 1], *mat)] * (2 if many else 1),
        )
        return outs[0], outs[-1]

    moves = {}

    def adjoint_send(x, r):
        moves["adjoint", r] = swap(x, r)

    def step(kind, r):
        if kind == "up":
            mine, send = up_round(r, moves["mine", r], moves["pair", r])
            moves["mine", r + 1] = mine
            moves["pair", r + 1] = swap(send, r + 1)
        elif kind == "ad":
            parts = moves["adjoint_mine", r] if r else [early_outs["e_m1"][2], early_outs["e_m2"][2]]
            mine, send = adjoint_round(r, parts, moves["adjoint", r])
            moves["adjoint_mine", r + 1] = [mine]
            adjoint_send(send, r + 1)
        elif kind == "dn":
            top = r == levels - 2
            own = moves["mine", r + 1] if top else moves["own", r + 1]
            received = moves["pair", r + 1] if top else moves.get(("state", r + 1))
            own, send = down_round(r, own, received)
            moves["own", r] = own
            if splits[r]:
                moves["state", r] = swap(send, r)
        else:
            top = r == levels - 2
            own = moves["adjoint", r + 1][:1] if top else moves["grad_own", r + 1]
            own, send = adjoint_down_round(r, own, moves.get(("grad", r + 1)))
            moves["grad_own", r] = own
            if splits[r]:
                moves["grad", r] = swap(send, r)

    def cover(name):
        kind, i = name[0], name[1:]
        if kind == "e":
            early(name)
        elif kind == "l":
            late(int(i))
        else:
            i = int(i)
            start = PARTS[i][0]
            if start < half:
                cross(i, moves["state", 0], start)
            else:
                cross(i, moves["own", 0], start - half)

    moves["mine", 0] = mine
    moves["pair", 0] = swap(other, 0)
    for name in call_order(levels):
        if name[:2] in ("up", "ad", "dn", "ed"):
            step(name[:2], int(name[2:]))
            if name == RELEASE:
                adjoint_send(order.start(early_outs["e_o"][2]), 0)
        else:
            cover(name)
    grad_own, grad_received = moves["grad_own", 0], moves["grad", 0]

    def part_spec(i, *shape):
        first, size = (n // per for n in PARTS[i])
        return pl.BlockSpec(
            (per,) + shape, lambda p: (jnp.clip(p - first, 0, size - 1),) + (0,) * len(shape)
        )

    indices = range(len(PARTS))
    layer_out, grad_queries, grad_values, grad_level_weights = pl.pallas_call(
        functools.partial(value_kernel, [n for _, n in PARTS], per),
        grid=(heads // per,),
        in_specs=[
            SMEM, grouped(width, tokens),
            pl.BlockSpec((1, per) + mat, lambda p: (0, jnp.minimum(p, half // per - 1), 0, 0)),
            pl.BlockSpec((1, per) + mat, lambda p: (0, jnp.maximum(p - half // per, 0), 0, 0)),
        ]
        + [part_spec(i, tokens, width) for i in indices]
        + [part_spec(i, tokens, width) for i in indices]
        + [part_spec(i, levels + 1, tokens) for i in indices]
        + [part_spec(i, width, tokens) for i in indices],
        out_specs=[
            packed, whole((tokens * heads, width)), whole((tokens * heads, width)),
            whole((levels + 1, heads, tokens)),
        ],
        out_shape=[
            struct(tokens, heads, width, dtype=BF16), struct(tokens * heads, width),
            struct(tokens * heads, width), struct(levels + 1, heads, tokens),
        ],
        scratch_shapes=[flat],
        compiler_params=params(BIG),
        cost_estimate=cost(5),
        name="value",
    )(
        order.start(sides), bt, grad_received, grad_own,
        *[cross_outs[i][0] for i in indices], *[cross_outs[i][1] for i in indices],
        *[cross_outs[i][2] for i in indices], *[late_outs[i][2] for i in indices],
    )
    shape = (tokens, heads, width)
    return (
        layer_out, grad_queries.reshape(shape), grad_values.reshape(shape), grad_level_weights
    )


def solution(mesh):
    tokens = P(("groups", "ctx"), None, None)
    rows = P(None, ("groups", "ctx"))
    weights = P(None, None, ("groups", "ctx"))
    return jax.shard_map(
        shards,
        mesh=mesh,
        in_specs=(tokens, tokens, tokens, rows, rows, weights, P(("groups", "ctx")), tokens),
        out_specs=(tokens, tokens, tokens, weights),
        check_vma=False,
    )
```
